32 devices in a mesh: dp: 4 (over z), row: 4 (over y, core), col: 2 (over x).
Axes of the slice: x: 2, y: 2, z: 4, core: 2. Of those that a mesh axis runs over, the one named last changes fastest.
Arguments:
- inputs: bfloat16 [8192, 1024], P('dp', ('row', 'col')), may hold values from -6 to 6
- norm_gain: float32 [1024], replicated, may hold values from 0.5 to 1.5
- norm_shift: float32 [1024], replicated, may hold values from -2 to 2
- gate_weight: bfloat16 [1024, 3072], P('row', 'col'), may hold values from -0.1875 to 0.1875
- gate_bias: float32 [3072], replicated, may hold values from -2 to 2
- value_weight: bfloat16 [1024, 512], P('row'), may hold values from -0.1875 to 0.1875
- value_bias: float32 [512], replicated, may hold values from -2 to 2
- log_step: float32 [512], P('row'), may hold values from -6.9 to -2.3
- decay_rate: float32 [512, 256], P('row'), may hold values from 0.05 to 1
- frequency: float32 [512, 256], P('row'), may hold values from 0 to 50
- readout: float32 [512, 512], P('row'), may hold values from -1.2 to 1.2
- passthrough: float32 [512], P('row'), may hold values from -4 to 4
- expand_weight: bfloat16 [512, 3072], P('row', 'col'), may hold values from -0.25 to 0.25
- output_weight: bfloat16 [3072, 1024], P('col', 'row'), may hold values from -0.21875 to 0.21875
- output_bias: float32 [1024], replicated, may hold values from -2 to 2
- cotangent: bfloat16 [8192, 1024], P('dp', ('row', 'col')), may hold values from -6 to 6
Outputs:
- block_output: bfloat16 [8192, 1024], P('dp', ('row', 'col'))
- input_delta: float32 [8192, 1024], P('dp', ('row', 'col'))
- gain_delta: float32 [1024], P(('row', 'col'))
- shift_delta: float32 [1024], P(('row', 'col'))
- gate_weight_delta: float32 [1024, 3072], P('row', 'col')
- gate_bias_delta: float32 [3072], P('col')
- value_weight_delta: float32 [1024, 512], P('row')
- value_bias_delta: float32 [512], replicated
- log_step_delta: float32 [512], P('row')
- decay_delta: float32 [512, 256], P('row')
- frequency_delta: float32 [512, 256], P('row')
- readout_delta: float32 [512, 512], P('row')
- passthrough_delta: float32 [512], P('row')
- expand_delta: float32 [512, 3072], P('row', 'col')
- output_weight_delta: float32 [3072, 1024], P('col', 'row')
- output_bias_delta: float32 [1024], P(('row', 'col'))
The draws below stay inside these ranges and needn't reach their ends.
All inputs are finite; a program needn't handle non-finite values.
Results may differ from the reference program's by a relative error of at most 0.009.
Values may be sent and summed in bfloat16 or wider, within the bound.
No kernel may reach another device: no remote copies, remote signals or barrier semaphores. Data moves between devices by JAX's collectives and lax.ppermute only.
A program may use at most 384 MiB of HBM per device.

```python
import math
import jax
import jax.numpy as jnp
from jax import lax

D = 1024
FF = 3072
VALUE = 512
MODES = 256
LEN = 2048
TOKENS = 8192


def block_scale(key, shape, shards, low, high):
    def one(axis_at, shards_of):
        steps = jax.random.uniform(jax.random.fold_in(jax.random.fold_in(key, 6), axis_at), (shards_of,), jnp.float32, low / len(shards), high / len(shards))
        return jnp.repeat(jnp.exp(steps), shape[axis_at] // shards_of).reshape((-1,) + (1,) * (len(shape) - axis_at - 1))

    gain = one(*shards[0])
    for cut in shards[1:]:
        gain = gain * one(*cut)
    return gain


def normal_values(rng, extent, deviation, bound, cuts=(), kind=jnp.bfloat16):
    array = jax.random.normal(rng, extent, jnp.float32) * deviation
    if len(cuts) > 0:
        array = block_scale(rng, extent, cuts, -0.22, 0.18) * array
    return jnp.clip(array, min=-bound, max=bound).astype(kind)


def setup_inputs(seed: int = 0) -> dict:
    keys = jax.random.split(jax.random.key(seed), 17)
    return {
        "inputs": normal_values(keys[0], (TOKENS, D), 1.0, 6.0, ((0, 4), (1, 8))),
        "norm_gain": jnp.clip(1.0 + 0.1 * jax.random.normal(keys[1], (D,), jnp.float32), 0.5, 1.5),
        "norm_shift": normal_values(keys[2], (D,), 0.3, 2.0, (), jnp.float32),
        "gate_weight": normal_values(keys[3], (D, FF), D ** -0.5, 0.1875, ((0, 4), (1, 2))),
        "gate_bias": normal_values(keys[4], (FF,), 0.3, 2.0, (), jnp.float32),
        "value_weight": normal_values(keys[5], (D, VALUE), D ** -0.5, 0.1875, ((0, 4),)),
        "value_bias": normal_values(keys[6], (VALUE,), 0.3, 2.0, (), jnp.float32),
        "log_step": jnp.clip(-6.9 + 4.6000001430511475 * jax.random.uniform(keys[7], (VALUE,), jnp.float32) ** block_scale(keys[7], (VALUE,), ((0, 4),), -0.2, 0.2), -6.9, -2.3),
        "decay_rate": jnp.clip(jnp.exp(math.log(1.0) - 2.9957323 * jax.random.uniform(keys[8], (VALUE, MODES), jnp.float32) ** block_scale(keys[8], (VALUE, MODES), ((0, 4),), -0.2, 0.2)), 0.05, 1.0),
        "frequency": jnp.clip(50.0 * jax.random.uniform(keys[9], (VALUE, MODES), jnp.float32) ** block_scale(keys[9], (VALUE, MODES), ((0, 4),), -0.2, 0.2), 0.0, 50.0),
        "readout": normal_values(keys[10], (VALUE, 2 * MODES), 0.2, 1.2, ((0, 4),), jnp.float32),
        "passthrough": normal_values(keys[11], (VALUE,), 1.0, 4.0, ((0, 4),), jnp.float32),
        "expand_weight": normal_values(keys[12], (VALUE, FF), VALUE ** -0.5, 0.25, ((0, 4), (1, 2))),
        "output_weight": normal_values(keys[13], (FF, D), (FF // 4) ** -0.5, 0.21875, ((0, 2), (1, 4))),
        "output_bias": normal_values(keys[14], (D,), 0.3, 2.0, (), jnp.float32),
        "cotangent": normal_values(keys[15], (TOKENS, D), 1.0, 6.0, ((0, 4), (1, 8))),
    }


EPSILON = 1e-05

@jax.custom_vjp
def low(v):
    return lax.optimization_barrier(v.astype(jnp.bfloat16)).astype(jnp.float32)

@jax.custom_vjp
def low_back(v):
    return v

def low_keep(v):
    return (low(v), None)

def low_pass(kept, grad):
    return (grad,)

def back_keep(v):
    return (v, None)

def back_low(kept, grad):
    return (low(grad),)
low.defvjp(low_keep, low_pass)
low_back.defvjp(back_keep, back_low)

def precise_dot(left, right):
    return jnp.dot(left, right, precision=lax.Precision.HIGHEST, preferred_element_type=jnp.float32)

def mode_weights(log_step, decay_rate, frequency, readout):
    time_step = jnp.exp(log_step)[:, None]
    real_rate = -decay_rate * time_step
    imag_rate = frequency * time_step
    growth = jnp.exp(real_rate)
    shift_real = growth * jnp.cos(imag_rate) - 1.0
    shift_imag = growth * jnp.sin(imag_rate)
    modulus = decay_rate * decay_rate + frequency * frequency
    ratio_real = (shift_imag * frequency - shift_real * decay_rate) / modulus
    ratio_imag = (-shift_imag * decay_rate - shift_real * frequency) / modulus
    modes = decay_rate.shape[1]
    out_real = readout[:, :modes]
    out_imag = readout[:, modes:]
    mode_real = out_real * ratio_real - out_imag * ratio_imag
    mode_imag = out_real * ratio_imag + out_imag * ratio_real
    return (real_rate, imag_rate, mode_real, mode_imag)

def powers(real_rate, imag_rate, exponents):
    magnitude = jnp.exp(real_rate[:, :, None] * exponents)
    angle = imag_rate[:, :, None] * exponents
    return (magnitude * jnp.cos(angle), magnitude * jnp.sin(angle))

def state_kernel(log_step, decay_rate, frequency, readout):
    real_rate, imag_rate, mode_real, mode_imag = mode_weights(log_step, decay_rate, frequency, readout)
    block_size = math.gcd(LEN, 64)
    block_count = LEN // block_size
    far_real, far_imag = powers(real_rate, imag_rate, jnp.arange(block_count, dtype=jnp.float32) * block_size)
    near_real, near_imag = powers(real_rate, imag_rate, jnp.arange(block_size, dtype=jnp.float32))
    lead_real = mode_real[:, :, None] * far_real - mode_imag[:, :, None] * far_imag
    lead_imag = mode_real[:, :, None] * far_imag + mode_imag[:, :, None] * far_real
    kernel = jnp.einsum('cmk,cmb->ckb', lead_real, near_real, precision=lax.Precision.HIGHEST)
    kernel = kernel - jnp.einsum('cmk,cmb->ckb', lead_imag, near_imag, precision=lax.Precision.HIGHEST)
    return kernel.reshape(kernel.shape[0], LEN)

def causal_mix(signal, kernel):
    doubled = 2 * LEN
    spectrum = jnp.fft.rfft(signal, n=doubled, axis=0) * jnp.fft.rfft(kernel.T, n=doubled, axis=0)
    return jnp.fft.irfft(spectrum, n=doubled, axis=0)[:LEN]

def block_forward(source, params):
    norm_gain, norm_shift, gate_weight, gate_bias, value_weight, value_bias, log_step, decay_rate, frequency, readout, passthrough, expand_weight, output_weight, output_bias = params
    row_mean = lax.optimization_barrier(jnp.mean(source, axis=-1, keepdims=True))
    centered = source - row_mean
    variance = lax.optimization_barrier(jnp.mean(centered * centered, axis=-1, keepdims=True))
    normed = centered * lax.rsqrt(variance + EPSILON)
    acts = low(normed * norm_gain + norm_shift)
    gate_pre = low_back(precise_dot(acts, gate_weight) + gate_bias)
    gate_act = jax.nn.gelu(gate_pre, approximate=True)
    value_pre = low_back(precise_dot(acts, value_weight) + value_bias)
    values = jax.nn.gelu(value_pre, approximate=True)
    kernel = state_kernel(log_step, decay_rate, frequency, readout)
    mixed = low(causal_mix(values, kernel) + passthrough * values)
    expanded = low_back(precise_dot(mixed, expand_weight))
    product = low(gate_act * expanded)
    return source + precise_dot(product, output_weight) + output_bias

def reference(inputs, norm_gain, norm_shift, gate_weight, gate_bias, value_weight, value_bias, log_step, decay_rate, frequency, readout, passthrough, expand_weight, output_weight, output_bias, cotangent):
    params = tuple((member.astype(jnp.float32) for member in (norm_gain, norm_shift, gate_weight, gate_bias, value_weight, value_bias, log_step, decay_rate, frequency, readout, passthrough, expand_weight, output_weight, output_bias)))
    sequences = inputs.astype(jnp.float32).reshape(TOKENS // LEN, LEN, D)
    upstream = cotangent.astype(jnp.float32).reshape(TOKENS // LEN, LEN, D)

    def per_sequence(totals, sequence_pair):
        source, incoming = sequence_pair
        result, pullback = jax.vjp(block_forward, source, params)
        source_delta, param_delta = pullback(incoming)
        totals = jax.tree.map(jnp.add, totals, param_delta)
        return (totals, (result.astype(jnp.bfloat16), source_delta))
    totals, (results, deltas) = lax.scan(per_sequence, jax.tree.map(jnp.zeros_like, params), (sequences, upstream))
    gain_delta, shift_delta, gate_weight_delta, gate_bias_delta, value_weight_delta, value_bias_delta, log_step_delta, decay_delta, frequency_delta, readout_delta, passthrough_delta, expand_delta, output_weight_delta, output_bias_delta = totals
    return (results.reshape(TOKENS, D), deltas.reshape(TOKENS, D), gain_delta, shift_delta, gate_weight_delta, gate_bias_delta, value_weight_delta, value_bias_delta, log_step_delta, decay_delta, frequency_delta, readout_delta, passthrough_delta, expand_delta, output_weight_delta, output_bias_delta)
```

```python
from functools import partial
import math

import jax
import jax.numpy as jnp
from jax import lax
from jax.experimental import pallas as pl
from jax.experimental.pallas import tpu as pltpu
from jax.sharding import PartitionSpec as P

D = 1024
FF = 3072
VALUE = 512
LEN = 2048
EPSILON = 1e-05
BL = 128
GROUP = 8
BF = jnp.bfloat16
F32 = jnp.float32


def dot(left, right, left_dim, right_dim):
    return lax.dot_general(
        left, right, (((left_dim,), (right_dim,)), ((), ())), preferred_element_type=F32
    )


def gelu(pre_act):
    return jax.nn.gelu(pre_act, approximate=True)


def gelu_back(pre_act, upstream):
    return jax.vjp(gelu, pre_act)[1](upstream)[0]


def mode_weights(log_step, decay_rate, frequency, readout):
    time_step = jnp.exp(log_step)[:, None]
    real_rate = -decay_rate * time_step
    imag_rate = frequency * time_step
    growth = jnp.exp(real_rate)
    shift_real = growth * jnp.cos(imag_rate) - 1.0
    shift_imag = growth * jnp.sin(imag_rate)
    modulus = decay_rate * decay_rate + frequency * frequency
    ratio_real = (shift_imag * frequency - shift_real * decay_rate) / modulus
    ratio_imag = (-shift_imag * decay_rate - shift_real * frequency) / modulus
    modes = decay_rate.shape[1]
    out_real = readout[:, :modes]
    out_imag = readout[:, modes:]
    mode_real = out_real * ratio_real - out_imag * ratio_imag
    mode_imag = out_real * ratio_imag + out_imag * ratio_real
    return (real_rate, imag_rate, mode_real, mode_imag)


def cmul(a, b):
    return a[0]*b[0]-a[1]*b[1], a[0]*b[1]+a[1]*b[0]

def squarings(z, n):
    out=[z]
    for _ in range(n):
        r,i=out[-1]
        out.append((r*r-i*i, 2.0*r*i))
    return out

def ladder(steps, rows, order, first=None):
    M = steps[0][0].shape[1]
    idx = lax.broadcasted_iota(jnp.int32, (8, M), 0)
    if order < 0: idx = 7-idx
    wr = jnp.ones((8,M), jnp.float32); wi = jnp.zeros((8,M), jnp.float32)
    for b in range(3):
        hit = (idx >> b) & 1
        nr, ni = cmul((wr,wi), steps[b])
        wr = jnp.where(hit==1, nr, wr); wi = jnp.where(hit==1, ni, wi)
    groups=[(wr,wi)]
    k=3
    while len(groups)*8 < rows:
        groups += [cmul(g, steps[k]) for g in groups]
        k+=1
    if order<0: groups = groups[::-1]
    return jnp.concatenate([g[0] for g in groups],0), jnp.concatenate([g[1] for g in groups],0)

def row(p, i):
    return p[0][i:i+1], p[1][i:i+1]

def gen_kernel(prec, nb, zr, zi, cr, ci, k_out, kr_out):
    steps = squarings((zr[...], zi[...]), 6 + int(math.log2(nb)))
    rev = (lax.broadcasted_iota(jnp.int32,(BL,BL),0)+lax.broadcasted_iota(jnp.int32,(BL,BL),1)==BL-1).astype(jnp.float32).astype(jnp.bfloat16)
    nt = (((1,),(1,)),((),()))
    for i in range(GROUP):
        st = [row(s,i) for s in steps]
        near = ladder(st[:7], BL, 1)
        far = ladder(st[7:], nb, 1)
        lead = cmul((cr[i:i+1,:], ci[i:i+1,:]), far)
        k = lax.dot_general(jnp.concatenate([lead[0], -lead[1]],1), jnp.concatenate(near,1), nt, precision=prec, preferred_element_type=jnp.float32)
        kb = k.astype(jnp.bfloat16)
        k_out[i] = kb
        kr_out[i] = jnp.dot(kb, rev, preferred_element_type=jnp.float32).astype(jnp.bfloat16)

def generate(zr, zi, cr, ci, length, prec=lax.Precision.HIGHEST):
    C, M = zr.shape
    nb = length//BL
    spec = pl.BlockSpec((GROUP, M), lambda i:(i,0))
    ospec = pl.BlockSpec((GROUP, nb, BL), lambda i:(i,0,0))
    sh = jax.ShapeDtypeStruct((C,nb,BL), jnp.bfloat16)
    return pl.pallas_call(partial(gen_kernel, prec, nb), grid=(C//GROUP,), in_specs=[spec]*4, out_specs=[ospec]*2, out_shape=[sh,sh])(zr,zi,cr,ci)

def toeplitz_blocks(load, count, shift):
    r = lax.broadcasted_iota(jnp.int32,(BL,BL),0); c = lax.broadcasted_iota(jnp.int32,(BL,BL),1)
    mask = c >= r + shift
    def rot(j):
        x = load(j)
        if x is None: return jnp.zeros((BL,BL), jnp.float32)
        return pltpu.roll(jnp.broadcast_to(x,(BL,BL)), shift, 1, stride=1, stride_axis=0)
    out=[]
    cur = rot(0)
    for j in range(count):
        nxt = rot(j+1)
        out.append(jnp.where(mask, nxt, cur).astype(jnp.bfloat16))
        cur = nxt
    return jnp.concatenate(out,0)

def shifted(pad_ref, nb, d):
    return pad_ref[pl.ds(nb-d, nb), :]

def fwd_kernel(nb, tb, v_ref, kr_ref, p_ref, out_ref, pad):
    per = tb//BL
    pad[0:nb,:] = jnp.zeros((nb,BL), jnp.float32)
    for i in range(GROUP):
        def load(j):
            if j==0: return None
            j-=1
            return v_ref[j//per, i:i+1, (j%per)*BL:(j%per+1)*BL].astype(jnp.float32)
        H = toeplitz_blocks(load, nb, 0)
        pad[nb:2*nb,:] = kr_ref[i].astype(jnp.float32)
        X = jnp.concatenate([shifted(pad,nb,d) for d in range(nb)],1).astype(jnp.bfloat16)
        out = jnp.dot(X, H, preferred_element_type=jnp.float32)
        for j in range(nb):
            sl = (j//per, slice(i,i+1), slice((j%per)*BL,(j%per+1)*BL))
            out_ref[sl] = (out[j:j+1,:] + p_ref[i:i+1,:]*v_ref[sl].astype(jnp.float32)).astype(out_ref.dtype)

def forward(v, kr, passthrough, out_dtype=jnp.float32):
    R,C,tb = v.shape
    nb = R*tb//BL
    spec = pl.BlockSpec((R,GROUP,tb), lambda i:(0,i,0))
    kspec = pl.BlockSpec((GROUP,nb,BL), lambda i:(i,0,0))
    pspec = pl.BlockSpec((GROUP,BL), lambda i:(i,0))
    return pl.pallas_call(partial(fwd_kernel,nb,tb), grid=(C//GROUP,), in_specs=[spec,kspec,pspec], out_specs=spec,
        out_shape=jax.ShapeDtypeStruct(v.shape,out_dtype), scratch_shapes=[pltpu.VMEM((2*nb,BL),jnp.float32)])(v,kr,jnp.broadcast_to(passthrough[:,None],(C,BL)))

def bwd_kernel(prec, nb, tb, v_ref, m_ref, k_ref, p_ref, zr, zi, vb_ref, s_ref, pad, pad2):
    per = tb//BL
    pad[0:nb,:] = jnp.zeros((nb,BL), jnp.float32)
    pad2[0:nb,:] = jnp.zeros((nb,BL), jnp.float32)
    steps = squarings((zr[...], zi[...]), 6 + int(math.log2(nb)))
    rev = (lax.broadcasted_iota(jnp.int32,(BL,BL),0)+lax.broadcasted_iota(jnp.int32,(BL,BL),1)==BL-1).astype(jnp.float32).astype(jnp.bfloat16)
    lane = lax.broadcasted_iota(jnp.int32,(nb,BL),1).astype(jnp.float32)
    M = zr.shape[1]
    arow = (nb-1-lax.broadcasted_iota(jnp.int32,(nb,M),0)).astype(jnp.float32)*BL
    for i in range(GROUP):
        def at(j): return (j//per, slice(i,i+1), slice((j%per)*BL,(j%per+1)*BL))
        def load(j):
            if j==nb: return None
            return m_ref[at(j)].astype(jnp.float32)
        H = toeplitz_blocks(load, nb, 1)
        pad[nb:2*nb,:] = k_ref[i].astype(jnp.float32)
        for j in range(nb):
            pad2[nb+j:nb+j+1,:] = v_ref[at(j)].astype(jnp.float32)
        pad2[nb:2*nb,:] = jnp.dot(pad2[nb:2*nb,:].astype(jnp.bfloat16), rev, preferred_element_type=jnp.float32)
        X = jnp.concatenate([jnp.concatenate([shifted(pad,nb,nb-1-e) for e in range(nb)],1), jnp.concatenate([shifted(pad2,nb,nb-1-e) for e in range(nb)],1)],0).astype(jnp.bfloat16)
        out = jnp.dot(X, H, preferred_element_type=jnp.float32)
        for j in range(nb):
            vb_ref[at(j)] = (out[nb-1-j:nb-j,:] + p_ref[i:i+1,:]*m_ref[at(j)].astype(jnp.float32)).astype(vb_ref.dtype)
        kb = out[nb:,:]
        st = [row(s,i) for s in steps]
        near = ladder(st[:7], BL, 1)
        far = ladder(st[7:], nb, -1)
        U = jnp.dot(jnp.concatenate([kb, kb*lane],0), jnp.concatenate(near,1), precision=prec, preferred_element_type=jnp.float32)
        u = U[:nb,:M], U[:nb,M:]
        w = U[nb:,:M]+arow*u[0], U[nb:,M:]+arow*u[1]
        s1 = cmul(u, far); s2 = cmul(w, far)
        for n,x in enumerate((*s1,*s2)):
            s_ref[n, i:i+1, :] = jnp.sum(x,0,keepdims=True)

def backward(v, mb, k, passthrough, zr, zi, out_dtype=jnp.float32, prec=lax.Precision.HIGHEST):
    R,C,tb = v.shape
    M = zr.shape[1]
    nb = R*tb//BL
    spec = pl.BlockSpec((R,GROUP,tb), lambda i:(0,i,0))
    kspec = pl.BlockSpec((GROUP,nb,BL), lambda i:(i,0,0))
    pspec = pl.BlockSpec((GROUP,BL), lambda i:(i,0))
    zspec = pl.BlockSpec((GROUP,M), lambda i:(i,0))
    return pl.pallas_call(partial(bwd_kernel,prec,nb,tb), grid=(C//GROUP,), in_specs=[spec,spec,kspec,pspec,zspec,zspec],
        out_specs=[spec, pl.BlockSpec((4,GROUP,M), lambda i:(0,i,0))],
        out_shape=[jax.ShapeDtypeStruct(v.shape,out_dtype), jax.ShapeDtypeStruct((4,C,M),jnp.float32)],
        scratch_shapes=[pltpu.VMEM((2*nb,BL),jnp.float32)]*2)(v,mb,k,jnp.broadcast_to(passthrough[:,None],(C,BL)),zr,zi)


def shards(
    inputs,
    norm_gain,
    norm_shift,
    gate_weight,
    gate_bias,
    value_weight,
    value_bias,
    log_step,
    decay_rate,
    frequency,
    readout,
    passthrough,
    expand_weight,
    output_weight,
    output_bias,
    cotangent,
):
    rows = lax.axis_size("row")
    cols = lax.axis_size("col")
    row_index = lax.axis_index("row")
    col_index = lax.axis_index("col")
    tokens, narrow = inputs.shape
    block = tokens // rows
    half_ff = FF // cols
    row_channels = VALUE // rows
    channels = row_channels // cols
    local_channels = rows * channels

    def own_channels(array):
        return lax.dynamic_slice_in_dim(array, col_index * channels, channels, 0)

    state_params = tuple(own_channels(a) for a in (log_step, decay_rate, frequency, readout))
    own_pass = own_channels(passthrough)
    weights, weights_pullback = jax.vjp(mode_weights, *state_params)
    real_rate, imag_rate, mode_real, mode_imag = weights
    growth = jnp.exp(real_rate)
    z_real, z_imag = growth * jnp.cos(imag_rate), growth * jnp.sin(imag_rate)
    kernel, kernel_flipped = generate(z_real, z_imag, mode_real, mode_imag, tokens)

    both = jnp.stack([inputs, cotangent]).reshape(2, rows, block, narrow)
    both = lax.all_to_all(both, "row", 1, 1)
    both = lax.all_gather(both, "col", axis=3)
    both = both.transpose(0, 2, 1, 3, 4).reshape(2, block, D)
    source = both[0].astype(F32)
    upstream = both[1]
    value_half = lax.dynamic_index_in_dim(
        value_weight.reshape(-1, rows, cols, channels), col_index, 2, False
    ).reshape(-1, local_channels)
    value_half = lax.all_gather(value_half, "row", axis=0, tiled=True)
    gate_full = lax.all_gather(gate_weight, "row", axis=0, tiled=True)
    output_full = lax.all_gather(output_weight, "row", axis=1, tiled=True)
    expand_full = lax.all_gather(expand_weight, "row", axis=0, tiled=True)
    value_bias_half = lax.dynamic_index_in_dim(
        value_bias.reshape(rows, cols, channels), col_index, 1, False
    ).reshape(local_channels, 1)
    gate_bias_half = lax.dynamic_slice_in_dim(gate_bias, col_index * half_ff, half_ff)

    row_mean = jnp.mean(source, axis=-1, keepdims=True)
    centered = source - row_mean
    variance = jnp.mean(centered * centered, axis=-1, keepdims=True)
    rescale = lax.rsqrt(variance + EPSILON)
    normed = centered * rescale
    acts = (normed * norm_gain + norm_shift).astype(BF)

    value_pre = dot(value_half, acts, 0, 1) + value_bias_half
    values = gelu(value_pre).astype(BF).reshape(rows, channels, block)
    values = lax.all_to_all(values, "row", 0, 0)
    mixed = forward(values, kernel, own_pass, BF)
    mixed = lax.all_to_all(mixed, "row", 0, 0)
    mixed = lax.all_gather(mixed, "col", axis=1).reshape(VALUE, block)

    gate_pre = dot(acts, gate_full, 1, 0) + gate_bias_half
    gate_act = gelu(gate_pre)
    product_back = dot(upstream, output_full, 1, 1)
    expand_back = (product_back * gate_act).astype(BF)
    mixed_back = dot(expand_full, expand_back, 1, 1).astype(BF)
    mixed_back = lax.psum_scatter(
        mixed_back.reshape(rows, cols, channels, block), "col", scatter_dimension=1, tiled=False
    )
    mixed_back = lax.all_to_all(mixed_back, "row", 0, 0)

    expanded = dot(mixed, expand_full, 0, 0)
    product = (gate_act * expanded).astype(BF)
    gate_back = gelu_back(gate_pre, product_back * expanded).astype(BF)
    output_weight_delta = dot(product, upstream, 0, 0)
    expand_delta = dot(mixed, expand_back, 1, 0)
    gate_weight_delta = dot(acts, gate_back, 0, 0)
    gate_bias_delta = jnp.sum(gate_back, axis=0, dtype=F32)

    def row_sum(array, dim):
        return lax.psum_scatter(array.astype(BF), "row", scatter_dimension=dim, tiled=True).astype(F32)

    output_weight_delta = row_sum(output_weight_delta, 1)
    expand_delta = row_sum(expand_delta, 0)
    gate_weight_delta = row_sum(gate_weight_delta, 0)

    out_sum = dot(product, output_full, 1, 0).astype(BF).reshape(block, rows, cols, narrow)
    out_sum = lax.psum_scatter(out_sum, "col", scatter_dimension=2, tiled=False).astype(F32)

    def own_features(array):
        return lax.dynamic_index_in_dim(
            array.reshape(-1, rows, cols, narrow), col_index, 2, False
        )

    block_output = (own_features(source) + out_sum + own_features(output_bias)).astype(BF)
    block_output = lax.all_to_all(block_output, "row", 1, 0, tiled=True).reshape(tokens, narrow)

    values_back, sums = backward(
        values, mixed_back, kernel_flipped, own_pass, z_real, z_imag, BF
    )
    values_back = lax.all_to_all(values_back, "row", 0, 0).reshape(local_channels, block)
    value_back = gelu_back(value_pre, values_back.astype(F32)).astype(BF)
    value_weight_delta = row_sum(dot(acts, value_back, 0, 1), 0)
    value_bias_delta = jnp.sum(value_back, axis=1, dtype=F32)
    passthrough_delta = jnp.sum(mixed_back.astype(F32) * values.astype(F32), axis=(0, 2))
    first_real, first_imag, second_real, second_imag = sums
    state_deltas = weights_pullback(
        (
            mode_real * second_real - mode_imag * second_imag,
            -mode_real * second_imag - mode_imag * second_real,
            first_real,
            -first_imag,
        )
    )

    acts_back = dot(gate_back, gate_full, 1, 1) + dot(value_back, value_half, 0, 1)
    weighted = acts_back * norm_gain
    moments = jnp.stack([jnp.sum(weighted, axis=1), jnp.sum(weighted * normed, axis=1)])
    moments = lax.psum(moments, "col") / D
    acts_back = lax.psum_scatter(
        acts_back.astype(BF).reshape(block, rows, cols, narrow), "col", scatter_dimension=2, tiled=False
    ).astype(F32)
    own_normed = own_features(normed)
    gain_delta = jnp.sum(acts_back * own_normed, axis=0)
    shift_delta = jnp.sum(acts_back, axis=0)
    input_delta = rescale[:, :, None] * (
        acts_back * own_features(norm_gain) - moments[0][:, None, None] - own_normed * moments[1][:, None, None]
    )
    input_delta = lax.all_to_all(input_delta.astype(BF), "row", 1, 0, tiled=True).reshape(tokens, narrow)
    input_delta = cotangent.astype(F32) + input_delta.astype(F32)

    def place_features(array):
        full = jnp.zeros((rows, cols, narrow), F32)
        return lax.dynamic_update_slice(full, array[:, None, :], (0, col_index, 0)).reshape(-1)

    def place_channels(array, width):
        full = jnp.zeros((rows, cols, channels), F32)
        start = (row_index, col_index, 0) if width == 1 else (0, col_index, 0)
        return lax.dynamic_update_slice(full, array.reshape(width, 1, channels), start).reshape(-1)

    small = jnp.concatenate(
        [
            place_features(gain_delta.reshape(rows, narrow)),
            place_features(shift_delta.reshape(rows, narrow)),
            lax.dynamic_update_slice(jnp.zeros((FF,), F32), gate_bias_delta, (col_index * half_ff,)),
            place_channels(value_bias_delta, rows),
            lax.dynamic_update_slice(
                jnp.zeros((D,), F32),
                jnp.sum(cotangent, axis=0, dtype=F32),
                ((row_index * cols + col_index) * narrow,),
            ),
            place_channels(state_deltas[0], 1),
            place_channels(passthrough_delta, 1),
        ]
    )
    small = lax.psum(small, ("dp", "row", "col"))
    gain_sum, shift_sum, gate_bias_sum, value_bias_sum, bias_sum, step_sum, pass_sum = jnp.split(
        small, [D, 2 * D, 2 * D + FF, 2 * D + FF + VALUE, 3 * D + FF + VALUE, 3 * D + FF + 2 * VALUE]
    )
    start = (row_index * cols + col_index) * narrow

    state = jnp.concatenate(state_deltas[1:], axis=1)
    gate_weight_delta, expand_delta, output_weight_delta, value_weight_delta, state = lax.psum(
        (gate_weight_delta, expand_delta, output_weight_delta, value_weight_delta, state), "dp"
    )
    value_weight_delta = value_weight_delta.reshape(-1, rows, channels)
    value_weight_delta = lax.all_gather(value_weight_delta, "col", axis=2).reshape(-1, VALUE)
    state = lax.all_gather(state, "col", axis=0, tiled=True)
    modes = decay_rate.shape[1]
    return (
        block_output,
        input_delta,
        lax.dynamic_slice_in_dim(gain_sum, start, narrow),
        lax.dynamic_slice_in_dim(shift_sum, start, narrow),
        gate_weight_delta,
        lax.dynamic_slice_in_dim(gate_bias_sum, col_index * half_ff, half_ff),
        value_weight_delta,
        value_bias_sum,
        lax.dynamic_slice_in_dim(step_sum, row_index * row_channels, row_channels),
        state[:, :modes],
        state[:, modes : 2 * modes],
        state[:, 2 * modes :],
        lax.dynamic_slice_in_dim(pass_sum, row_index * row_channels, row_channels),
        expand_delta,
        output_weight_delta,
        lax.dynamic_slice_in_dim(bias_sum, start, narrow),
    )


def solution(mesh):
    placed = (
        P("dp", ("row", "col")),
        P(),
        P(),
        P("row", "col"),
        P(),
        P("row", None),
        P(),
        P("row"),
        P("row", None),
        P("row", None),
        P("row", None),
        P("row"),
        P("row", "col"),
        P("col", "row"),
        P(),
        P("dp", ("row", "col")),
    )
    return jax.shard_map(
        shards,
        mesh=mesh,
        in_specs=placed,
        out_specs=(
            P("dp", ("row", "col")),
            P("dp", ("row", "col")),
            P(("row", "col")),
            P(("row", "col")),
            P("row", "col"),
            P("col"),
            P("row", None),
            P(),
            P("row"),
            P("row", None),
            P("row", None),
            P("row", None),
            P("row"),
            P("row", "col"),
            P("col", "row"),
            P(("row", "col")),
        ),
        check_vma=False,
    )
```

```python
from functools import partial
import math

import jax
import jax.numpy as jnp
from jax import lax
from jax.experimental import pallas as pl
from jax.experimental.pallas import tpu as pltpu
from jax.sharding import PartitionSpec as P

D = 1024
FF = 3072
VALUE = 512
LEN = 2048
EPSILON = 1e-05
BL = 128
GROUP = 8
BF = jnp.bfloat16
F32 = jnp.float32


def dot(left, right, left_dim, right_dim):
    return lax.dot_general(
        left, right, (((left_dim,), (right_dim,)), ((), ())), preferred_element_type=F32
    )


def gelu(pre_act):
    return jax.nn.gelu(pre_act, approximate=True)


def gelu_back(pre_act, upstream):
    return jax.vjp(gelu, pre_act)[1](upstream)[0]


def mode_weights(log_step, decay_rate, frequency, readout):
    time_step = jnp.exp(log_step)[:, None]
    real_rate = -decay_rate * time_step
    imag_rate = frequency * time_step
    growth = jnp.exp(real_rate)
    shift_real = growth * jnp.cos(imag_rate) - 1.0
    shift_imag = growth * jnp.sin(imag_rate)
    modulus = decay_rate * decay_rate + frequency * frequency
    ratio_real = (shift_imag * frequency - shift_real * decay_rate) / modulus
    ratio_imag = (-shift_imag * decay_rate - shift_real * frequency) / modulus
    modes = decay_rate.shape[1]
    out_real = readout[:, :modes]
    out_imag = readout[:, modes:]
    mode_real = out_real * ratio_real - out_imag * ratio_imag
    mode_imag = out_real * ratio_imag + out_imag * ratio_real
    return (real_rate, imag_rate, mode_real, mode_imag)


def cmul(a, b):
    return a[0]*b[0]-a[1]*b[1], a[0]*b[1]+a[1]*b[0]

def squarings(z, n):
    out=[z]
    for _ in range(n):
        r,i=out[-1]
        out.append((r*r-i*i, 2.0*r*i))
    return out

def ladder(steps, rows, order, first=None):
    M = steps[0][0].shape[1]
    idx = lax.broadcasted_iota(jnp.int32, (8, M), 0)
    if order < 0: idx = 7-idx
    wr = jnp.ones((8,M), jnp.float32); wi = jnp.zeros((8,M), jnp.float32)
    for b in range(3):
        hit = (idx >> b) & 1
        nr, ni = cmul((wr,wi), steps[b])
        wr = jnp.where(hit==1, nr, wr); wi = jnp.where(hit==1, ni, wi)
    groups=[(wr,wi)]
    k=3
    while len(groups)*8 < rows:
        groups += [cmul(g, steps[k]) for g in groups]
        k+=1
    if order<0: groups = groups[::-1]
    return jnp.concatenate([g[0] for g in groups],0), jnp.concatenate([g[1] for g in groups],0)

def row(p, i):
    return p[0][i:i+1], p[1][i:i+1]

def gen_kernel(prec, nb, zr, zi, cr, ci, k_out, kr_out):
    steps = squarings((zr[...], zi[...]), 6 + int(math.log2(nb)))
    rev = (lax.broadcasted_iota(jnp.int32,(BL,BL),0)+lax.broadcasted_iota(jnp.int32,(BL,BL),1)==BL-1).astype(jnp.float32).astype(jnp.bfloat16)
    nt = (((1,),(1,)),((),()))
    for i in range(GROUP):
        st = [row(s,i) for s in steps]
        near = ladder(st[:7], BL, 1)
        far = ladder(st[7:], nb, 1)
        lead = cmul((cr[i:i+1,:], ci[i:i+1,:]), far)
        k = lax.dot_general(jnp.concatenate([lead[0], -lead[1]],1), jnp.concatenate(near,1), nt, precision=prec, preferred_element_type=jnp.float32)
        kb = k.astype(jnp.bfloat16)
        k_out[i] = kb
        kr_out[i] = jnp.dot(kb, rev, preferred_element_type=jnp.float32).astype(jnp.bfloat16)

def generate(zr, zi, cr, ci, length, prec=lax.Precision.HIGHEST):
    C, M = zr.shape
    nb = length//BL
    spec = pl.BlockSpec((GROUP, M), lambda i:(i,0))
    ospec = pl.BlockSpec((GROUP, nb, BL), lambda i:(i,0,0))
    sh = jax.ShapeDtypeStruct((C,nb,BL), jnp.bfloat16)
    return pl.pallas_call(partial(gen_kernel, prec, nb), grid=(C//GROUP,), in_specs=[spec]*4, out_specs=[ospec]*2, out_shape=[sh,sh])(zr,zi,cr,ci)

def toeplitz_blocks(load, count, shift):
    r = lax.broadcasted_iota(jnp.int32,(BL,BL),0); c = lax.broadcasted_iota(jnp.int32,(BL,BL),1)
    mask = c >= r + shift
    def rot(j):
        x = load(j)
        if x is None: return jnp.zeros((BL,BL), jnp.float32)
        return pltpu.roll(jnp.broadcast_to(x,(BL,BL)), shift, 1, stride=1, stride_axis=0)
    out=[]
    cur = rot(0)
    for j in range(count):
        nxt = rot(j+1)
        out.append(jnp.where(mask, nxt, cur).astype(jnp.bfloat16))
        cur = nxt
    return jnp.concatenate(out,0)

def shifted(pad_ref, nb, d):
    return pad_ref[pl.ds(nb-d, nb), :]

def fwd_kernel(nb, tb, me_ref, v_ref, kr_ref, p_ref, out_ref, pad):
    per = tb//BL
    me = me_ref[0]
    pad[0:nb,:] = jnp.zeros((nb,BL), jnp.float32)
    for i in range(GROUP):
        def load(j):
            if j==0: return None
            j-=1
            return v_ref[me ^ (j//per), i:i+1, (j%per)*BL:(j%per+1)*BL].astype(jnp.float32)
        H = toeplitz_blocks(load, nb, 0)
        pad[nb:2*nb,:] = kr_ref[i].astype(jnp.float32)
        X = jnp.concatenate([shifted(pad,nb,d) for d in range(nb)],1).astype(jnp.bfloat16)
        out = jnp.dot(X, H, preferred_element_type=jnp.float32)
        for j in range(nb):
            sl = (me ^ (j//per), slice(i,i+1), slice((j%per)*BL,(j%per+1)*BL))
            out_ref[sl] = (out[j:j+1,:] + p_ref[i:i+1,:]*v_ref[sl].astype(jnp.float32)).astype(out_ref.dtype)

def forward(me, v, kr, passthrough, out_dtype=jnp.float32):
    R,C,tb = v.shape
    nb = R*tb//BL
    spec = pl.BlockSpec((R,GROUP,tb), lambda i,_:(0,i,0))
    kspec = pl.BlockSpec((GROUP,nb,BL), lambda i,_:(i,0,0))
    pspec = pl.BlockSpec((GROUP,BL), lambda i,_:(i,0))
    grid_spec = pltpu.PrefetchScalarGridSpec(num_scalar_prefetch=1, grid=(C//GROUP,), in_specs=[spec,kspec,pspec], out_specs=spec,
        scratch_shapes=[pltpu.VMEM((2*nb,BL),jnp.float32)])
    return pl.pallas_call(partial(fwd_kernel,nb,tb), grid_spec=grid_spec,
        out_shape=jax.ShapeDtypeStruct(v.shape,out_dtype))(me,v,kr,jnp.broadcast_to(passthrough[:,None],(C,BL)))

def bwd_kernel(prec, nb, tb, me_ref, v_ref, m_ref, k_ref, p_ref, zr, zi, vb_ref, s_ref, pad, pad2):
    per = tb//BL
    pad[0:nb,:] = jnp.zeros((nb,BL), jnp.float32)
    pad2[0:nb,:] = jnp.zeros((nb,BL), jnp.float32)
    me = me_ref[0]
    steps = squarings((zr[...], zi[...]), 6 + int(math.log2(nb)))
    rev = (lax.broadcasted_iota(jnp.int32,(BL,BL),0)+lax.broadcasted_iota(jnp.int32,(BL,BL),1)==BL-1).astype(jnp.float32).astype(jnp.bfloat16)
    lane = lax.broadcasted_iota(jnp.int32,(nb,BL),1).astype(jnp.float32)
    M = zr.shape[1]
    arow = (nb-1-lax.broadcasted_iota(jnp.int32,(nb,M),0)).astype(jnp.float32)*BL
    for i in range(GROUP):
        def at(j): return (me ^ (j//per), slice(i,i+1), slice((j%per)*BL,(j%per+1)*BL))
        def load(j):
            if j==nb: return None
            return m_ref[at(j)].astype(jnp.float32)
        H = toeplitz_blocks(load, nb, 1)
        pad[nb:2*nb,:] = k_ref[i].astype(jnp.float32)
        for j in range(nb):
            pad2[nb+j:nb+j+1,:] = v_ref[at(j)].astype(jnp.float32)
        pad2[nb:2*nb,:] = jnp.dot(pad2[nb:2*nb,:].astype(jnp.bfloat16), rev, preferred_element_type=jnp.float32)
        X = jnp.concatenate([jnp.concatenate([shifted(pad,nb,nb-1-e) for e in range(nb)],1), jnp.concatenate([shifted(pad2,nb,nb-1-e) for e in range(nb)],1)],0).astype(jnp.bfloat16)
        out = jnp.dot(X, H, preferred_element_type=jnp.float32)
        for j in range(nb):
            vb_ref[at(j)] = (out[nb-1-j:nb-j,:] + p_ref[i:i+1,:]*m_ref[at(j)].astype(jnp.float32)).astype(vb_ref.dtype)
        kb = out[nb:,:]
        st = [row(s,i) for s in steps]
        near = ladder(st[:7], BL, 1)
        far = ladder(st[7:], nb, -1)
        U = jnp.dot(jnp.concatenate([kb, kb*lane],0), jnp.concatenate(near,1), precision=prec, preferred_element_type=jnp.float32)
        u = U[:nb,:M], U[:nb,M:]
        w = U[nb:,:M]+arow*u[0], U[nb:,M:]+arow*u[1]
        s1 = cmul(u, far); s2 = cmul(w, far)
        for n,x in enumerate((*s1,*s2)):
            s_ref[n, i:i+1, :] = jnp.sum(x,0,keepdims=True)

def backward(me, v, mb, k, passthrough, zr, zi, out_dtype=jnp.float32, prec=lax.Precision.DEFAULT):
    R,C,tb = v.shape
    M = zr.shape[1]
    nb = R*tb//BL
    spec = pl.BlockSpec((R,GROUP,tb), lambda i,_:(0,i,0))
    kspec = pl.BlockSpec((GROUP,nb,BL), lambda i,_:(i,0,0))
    pspec = pl.BlockSpec((GROUP,BL), lambda i,_:(i,0))
    zspec = pl.BlockSpec((GROUP,M), lambda i,_:(i,0))
    grid_spec = pltpu.PrefetchScalarGridSpec(num_scalar_prefetch=1, grid=(C//GROUP,), in_specs=[spec,spec,kspec,pspec,zspec,zspec],
        out_specs=[spec, pl.BlockSpec((4,GROUP,M), lambda i,_:(0,i,0))], scratch_shapes=[pltpu.VMEM((2*nb,BL),jnp.float32)]*2)
    return pl.pallas_call(partial(bwd_kernel,prec,nb,tb), grid_spec=grid_spec,
        out_shape=[jax.ShapeDtypeStruct(v.shape,out_dtype), jax.ShapeDtypeStruct((4,C,M),jnp.float32)],
        )(me,v,mb,k,jnp.broadcast_to(passthrough[:,None],(C,BL)),zr,zi)


def bits(axis):
    size = lax.axis_size(axis)
    return [1 << k for k in range(size.bit_length() - 1)]


def swap(array, axis, mask):
    return lax.ppermute(array, axis, [(i, i ^ mask) for i in range(lax.axis_size(axis))])


def gather_blocks(array, axis):
    parts = {0: array}
    for bit in reversed(bits(axis)):
        parts.update({q | bit: swap(parts[q], axis, bit) for q in sorted(parts)})
    return [parts[q] for q in sorted(parts)]


def exchange_blocks(blocks, axis):
    return [blocks[0]] + [swap(blocks[q], axis, q) for q in range(1, len(blocks))]


def reduce_blocks(blocks, axis):
    parts = dict(enumerate(blocks))
    for bit in bits(axis):
        for q in sorted(parts):
            if not q & bit:
                parts[q] = parts[q].astype(F32) + swap(parts.pop(q | bit).astype(BF), axis, bit).astype(F32)
    return parts[0]


def pair_sum(array, axis):
    size = lax.axis_size(axis)
    if size == 1:
        return array.astype(F32)
    index = lax.axis_index(axis)
    half = (index ^ (index >> 1)) & 1
    length = array.shape[0] // 2
    kept = lax.dynamic_slice_in_dim(array, half * length, length)
    sent = lax.dynamic_slice_in_dim(array, (1 - half) * length, length)
    total = kept.astype(F32) + swap(sent.astype(BF), axis, 1).astype(F32)
    for bit in bits(axis)[1:]:
        rounded = total.astype(BF)
        total = rounded.astype(F32) + swap(rounded, axis, 3 if bit == 2 else bit).astype(F32)
    mine = total.astype(BF)
    other = swap(mine, axis, 1)
    first = jnp.where(half == 0, mine, other)
    second = jnp.where(half == 0, other, mine)
    return jnp.concatenate([first, second]).astype(F32)


def small_sum(array, axis):
    left = bits(axis)
    while left:
        one, left = left[0], left[1:]
        if left:
            two, left = left[0], left[1:]
            array = (array + swap(array, axis, one)) + (swap(array, axis, two) + swap(array, axis, one | two))
        else:
            array = array + swap(array, axis, one)
    return array


def shards(
    inputs,
    norm_gain,
    norm_shift,
    gate_weight,
    gate_bias,
    value_weight,
    value_bias,
    log_step,
    decay_rate,
    frequency,
    readout,
    passthrough,
    expand_weight,
    output_weight,
    output_bias,
    cotangent,
):
    rows = lax.axis_size("row")
    cols = lax.axis_size("col")
    row_index = lax.axis_index("row")
    col_index = lax.axis_index("col")
    tokens, narrow = inputs.shape
    block = tokens // rows
    half_ff = FF // cols
    row_channels = VALUE // rows
    channels = row_channels // cols
    local_channels = rows * channels

    def own_channels(array):
        return lax.dynamic_slice_in_dim(array, col_index * channels, channels, 0)

    state_params = tuple(own_channels(a) for a in (log_step, decay_rate, frequency, readout))
    own_pass = own_channels(passthrough)
    weights, weights_pullback = jax.vjp(mode_weights, *state_params)
    real_rate, imag_rate, mode_real, mode_imag = weights
    growth = jnp.exp(real_rate)
    z_real, z_imag = growth * jnp.cos(imag_rate), growth * jnp.sin(imag_rate)
    kernel, kernel_flipped = generate(z_real, z_imag, mode_real, mode_imag, tokens)

    me = row_index.astype(jnp.int32).reshape(1)
    every = range(rows)

    def across(own, other):
        return [jnp.where(col_index == 0, own, other), jnp.where(col_index == 0, other, own)]

    def natural(blocks):
        stacked = jnp.stack(blocks)
        return jnp.stack([lax.dynamic_index_in_dim(stacked, row_index ^ q, 0, False) for q in every])

    def features(pieces):
        own = jnp.stack(pieces)
        first, second = across(own, swap(own, "col", 1))
        return jnp.concatenate([part[q] for q in every for part in (first, second)], axis=1)

    def own_features(array, flip=0):
        return jnp.concatenate(
            [
                lax.dynamic_slice_in_dim(array, (q * cols + (col_index ^ flip)) * narrow, narrow, array.ndim - 1)
                for q in every
            ],
            axis=-1,
        )

    def xor_features(vector):
        blocks = vector.reshape(rows, -1)
        return jnp.concatenate([lax.dynamic_index_in_dim(blocks, row_index ^ q, 0, False) for q in every])

    def token_blocks(array):
        blocks = array.reshape(rows, block, narrow)
        return [lax.dynamic_index_in_dim(blocks, row_index ^ q, 0, False) for q in every]

    x_full = features(exchange_blocks(token_blocks(inputs), "row"))
    value_half = lax.dynamic_index_in_dim(
        value_weight.reshape(-1, rows, cols, channels), col_index, 2, False
    ).reshape(-1, local_channels)
    value_half = jnp.concatenate(gather_blocks(value_half, "row"))
    upstream = features(exchange_blocks(token_blocks(cotangent), "row"))
    output_full = jnp.concatenate(gather_blocks(output_weight, "row"), axis=1)
    gate_full = jnp.concatenate(gather_blocks(gate_weight, "row"))
    expand_full = jnp.concatenate(gather_blocks(expand_weight, "row"))
    value_bias_half = lax.dynamic_index_in_dim(
        value_bias.reshape(rows, cols, channels), col_index, 1, False
    ).reshape(local_channels, 1)
    gate_bias_half = lax.dynamic_slice_in_dim(gate_bias, col_index * half_ff, half_ff)
    gain = xor_features(norm_gain)
    shift = xor_features(norm_shift)

    source = x_full.astype(F32)
    row_mean = jnp.mean(source, axis=-1, keepdims=True)
    centered = source - row_mean
    variance = jnp.mean(centered * centered, axis=-1, keepdims=True)
    rescale = lax.rsqrt(variance + EPSILON)
    normed = centered * rescale
    acts = (normed * gain + shift).astype(BF)

    value_pre = dot(value_half, acts, 0, 1) + value_bias_half
    values = gelu(value_pre).astype(BF).reshape(rows, channels, block)
    values = [lax.dynamic_index_in_dim(values, row_index ^ q, 0, False) for q in every]
    values = jnp.stack(exchange_blocks(values, "row"))
    mixed = forward(me, values, kernel, own_pass, BF)
    mixed = jnp.stack(exchange_blocks([mixed[q] for q in every], "row"))
    mixed = jnp.stack(across(mixed, swap(mixed, "col", 1)), axis=1).reshape(VALUE, block)

    gate_pre = dot(acts, gate_full, 1, 0) + gate_bias_half
    gate_act = gelu(gate_pre)
    product_back = dot(upstream, output_full, 1, 1)
    expand_back = (product_back * gate_act).astype(BF)
    mixed_back = dot(expand_full, expand_back, 1, 1).reshape(rows, cols, channels, block)
    sent = lax.dynamic_index_in_dim(mixed_back, 1 - col_index, 1, False).astype(BF)
    mixed_back = lax.dynamic_index_in_dim(mixed_back, col_index, 1, False)
    mixed_back = (mixed_back + swap(sent, "col", 1).astype(F32)).astype(BF)
    mixed_back = jnp.stack(exchange_blocks([mixed_back[q] for q in every], "row"))

    expanded = dot(mixed, expand_full, 0, 0)
    product = (gate_act * expanded).astype(BF)
    gate_back = gelu_back(gate_pre, product_back * expanded).astype(BF)

    def parts(array, axis):
        return jnp.split(array, rows, axis)

    def row_sum(left_parts, right, left_dim, right_dim):
        return reduce_blocks([dot(part, right, left_dim, right_dim).astype(BF) for part in left_parts], "row")

    output_weight_delta = reduce_blocks(
        [dot(product, part, 0, 0).astype(BF) for part in parts(upstream, 1)], "row"
    )
    gate_weight_delta = row_sum(parts(acts, 1), gate_back, 0, 0)
    expand_delta = row_sum(parts(mixed, 0), expand_back, 1, 0)
    output_weight_delta, gate_weight_delta, expand_delta = (
        pair_sum(a, "dp") for a in (output_weight_delta, gate_weight_delta, expand_delta)
    )
    gate_bias_delta = jnp.sum(gate_back, axis=0, dtype=F32)

    out_sum = dot(product, output_full, 1, 0)
    out_sum = own_features(out_sum) + swap(own_features(out_sum, 1).astype(BF), "col", 1).astype(F32)
    bias = own_features(xor_features(output_bias))
    block_output = (own_features(source) + out_sum + bias).astype(BF)
    block_output = natural(exchange_blocks(parts(block_output, 1), "row")).reshape(tokens, narrow)

    values_back, sums = backward(me, values, mixed_back, kernel_flipped, own_pass, z_real, z_imag, BF)
    values_back = natural(exchange_blocks([values_back[q] for q in every], "row")).reshape(local_channels, block)
    value_back = gelu_back(value_pre, values_back.astype(F32)).astype(BF)
    value_weight_delta = row_sum(parts(acts, 1), value_back, 0, 1)
    value_bias_delta = jnp.sum(value_back, axis=1, dtype=F32)
    passthrough_delta = jnp.sum(mixed_back.astype(F32) * values.astype(F32), axis=(0, 2))
    first_real, first_imag, second_real, second_imag = sums
    state_deltas = weights_pullback(
        (
            mode_real * second_real - mode_imag * second_imag,
            -mode_real * second_imag - mode_imag * second_real,
            first_real,
            -first_imag,
        )
    )

    acts_back = dot(gate_back, gate_full, 1, 1) + dot(value_back, value_half, 0, 1)
    weighted = acts_back * gain
    moments = jnp.stack([jnp.sum(weighted, axis=1), jnp.sum(weighted * normed, axis=1)])
    moments = small_sum(moments, "col") / D
    acts_back = own_features(acts_back) + swap(own_features(acts_back, 1).astype(BF), "col", 1).astype(F32)
    own_normed = own_features(normed)
    gain_delta = jnp.sum(acts_back * own_normed, axis=0)
    shift_delta = jnp.sum(acts_back, axis=0)
    input_delta = rescale * (acts_back * own_features(gain) - moments[0][:, None] - own_normed * moments[1][:, None])
    input_delta = natural(exchange_blocks(parts(input_delta.astype(BF), 1), "row")).reshape(tokens, narrow)
    input_delta = cotangent.astype(F32) + input_delta.astype(F32)

    norm_parts = jnp.stack([gain_delta, shift_delta]).reshape(2, rows, narrow)
    norm_parts = exchange_blocks([norm_parts[:, q] for q in every], "row")
    while len(norm_parts) > 1:
        norm_parts = [a + b for a, b in zip(norm_parts[::2], norm_parts[1::2])]
    bias_parts = small_sum(jnp.concatenate([gate_bias_delta, value_bias_delta]), "row")
    small = jnp.concatenate(
        [
            norm_parts[0].reshape(-1),
            bias_parts,
            jnp.sum(cotangent, axis=0, dtype=F32),
            state_deltas[0],
            passthrough_delta,
        ]
    )
    small = small_sum(small, "dp")
    gain_sum, shift_sum, gate_bias_sum, value_bias_sum, bias_sum, shared = jnp.split(
        small,
        [narrow, 2 * narrow, 2 * narrow + half_ff, 2 * narrow + half_ff + local_channels, 3 * narrow + half_ff + local_channels],
    )
    shared = jnp.concatenate([value_bias_sum, shared]).reshape(rows + 2, channels)
    shared = jnp.stack(across(shared, swap(shared, "col", 1)), axis=1).reshape(-1)
    value_bias_sum, step_sum, pass_sum = jnp.split(shared, [VALUE, VALUE + row_channels])

    state = jnp.concatenate(state_deltas[1:], axis=1)
    late = jnp.concatenate([value_weight_delta.reshape(-1), state.reshape(-1)]).reshape(-1, local_channels)
    late = pair_sum(late, "dp").astype(BF)
    late = jnp.stack(across(late, swap(late, "col", 1)))
    value_weight_delta = late[:, : value_weight_delta.shape[0]].reshape(cols, -1, rows, channels)
    value_weight_delta = value_weight_delta.transpose(1, 2, 0, 3).reshape(-1, VALUE).astype(F32)
    state = late[:, value_weight_delta.shape[0] :].reshape(row_channels, -1).astype(F32)
    modes = decay_rate.shape[1]
    return (
        block_output,
        input_delta,
        gain_sum,
        shift_sum,
        gate_weight_delta,
        gate_bias_sum,
        value_weight_delta,
        value_bias_sum,
        step_sum,
        state[:, :modes],
        state[:, modes : 2 * modes],
        state[:, 2 * modes :],
        pass_sum,
        expand_delta,
        output_weight_delta,
        bias_sum,
    )


def solution(mesh):
    placed = (
        P("dp", ("row", "col")),
        P(),
        P(),
        P("row", "col"),
        P(),
        P("row", None),
        P(),
        P("row"),
        P("row", None),
        P("row", None),
        P("row", None),
        P("row"),
        P("row", "col"),
        P("col", "row"),
        P(),
        P("dp", ("row", "col")),
    )
    return jax.shard_map(
        shards,
        mesh=mesh,
        in_specs=placed,
        out_specs=(
            P("dp", ("row", "col")),
            P("dp", ("row", "col")),
            P(("row", "col")),
            P(("row", "col")),
            P("row", "col"),
            P("col"),
            P("row", None),
            P(),
            P("row"),
            P("row", None),
            P("row", None),
            P("row", None),
            P("row"),
            P("row", "col"),
            P("col", "row"),
            P(("row", "col")),
        ),
        check_vma=False,
    )
```

```python
from functools import partial
import math

import jax
import jax.numpy as jnp
from jax import lax
from jax.experimental import pallas as pl
from jax.experimental.pallas import tpu as pltpu
from jax.sharding import PartitionSpec as P

D = 1024
FF = 3072
VALUE = 512
LEN = 2048
EPSILON = 1e-05
BL = 128
GROUP = 8
BF = jnp.bfloat16
F32 = jnp.float32


def dot(left, right, left_dim, right_dim):
    return lax.dot_general(
        left, right, (((left_dim,), (right_dim,)), ((), ())), preferred_element_type=F32
    )


def gelu(pre_act):
    return jax.nn.gelu(pre_act, approximate=True)


def gelu_back(pre_act, upstream):
    return jax.vjp(gelu, pre_act)[1](upstream)[0]


def mode_weights(log_step, decay_rate, frequency, readout):
    time_step = jnp.exp(log_step)[:, None]
    real_rate = -decay_rate * time_step
    imag_rate = frequency * time_step
    growth = jnp.exp(real_rate)
    shift_real = growth * jnp.cos(imag_rate) - 1.0
    shift_imag = growth * jnp.sin(imag_rate)
    modulus = decay_rate * decay_rate + frequency * frequency
    ratio_real = (shift_imag * frequency - shift_real * decay_rate) / modulus
    ratio_imag = (-shift_imag * decay_rate - shift_real * frequency) / modulus
    modes = decay_rate.shape[1]
    out_real = readout[:, :modes]
    out_imag = readout[:, modes:]
    mode_real = out_real * ratio_real - out_imag * ratio_imag
    mode_imag = out_real * ratio_imag + out_imag * ratio_real
    return (real_rate, imag_rate, mode_real, mode_imag)


def cmul(a, b):
    return a[0]*b[0]-a[1]*b[1], a[0]*b[1]+a[1]*b[0]

def squarings(z, n):
    out=[z]
    for _ in range(n):
        r,i=out[-1]
        out.append((r*r-i*i, 2.0*r*i))
    return out

def ladder(steps, rows, order, first=None):
    M = steps[0][0].shape[1]
    idx = lax.broadcasted_iota(jnp.int32, (8, M), 0)
    if order < 0: idx = 7-idx
    wr = jnp.ones((8,M), jnp.float32); wi = jnp.zeros((8,M), jnp.float32)
    for b in range(3):
        hit = (idx >> b) & 1
        nr, ni = cmul((wr,wi), steps[b])
        wr = jnp.where(hit==1, nr, wr); wi = jnp.where(hit==1, ni, wi)
    groups=[(wr,wi)]
    k=3
    while len(groups)*8 < rows:
        groups += [cmul(g, steps[k]) for g in groups]
        k+=1
    if order<0: groups = groups[::-1]
    return jnp.concatenate([g[0] for g in groups],0), jnp.concatenate([g[1] for g in groups],0)

def row(p, i):
    return p[0][i:i+1], p[1][i:i+1]

def two_terms(x):
    high = x.astype(BF)
    return high, (x - high.astype(F32)).astype(BF)


def gen_kernel(nb, zr, zi, cr, ci, *refs):
    k_out, kr_out = refs[-2:]
    steps = squarings((zr[...], zi[...]), 6 + int(math.log2(nb)))
    rev = (lax.broadcasted_iota(jnp.int32,(BL,BL),0)+lax.broadcasted_iota(jnp.int32,(BL,BL),1)==BL-1).astype(F32).astype(BF)
    nt = (((1,),(1,)),((),()))
    for i in range(GROUP):
        st = [row(x,i) for x in steps]
        near = ladder(st[:7], BL, 1)
        far = ladder(st[7:], nb, 1)
        lead = cmul((cr[i:i+1,:], ci[i:i+1,:]), far)
        lh, ll = two_terms(jnp.concatenate([lead[0], -lead[1]],1))
        nh, nl = two_terms(jnp.concatenate(near,1))
        first = lax.dot_general(jnp.concatenate([lh, ll]), nh, nt, preferred_element_type=F32)
        k = first[:nb] + (first[nb:] + lax.dot_general(lh, nl, nt, preferred_element_type=F32))
        kb = k.astype(BF)
        k_out[i] = kb
        kr_out[i] = jnp.dot(kb, rev, preferred_element_type=F32).astype(BF)


def cost(microseconds):
    return pl.CostEstimate(flops=int(microseconds * 1e9), bytes_accessed=1 << 20, transcendentals=0)


def generate(modes, length, part, parts, earlier=()):
    C, M = modes[0].shape
    nb = length//BL
    steps = C//GROUP//parts
    spec = pl.BlockSpec((GROUP, M), lambda i:(i + part*steps,0))
    ospec = pl.BlockSpec((GROUP, nb, BL), lambda i:(i + part*steps,0,0))
    sh = jax.ShapeDtypeStruct((C,nb,BL), BF)
    return pl.pallas_call(partial(gen_kernel, nb), grid=(steps,), in_specs=[spec]*4 + [pl.BlockSpec(memory_space=pl.ANY)]*len(earlier), out_specs=[ospec]*2,
        out_shape=[sh,sh], cost_estimate=cost(18/parts), input_output_aliases={4+k:k for k in range(len(earlier))})(*modes, *earlier)


def toeplitz_blocks(load, count, shift):
    r = lax.broadcasted_iota(jnp.int32,(BL,BL),0); c = lax.broadcasted_iota(jnp.int32,(BL,BL),1)
    mask = c >= r + shift
    def rot(j):
        x = load(j)
        if x is None: return jnp.zeros((BL,BL), jnp.float32)
        return pltpu.roll(jnp.broadcast_to(x,(BL,BL)), shift, 1, stride=1, stride_axis=0)
    out=[]
    cur = rot(0)
    for j in range(count):
        nxt = rot(j+1)
        out.append(jnp.where(mask, nxt, cur).astype(jnp.bfloat16))
        cur = nxt
    return jnp.concatenate(out,0)

def shifted(pad_ref, nb, d):
    return pad_ref[pl.ds(nb-d, nb), :]

def fwd_kernel(nb, tb, me_ref, v_ref, kr_ref, p_ref, out_ref, pad):
    per = tb//BL
    me = me_ref[0]
    pad[0:nb,:] = jnp.zeros((nb,BL), jnp.float32)
    for i in range(GROUP):
        def load(j):
            if j==0: return None
            j-=1
            return v_ref[me ^ (j//per), i:i+1, (j%per)*BL:(j%per+1)*BL].astype(jnp.float32)
        H = toeplitz_blocks(load, nb, 0)
        pad[nb:2*nb,:] = kr_ref[i].astype(jnp.float32)
        X = jnp.concatenate([shifted(pad,nb,d) for d in range(nb)],1).astype(jnp.bfloat16)
        out = jnp.dot(X, H, preferred_element_type=jnp.float32)
        for j in range(nb):
            sl = (me ^ (j//per), slice(i,i+1), slice((j%per)*BL,(j%per+1)*BL))
            out_ref[sl] = (out[j:j+1,:] + p_ref[i:i+1,:]*v_ref[sl].astype(jnp.float32)).astype(out_ref.dtype)

def forward(me, v, kr, passthrough, out_dtype=jnp.float32):
    R,C,tb = v.shape
    nb = R*tb//BL
    spec = pl.BlockSpec((R,GROUP,tb), lambda i,_:(0,i,0))
    kspec = pl.BlockSpec((GROUP,nb,BL), lambda i,_:(i,0,0))
    pspec = pl.BlockSpec((GROUP,1), lambda i,_:(i,0))
    grid_spec = pltpu.PrefetchScalarGridSpec(num_scalar_prefetch=1, grid=(C//GROUP,), in_specs=[spec,kspec,pspec], out_specs=spec,
        scratch_shapes=[pltpu.VMEM((2*nb,BL),jnp.float32)])
    return pl.pallas_call(partial(fwd_kernel,nb,tb), grid_spec=grid_spec,
        out_shape=jax.ShapeDtypeStruct(v.shape,out_dtype), cost_estimate=cost(13))(me,v,kr,passthrough[:,None])

def bwd_kernel(prec, nb, tb, me_ref, v_ref, m_ref, k_ref, p_ref, zr, zi, *refs):
    vb_ref, s_ref, pad, pad2 = refs[-4:]
    per = tb//BL
    pad[0:nb,:] = jnp.zeros((nb,BL), jnp.float32)
    pad2[0:nb,:] = jnp.zeros((nb,BL), jnp.float32)
    me = me_ref[0]
    steps = squarings((zr[...], zi[...]), 6 + int(math.log2(nb)))
    rev = (lax.broadcasted_iota(jnp.int32,(BL,BL),0)+lax.broadcasted_iota(jnp.int32,(BL,BL),1)==BL-1).astype(jnp.float32).astype(jnp.bfloat16)
    lane = lax.broadcasted_iota(jnp.int32,(nb,BL),1).astype(jnp.float32)
    M = zr.shape[1]
    arow = (nb-1-lax.broadcasted_iota(jnp.int32,(nb,M),0)).astype(jnp.float32)*BL
    for i in range(GROUP):
        def at(j): return (me ^ (j//per), slice(i,i+1), slice((j%per)*BL,(j%per+1)*BL))
        def load(j):
            if j==nb: return None
            return m_ref[at(j)].astype(jnp.float32)
        H = toeplitz_blocks(load, nb, 1)
        pad[nb:2*nb,:] = k_ref[i].astype(jnp.float32)
        for j in range(nb):
            pad2[nb+j:nb+j+1,:] = v_ref[at(j)].astype(jnp.float32)
        pad2[nb:2*nb,:] = jnp.dot(pad2[nb:2*nb,:].astype(jnp.bfloat16), rev, preferred_element_type=jnp.float32)
        X = jnp.concatenate([jnp.concatenate([shifted(pad,nb,nb-1-e) for e in range(nb)],1), jnp.concatenate([shifted(pad2,nb,nb-1-e) for e in range(nb)],1)],0).astype(jnp.bfloat16)
        out = jnp.dot(X, H, preferred_element_type=jnp.float32)
        for j in range(nb):
            vb_ref[at(j)] = (out[nb-1-j:nb-j,:] + p_ref[i:i+1,:]*m_ref[at(j)].astype(jnp.float32)).astype(vb_ref.dtype)
        kb = out[nb:,:]
        st = [row(s,i) for s in steps]
        near = ladder(st[:7], BL, 1)
        far = ladder(st[7:], nb, -1)
        U = jnp.dot(jnp.concatenate([kb, kb*lane],0), jnp.concatenate(near,1), precision=prec, preferred_element_type=jnp.float32)
        u = U[:nb,:M], U[:nb,M:]
        w = U[nb:,:M]+arow*u[0], U[nb:,M:]+arow*u[1]
        s1 = cmul(u, far); s2 = cmul(w, far)
        for n,x in enumerate((*s1,*s2)):
            s_ref[n, i:i+1, :] = jnp.sum(x,0,keepdims=True)

def backward(me, v, mb, k, passthrough, zr, zi, part, parts, earlier=(), prec=lax.Precision.DEFAULT):
    R,C,tb = v.shape
    M = zr.shape[1]
    nb = R*tb//BL
    steps = C//GROUP//parts
    spec = pl.BlockSpec((R,GROUP,tb), lambda i,_:(0,i + part*steps,0))
    kspec = pl.BlockSpec((GROUP,nb,BL), lambda i,_:(i + part*steps,0,0))
    pspec = pl.BlockSpec((GROUP,1), lambda i,_:(i + part*steps,0))
    zspec = pl.BlockSpec((GROUP,M), lambda i,_:(i + part*steps,0))
    grid_spec = pltpu.PrefetchScalarGridSpec(num_scalar_prefetch=1, grid=(steps,),
        in_specs=[spec,spec,kspec,pspec,zspec,zspec] + [pl.BlockSpec(memory_space=pl.ANY)]*len(earlier),
        out_specs=[spec, pl.BlockSpec((4,GROUP,M), lambda i,_:(0,i + part*steps,0))], scratch_shapes=[pltpu.VMEM((2*nb,BL),jnp.float32)]*2)
    return pl.pallas_call(partial(bwd_kernel,prec,nb,tb), grid_spec=grid_spec,
        out_shape=[jax.ShapeDtypeStruct(v.shape,BF), jax.ShapeDtypeStruct((4,C,M),jnp.float32)],
        cost_estimate=cost(26/parts), input_output_aliases={7+n:n for n in range(len(earlier))})(me,v,mb,k,passthrough[:,None],zr,zi,*earlier)


def bits(axis):
    size = lax.axis_size(axis)
    return [1 << k for k in range(size.bit_length() - 1)]


def swap(array, axis, mask):
    return lax.ppermute(array, axis, [(i, i ^ mask) for i in range(lax.axis_size(axis))])


def gather_rows(array, dim=0):
    for bit in reversed(bits("row")):
        array = jnp.concatenate([array, swap(array, "row", bit)], axis=dim)
    return array


def exchange_blocks(blocks, axis):
    return [blocks[0]] + [swap(blocks[q], axis, q) for q in range(1, len(blocks))]


def fence(*values):
    return lax.optimization_barrier(values)


def halve(array, dim):
    return jnp.split(array, 2, dim)


class PairSum:
    def __init__(self, array, axis):
        self.axis = axis
        index = lax.axis_index(axis)
        self.half = (index ^ (index >> 1)) & 1
        length = array.shape[0] // 2
        self.kept = lax.dynamic_slice_in_dim(array, self.half * length, length)
        self.sent = lax.dynamic_slice_in_dim(array, (1 - self.half) * length, length).astype(BF)

    def pairs(self):
        return swap(self.sent, self.axis, 1)

    def add_pairs(self, got):
        self.total = (self.kept.astype(F32) + got.astype(F32)).astype(BF)

    def mirrored(self):
        for bit in bits(self.axis)[2:]:
            self.total = (self.total.astype(F32) + swap(self.total, self.axis, bit).astype(F32)).astype(BF)
        return swap(self.total, self.axis, 3) if lax.axis_size(self.axis) > 2 else None

    def add_mirrored(self, got):
        if got is not None:
            self.total = (self.total.astype(F32) + got.astype(F32)).astype(BF)

    def back(self):
        return swap(self.total, self.axis, 1)

    def join(self, got):
        first = jnp.where(self.half == 0, self.total, got)
        second = jnp.where(self.half == 0, got, self.total)
        return jnp.concatenate([first, second]).astype(F32)


def small_sum(array, axis):
    left = bits(axis)
    while left:
        one, left = left[0], left[1:]
        if left:
            two, left = left[0], left[1:]
            array = (array + swap(array, axis, one)) + (swap(array, axis, two) + swap(array, axis, one | two))
        else:
            array = array + swap(array, axis, one)
    return array


def shards(
    inputs,
    norm_gain,
    norm_shift,
    gate_weight,
    gate_bias,
    value_weight,
    value_bias,
    log_step,
    decay_rate,
    frequency,
    readout,
    passthrough,
    expand_weight,
    output_weight,
    output_bias,
    cotangent,
):
    rows = lax.axis_size("row")
    cols = lax.axis_size("col")
    row_index = lax.axis_index("row")
    col_index = lax.axis_index("col")
    tokens, narrow = inputs.shape
    block = tokens // rows
    half_ff = FF // cols
    row_channels = VALUE // rows
    channels = row_channels // cols
    local_channels = rows * channels

    def own_channels(array):
        return lax.dynamic_slice_in_dim(array, col_index * channels, channels, 0)

    state_params = tuple(own_channels(a) for a in (log_step, decay_rate, frequency, readout))
    own_pass = own_channels(passthrough)
    weights, weights_pullback = jax.vjp(mode_weights, *state_params)
    real_rate, imag_rate, mode_real, mode_imag = weights
    growth = jnp.exp(real_rate)
    z_real, z_imag = growth * jnp.cos(imag_rate), growth * jnp.sin(imag_rate)
    me = row_index.astype(jnp.int32).reshape(1)
    every = range(rows)
    order = [0]
    for bit in reversed(bits("row")):
        order = order + [q | bit for q in order]

    def across(own, other):
        return [jnp.where(col_index == 0, own, other), jnp.where(col_index == 0, other, own)]

    def at_xor(array, q, dim=0):
        return lax.dynamic_index_in_dim(array, row_index ^ q, dim, False)

    def natural(blocks):
        stacked = jnp.stack(blocks)
        return jnp.stack([at_xor(stacked, q) for q in every])

    def features(own, other):
        first, second = across(own, other)
        return jnp.concatenate([part[k] for k in every for part in (first, second)], axis=1)

    def own_features(array, flip=0):
        return jnp.concatenate(
            [
                lax.dynamic_slice_in_dim(array, (k * cols + (col_index ^ flip)) * narrow, narrow, array.ndim - 1)
                for k in every
            ],
            axis=-1,
        )

    def by_order(blocks):
        return [blocks[q] for q in order]

    def ordered_features(vectors):
        blocks = vectors.reshape(vectors.shape[0], rows, -1)
        return jnp.concatenate([at_xor(blocks, q, 1) for q in order], axis=1)

    modes_in = (z_real, z_imag, mode_real, mode_imag)
    value_half = lax.dynamic_index_in_dim(
        value_weight.reshape(-1, rows, cols, channels), col_index, 2, False
    ).reshape(-1, local_channels)
    value_bias_half = lax.dynamic_index_in_dim(
        value_bias.reshape(rows, cols, channels), col_index, 1, False
    ).reshape(local_channels, 1)
    gate_bias_half = lax.dynamic_slice_in_dim(gate_bias, col_index * half_ff, half_ff)
    gain, shift, bias = ordered_features(jnp.stack([norm_gain, norm_shift, output_bias]))

    x_parts = exchange_blocks([at_xor(inputs.reshape(rows, block, narrow), q) for q in every], "row")
    value_pair = swap(value_half, "row", 2)
    x_parts, value_pair, modes_in, upstream_blocks, gate_in = fence(
        x_parts, value_pair, modes_in, cotangent.reshape(rows, block, narrow), gate_weight
    )
    x_own = jnp.stack(by_order(x_parts))
    x_other = swap(x_own, "col", 1)
    value_half = jnp.concatenate([value_half, value_pair])
    value_pair = swap(value_half, "row", 1)
    g_parts = exchange_blocks([at_xor(upstream_blocks, q) for q in every], "row")
    gate_pair = swap(gate_in, "row", 2)
    kernels = generate(modes_in, tokens, 0, 2)
    x_other, g_parts, value_pair, kernels, output_in = fence(x_other, g_parts, value_pair, kernels, output_weight)
    value_half = jnp.concatenate([value_half, value_pair])
    x_full = features(x_own, x_other)
    g_own = jnp.stack(by_order(g_parts))
    g_other = swap(g_own, "col", 1)
    output_pair = swap(output_in, "row", 2)

    source = x_full.astype(F32)
    row_mean = jnp.mean(source, axis=-1, keepdims=True)
    centered = source - row_mean
    variance = jnp.mean(centered * centered, axis=-1, keepdims=True)
    rescale = lax.rsqrt(variance + EPSILON)
    normed = centered * rescale
    acts = (normed * gain + shift).astype(BF)

    value_pre = dot(value_half, acts, 0, 1) + value_bias_half
    values = gelu(value_pre).astype(BF).reshape(rows, channels, block)
    values_sent = [at_xor(values, q) for q in every]
    values_sent, modes_in, kernels = fence(values_sent, modes_in, kernels)
    values = exchange_blocks(values_sent, "row")
    kernels = generate(modes_in, tokens, 1, 2, kernels)
    values, kernels, g_other, gate_pair, expand_in = fence(values, kernels, g_other, gate_pair, expand_weight)
    kernel, kernel_flipped = kernels
    values = jnp.stack(values)
    gate_pair = jnp.concatenate([gate_in, gate_pair])
    gate_other = swap(gate_pair, "row", 1)
    expand_pair = swap(expand_in, "row", 2)
    mixed = forward(me, values, kernel, own_pass, BF)
    mixed, gate_other, output_pair, expand_pair = fence(mixed, gate_other, output_pair, expand_pair)
    mixed = exchange_blocks([mixed[q] for q in every], "row")
    output_pair = jnp.concatenate([output_in, output_pair], axis=1)
    output_other = swap(output_pair, "row", 1)
    expand_pair = jnp.concatenate([expand_in, expand_pair])
    expand_other = swap(expand_pair, "row", 1)
    gate_full = jnp.concatenate([gate_pair, gate_other])
    upstream = features(g_own, g_other)
    mixed, output_other, expand_other = fence(mixed, output_other, expand_other)
    mixed = jnp.stack(by_order(mixed))
    mixed = jnp.stack(across(mixed, swap(mixed, "col", 1)), axis=1).reshape(VALUE, block)
    output_full = jnp.concatenate([output_pair, output_other], axis=1)
    expand_full = jnp.concatenate([expand_pair, expand_other])

    gate_pre = dot(acts, gate_full, 1, 0) + gate_bias_half
    gate_act = gelu(gate_pre)
    product_back = dot(upstream, output_full, 1, 1)
    expand_back = (product_back * gate_act).astype(BF)
    mixed_back = dot(expand_full, expand_back, 1, 1).reshape(rows, cols, channels, block)
    sent = lax.dynamic_index_in_dim(mixed_back, 1 - col_index, 1, False).astype(BF)
    mixed_back = lax.dynamic_index_in_dim(mixed_back, col_index, 1, False)
    mixed_back = (mixed_back + swap(sent, "col", 1).astype(F32)).astype(BF)

    expanded = dot(mixed, expand_full, 0, 0)
    expand_kept, expand_sent = [dot(piece, expand_back, 1, 0).astype(BF) for piece in halve(mixed, 0)]
    expand_got = swap(expand_sent, "row", 1)
    product = (gate_act * expanded).astype(BF)
    output_kept, output_sent = [dot(product, piece, 0, 0).astype(BF) for piece in halve(upstream, 1)]
    output_got = swap(output_sent, "row", 1)
    gate_back = gelu_back(gate_pre, product_back * expanded).astype(BF)
    gate_kept, gate_sent = [dot(piece, gate_back, 0, 0).astype(BF) for piece in halve(acts, 1)]
    gate_bias_delta = jnp.sum(gate_back, axis=0, dtype=F32)

    def second(kept, got, dim):
        total = kept.astype(F32) + got.astype(F32)
        return halve(total.astype(BF), dim)

    gate_got = swap(gate_sent, "row", 1)
    mixed_back = exchange_blocks(by_order(mixed_back), "row")
    mixed_back, expand_got, output_got, gate_got = fence(mixed_back, expand_got, output_got, gate_got)
    mixed_back = jnp.stack(mixed_back)
    expand_kept, expand_sent = second(expand_kept, expand_got, 0)
    output_kept, output_sent = second(output_kept, output_got, 1)
    gate_kept, gate_sent = second(gate_kept, gate_got, 0)
    mixed_back, expand_sent, output_sent, gate_sent = fence(mixed_back, expand_sent, output_sent, gate_sent)
    expand_got = swap(expand_sent, "row", 2)
    output_got = swap(output_sent, "row", 2)
    state_args = (me, values, mixed_back, kernel_flipped, own_pass, z_real, z_imag)
    back = backward(*state_args, 0, 2)
    back, expand_got = fence(back, expand_got)
    expand_sum = PairSum(expand_kept.astype(F32) + expand_got.astype(F32), "dp")
    back, expand_sum.sent, gate_sent = fence(back, expand_sum.sent, gate_sent)
    expand_got = expand_sum.pairs()
    gate_got = swap(gate_sent, "row", 2)
    back = backward(*state_args, 1, 2, back)
    back, expand_got, output_got = fence(back, expand_got, output_got)
    values_back, sums = back
    values_back = exchange_blocks([values_back[q] for q in every], "row")
    expand_sum.add_pairs(expand_got)
    output_sum = PairSum(output_kept.astype(F32) + output_got.astype(F32), "dp")
    output_sum.sent, expand_sum.total = fence(output_sum.sent, expand_sum.total)
    expand_got = expand_sum.mirrored()
    output_got = output_sum.pairs()
    values_back, expand_got, output_got = fence(values_back, expand_got, output_got)
    expand_sum.add_mirrored(expand_got)
    output_sum.add_pairs(output_got)
    expand_got = expand_sum.back()
    output_got = output_sum.mirrored()

    def to_tokens(array):
        blocks = by_order(jnp.split(array, rows, 1))
        return natural(exchange_blocks(blocks, "row")).reshape(tokens, narrow)

    values_back = natural(values_back).reshape(local_channels, block)
    value_back = gelu_back(value_pre, values_back.astype(F32)).astype(BF)
    value_kept, value_sent = [dot(piece, value_back, 0, 1).astype(BF) for piece in halve(acts, 1)]
    value_kept, value_sent = second(value_kept, swap(value_sent, "row", 1), 0)
    value_weight_delta = value_kept.astype(F32) + swap(value_sent, "row", 2).astype(F32)
    value_bias_delta = jnp.sum(value_back, axis=1, dtype=F32)
    passthrough_delta = jnp.sum(mixed_back.astype(F32) * values.astype(F32), axis=(0, 2))
    first_real, first_imag, second_real, second_imag = sums
    state_deltas = weights_pullback(
        (
            mode_real * second_real - mode_imag * second_imag,
            -mode_real * second_imag - mode_imag * second_real,
            first_real,
            -first_imag,
        )
    )

    acts_back = dot(gate_back, gate_full, 1, 1) + dot(value_back, value_half, 0, 1)
    weighted = acts_back * gain
    moments = jnp.stack([jnp.sum(weighted, axis=1), jnp.sum(weighted * normed, axis=1)])
    acts_sent = own_features(acts_back, 1).astype(BF)
    acts_got = swap(acts_sent, "col", 1)
    moments = small_sum(moments, "col") / D
    acts_got, moments, gate_got, expand_got = fence(acts_got, moments, gate_got, expand_got)
    expand_delta = expand_sum.join(expand_got)
    gate_sum = PairSum(gate_kept.astype(F32) + gate_got.astype(F32), "dp")
    gate_got = gate_sum.pairs()

    acts_back = own_features(acts_back) + acts_got.astype(F32)
    own_normed = own_features(normed)
    gain_delta = jnp.sum(acts_back * own_normed, axis=0)
    shift_delta = jnp.sum(acts_back, axis=0)
    input_delta = rescale * (acts_back * own_features(gain) - moments[0][:, None] - own_normed * moments[1][:, None])
    input_delta = cotangent.astype(F32) + to_tokens(input_delta.astype(BF)).astype(F32)
    input_delta, output_got, gate_got, product = fence(input_delta, output_got, gate_got, product)
    output_sum.add_mirrored(output_got)
    gate_sum.add_pairs(gate_got)
    output_got = output_sum.back()
    gate_got = gate_sum.mirrored()
    out_sum = dot(product, output_full, 1, 0)
    out_sum = own_features(out_sum) + swap(own_features(out_sum, 1).astype(BF), "col", 1).astype(F32)
    block_output = to_tokens((own_features(source) + out_sum + own_features(bias)).astype(BF))
    output_weight_delta = output_sum.join(output_got)
    gate_sum.add_mirrored(gate_got)
    gate_weight_delta = gate_sum.join(gate_sum.back())

    biases = jnp.concatenate([gate_bias_delta, value_bias_delta])
    norms = jnp.stack([gain_delta, shift_delta]).reshape(2, rows, narrow)
    small = exchange_blocks(
        [jnp.concatenate([norms[:, k].reshape(-1), biases]) for k in (order.index(q) for q in every)], "row"
    )
    while len(small) > 1:
        small = [a + b for a, b in zip(small[::2], small[1::2])]
    small = jnp.concatenate(
        [small[0], jnp.sum(cotangent, axis=0, dtype=F32), state_deltas[0], passthrough_delta]
    )
    small = small_sum(small, "dp")
    ends = [narrow, 2 * narrow, 2 * narrow + half_ff, 2 * narrow + half_ff + local_channels]
    gain_sum, shift_sum, gate_bias_sum, value_bias_sum, bias_sum, shared = jnp.split(small, ends + [ends[-1] + narrow])
    shared = jnp.concatenate([value_bias_sum, shared]).reshape(rows + 2, channels)
    shared = jnp.stack(across(shared, swap(shared, "col", 1)), axis=1).reshape(-1)
    value_bias_sum, step_sum, pass_sum = jnp.split(shared, [VALUE, VALUE + row_channels])

    state = jnp.concatenate(state_deltas[1:], axis=1)
    late = jnp.concatenate([value_weight_delta.reshape(-1), state.reshape(-1)]).reshape(-1, local_channels)
    late_sum = PairSum(late, "dp")
    late_sum.add_pairs(late_sum.pairs())
    late_sum.add_mirrored(late_sum.mirrored())
    late = late_sum.join(late_sum.back()).astype(BF)
    late = jnp.stack(across(late, swap(late, "col", 1)))
    value_rows = value_weight_delta.shape[0]
    value_weight_delta = late[:, :value_rows].reshape(cols, -1, rows, channels)
    value_weight_delta = value_weight_delta.transpose(1, 2, 0, 3).reshape(-1, VALUE).astype(F32)
    state = late[:, value_rows:].reshape(row_channels, -1).astype(F32)
    modes = decay_rate.shape[1]
    return (
        block_output,
        input_delta,
        gain_sum,
        shift_sum,
        gate_weight_delta,
        gate_bias_sum,
        value_weight_delta,
        value_bias_sum,
        step_sum,
        state[:, :modes],
        state[:, modes : 2 * modes],
        state[:, 2 * modes :],
        pass_sum,
        expand_delta,
        output_weight_delta,
        bias_sum,
    )


def solution(mesh):
    placed = (
        P("dp", ("row", "col")),
        P(),
        P(),
        P("row", "col"),
        P(),
        P("row", None),
        P(),
        P("row"),
        P("row", None),
        P("row", None),
        P("row", None),
        P("row"),
        P("row", "col"),
        P("col", "row"),
        P(),
        P("dp", ("row", "col")),
    )
    return jax.shard_map(
        shards,
        mesh=mesh,
        in_specs=placed,
        out_specs=(
            P("dp", ("row", "col")),
            P("dp", ("row", "col")),
            P(("row", "col")),
            P(("row", "col")),
            P("row", "col"),
            P("col"),
            P("row", None),
            P(),
            P("row"),
            P("row", None),
            P("row", None),
            P("row", None),
            P("row"),
            P("row", "col"),
            P("col", "row"),
            P(("row", "col")),
        ),
        check_vma=False,
    )
```

```python
from functools import partial
import math

import jax
import jax.numpy as jnp
from jax import lax
from jax.experimental import pallas as pl
from jax.experimental.pallas import tpu as pltpu
from jax.sharding import PartitionSpec as P

D = 1024
FF = 3072
VALUE = 512
LEN = 2048
EPSILON = 1e-05
BL = 128
GROUP = 8
BF = jnp.bfloat16
F32 = jnp.float32


def dot(left, right, left_dim, right_dim):
    return lax.dot_general(
        left, right, (((left_dim,), (right_dim,)), ((), ())), preferred_element_type=F32
    )


def gelu(pre_act):
    return jax.nn.gelu(pre_act, approximate=True)


def gelu_back(pre_act, upstream):
    return jax.vjp(gelu, pre_act)[1](upstream)[0]


def mode_weights(log_step, decay_rate, frequency, readout):
    time_step = jnp.exp(log_step)[:, None]
    real_rate = -decay_rate * time_step
    imag_rate = frequency * time_step
    growth = jnp.exp(real_rate)
    shift_real = growth * jnp.cos(imag_rate) - 1.0
    shift_imag = growth * jnp.sin(imag_rate)
    modulus = decay_rate * decay_rate + frequency * frequency
    ratio_real = (shift_imag * frequency - shift_real * decay_rate) / modulus
    ratio_imag = (-shift_imag * decay_rate - shift_real * frequency) / modulus
    modes = decay_rate.shape[1]
    out_real = readout[:, :modes]
    out_imag = readout[:, modes:]
    mode_real = out_real * ratio_real - out_imag * ratio_imag
    mode_imag = out_real * ratio_imag + out_imag * ratio_real
    return (real_rate, imag_rate, mode_real, mode_imag)


def cmul(a, b):
    return a[0]*b[0]-a[1]*b[1], a[0]*b[1]+a[1]*b[0]

def squarings(z, n):
    out=[z]
    for _ in range(n):
        r,i=out[-1]
        out.append((r*r-i*i, 2.0*r*i))
    return out

def ladder(steps, rows, order, first=None):
    M = steps[0][0].shape[1]
    idx = lax.broadcasted_iota(jnp.int32, (8, M), 0)
    if order < 0: idx = 7-idx
    wr = jnp.ones((8,M), jnp.float32); wi = jnp.zeros((8,M), jnp.float32)
    for b in range(3):
        hit = (idx >> b) & 1
        nr, ni = cmul((wr,wi), steps[b])
        wr = jnp.where(hit==1, nr, wr); wi = jnp.where(hit==1, ni, wi)
    groups=[(wr,wi)]
    k=3
    while len(groups)*8 < rows:
        groups += [cmul(g, steps[k]) for g in groups]
        k+=1
    if order<0: groups = groups[::-1]
    return jnp.concatenate([g[0] for g in groups],0), jnp.concatenate([g[1] for g in groups],0)

def row(p, i):
    return p[0][i:i+1], p[1][i:i+1]

def two_terms(x):
    high = x.astype(BF)
    return high, (x - high.astype(F32)).astype(BF)


def gen_kernel(nb, zr, zi, cr, ci, *refs):
    k_out, kr_out = refs[-2:]
    steps = squarings((zr[...], zi[...]), 6 + int(math.log2(nb)))
    rev = (lax.broadcasted_iota(jnp.int32,(BL,BL),0)+lax.broadcasted_iota(jnp.int32,(BL,BL),1)==BL-1).astype(F32).astype(BF)
    nt = (((1,),(1,)),((),()))
    for i in range(GROUP):
        st = [row(x,i) for x in steps]
        near = ladder(st[:7], BL, 1)
        far = ladder(st[7:], nb, 1)
        lead = cmul((cr[i:i+1,:], ci[i:i+1,:]), far)
        lh, ll = two_terms(jnp.concatenate([lead[0], -lead[1]],1))
        nh, nl = two_terms(jnp.concatenate(near,1))
        first = lax.dot_general(jnp.concatenate([lh, ll]), nh, nt, preferred_element_type=F32)
        k = first[:nb] + (first[nb:] + lax.dot_general(lh, nl, nt, preferred_element_type=F32))
        kb = k.astype(BF)
        k_out[i] = kb
        kr_out[i] = jnp.dot(kb, rev, preferred_element_type=F32).astype(BF)


def cost(microseconds):
    return pl.CostEstimate(flops=int(microseconds * 1e9), bytes_accessed=1 << 20, transcendentals=0)


def generate(modes, length, part, parts, earlier=()):
    C, M = modes[0].shape
    nb = length//BL
    steps = C//GROUP//parts
    spec = pl.BlockSpec((GROUP, M), lambda i:(i + part*steps,0))
    ospec = pl.BlockSpec((GROUP, nb, BL), lambda i:(i + part*steps,0,0))
    sh = jax.ShapeDtypeStruct((C,nb,BL), BF)
    return pl.pallas_call(partial(gen_kernel, nb), grid=(steps,), in_specs=[spec]*4 + [pl.BlockSpec(memory_space=pl.ANY)]*len(earlier), out_specs=[ospec]*2,
        out_shape=[sh,sh], cost_estimate=cost(18/parts), input_output_aliases={4+k:k for k in range(len(earlier))})(*modes, *earlier)


def toeplitz_blocks(load, count, shift):
    r = lax.broadcasted_iota(jnp.int32,(BL,BL),0); c = lax.broadcasted_iota(jnp.int32,(BL,BL),1)
    mask = c >= r + shift
    def rot(j):
        x = load(j)
        if x is None: return jnp.zeros((BL,BL), jnp.float32)
        return pltpu.roll(jnp.broadcast_to(x,(BL,BL)), shift, 1, stride=1, stride_axis=0)
    out=[]
    cur = rot(0)
    for j in range(count):
        nxt = rot(j+1)
        out.append(jnp.where(mask, nxt, cur).astype(jnp.bfloat16))
        cur = nxt
    return jnp.concatenate(out,0)

def shifted(pad_ref, nb, d):
    return pad_ref[pl.ds(nb-d, nb), :]

def fwd_kernel(nb, tb, me_ref, v_ref, kr_ref, p_ref, out_ref, pad):
    per = tb//BL
    me = me_ref[0]
    pad[0:nb,:] = jnp.zeros((nb,BL), jnp.float32)
    for i in range(GROUP):
        def load(j):
            if j==0: return None
            j-=1
            return v_ref[me ^ (j//per), i:i+1, (j%per)*BL:(j%per+1)*BL].astype(jnp.float32)
        H = toeplitz_blocks(load, nb, 0)
        pad[nb:2*nb,:] = kr_ref[i].astype(jnp.float32)
        X = jnp.concatenate([shifted(pad,nb,d) for d in range(nb)],1).astype(jnp.bfloat16)
        out = jnp.dot(X, H, preferred_element_type=jnp.float32)
        for j in range(nb):
            sl = (me ^ (j//per), slice(i,i+1), slice((j%per)*BL,(j%per+1)*BL))
            out_ref[sl] = (out[j:j+1,:] + p_ref[i:i+1,:]*v_ref[sl].astype(jnp.float32)).astype(out_ref.dtype)

def forward(me, v, kr, passthrough, out_dtype=jnp.float32):
    R,C,tb = v.shape
    nb = R*tb//BL
    spec = pl.BlockSpec((R,GROUP,tb), lambda i,_:(0,i,0))
    kspec = pl.BlockSpec((GROUP,nb,BL), lambda i,_:(i,0,0))
    pspec = pl.BlockSpec((GROUP,1), lambda i,_:(i,0))
    grid_spec = pltpu.PrefetchScalarGridSpec(num_scalar_prefetch=1, grid=(C//GROUP,), in_specs=[spec,kspec,pspec], out_specs=spec,
        scratch_shapes=[pltpu.VMEM((2*nb,BL),jnp.float32)])
    return pl.pallas_call(partial(fwd_kernel,nb,tb), grid_spec=grid_spec,
        out_shape=jax.ShapeDtypeStruct(v.shape,out_dtype), cost_estimate=cost(13))(me,v,kr,passthrough[:,None])

def bwd_kernel(prec, nb, tb, me_ref, v_ref, m_ref, k_ref, p_ref, zr, zi, *refs):
    vb_ref, s_ref, pad, pad2 = refs[-4:]
    per = tb//BL
    pad[0:nb,:] = jnp.zeros((nb,BL), jnp.float32)
    pad2[0:nb,:] = jnp.zeros((nb,BL), jnp.float32)
    me = me_ref[0]
    steps = squarings((zr[...], zi[...]), 6 + int(math.log2(nb)))
    rev = (lax.broadcasted_iota(jnp.int32,(BL,BL),0)+lax.broadcasted_iota(jnp.int32,(BL,BL),1)==BL-1).astype(jnp.float32).astype(jnp.bfloat16)
    lane = lax.broadcasted_iota(jnp.int32,(nb,BL),1).astype(jnp.float32)
    M = zr.shape[1]
    arow = (nb-1-lax.broadcasted_iota(jnp.int32,(nb,M),0)).astype(jnp.float32)*BL
    for i in range(GROUP):
        def at(j): return (me ^ (j//per), slice(i,i+1), slice((j%per)*BL,(j%per+1)*BL))
        def load(j):
            if j==nb: return None
            return m_ref[at(j)].astype(jnp.float32)
        H = toeplitz_blocks(load, nb, 1)
        pad[nb:2*nb,:] = k_ref[i].astype(jnp.float32)
        for j in range(nb):
            pad2[nb+j:nb+j+1,:] = v_ref[at(j)].astype(jnp.float32)
        pad2[nb:2*nb,:] = jnp.dot(pad2[nb:2*nb,:].astype(jnp.bfloat16), rev, preferred_element_type=jnp.float32)
        X = jnp.concatenate([jnp.concatenate([shifted(pad,nb,nb-1-e) for e in range(nb)],1), jnp.concatenate([shifted(pad2,nb,nb-1-e) for e in range(nb)],1)],0).astype(jnp.bfloat16)
        out = jnp.dot(X, H, preferred_element_type=jnp.float32)
        for j in range(nb):
            vb_ref[at(j)] = (out[nb-1-j:nb-j,:] + p_ref[i:i+1,:]*m_ref[at(j)].astype(jnp.float32)).astype(vb_ref.dtype)
        kb = out[nb:,:]
        st = [row(s,i) for s in steps]
        near = ladder(st[:7], BL, 1)
        far = ladder(st[7:], nb, -1)
        U = jnp.dot(jnp.concatenate([kb, kb*lane],0), jnp.concatenate(near,1), precision=prec, preferred_element_type=jnp.float32)
        u = U[:nb,:M], U[:nb,M:]
        w = U[nb:,:M]+arow*u[0], U[nb:,M:]+arow*u[1]
        s1 = cmul(u, far); s2 = cmul(w, far)
        for n,x in enumerate((*s1,*s2)):
            s_ref[n, i:i+1, :] = jnp.sum(x,0,keepdims=True)

def backward(me, v, mb, k, passthrough, zr, zi, part, parts, earlier=(), prec=lax.Precision.DEFAULT):
    R,C,tb = v.shape
    M = zr.shape[1]
    nb = R*tb//BL
    steps = C//GROUP//parts
    spec = pl.BlockSpec((R,GROUP,tb), lambda i,_:(0,i + part*steps,0))
    kspec = pl.BlockSpec((GROUP,nb,BL), lambda i,_:(i + part*steps,0,0))
    pspec = pl.BlockSpec((GROUP,1), lambda i,_:(i + part*steps,0))
    zspec = pl.BlockSpec((GROUP,M), lambda i,_:(i + part*steps,0))
    grid_spec = pltpu.PrefetchScalarGridSpec(num_scalar_prefetch=1, grid=(steps,),
        in_specs=[spec,spec,kspec,pspec,zspec,zspec] + [pl.BlockSpec(memory_space=pl.ANY)]*len(earlier),
        out_specs=[spec, pl.BlockSpec((4,GROUP,M), lambda i,_:(0,i + part*steps,0))], scratch_shapes=[pltpu.VMEM((2*nb,BL),jnp.float32)]*2)
    return pl.pallas_call(partial(bwd_kernel,prec,nb,tb), grid_spec=grid_spec,
        out_shape=[jax.ShapeDtypeStruct(v.shape,BF), jax.ShapeDtypeStruct((4,C,M),jnp.float32)],
        cost_estimate=cost(26/parts), input_output_aliases={7+n:n for n in range(len(earlier))})(me,v,mb,k,passthrough[:,None],zr,zi,*earlier)


def gate_kernel(pieces, acts_ref, up_ref, bias_ref, *refs):
    gates, outs, (act_ref, slope_ref, back_ref) = refs[:pieces], refs[pieces : 2 * pieces], refs[2 * pieces :]
    width = gates[0].shape[0]
    gate_pre = bias_ref[...]
    product_back = 0.0
    for k in range(pieces):
        lanes = slice(k * width, (k + 1) * width)
        gate_pre = gate_pre + jnp.dot(acts_ref[:, lanes], gates[k][...], preferred_element_type=F32)
        product_back = product_back + dot(up_ref[:, lanes], outs[k][...], 1, 1)
    square = gate_pre * gate_pre
    bend = jnp.tanh(0.7978845608 * gate_pre * (1.0 + 0.044715 * square))
    gate_act = 0.5 * gate_pre * (1.0 + bend)
    slope = 0.5 * (1.0 + bend) + 0.5 * gate_pre * (1.0 - bend * bend) * (0.7978845608 * (1.0 + 0.134145 * square))
    act_ref[...] = gate_act
    slope_ref[...] = slope * product_back
    back_ref[...] = (product_back * gate_act).astype(BF)


def gate_stage(acts, upstream, bias, gates, outs):
    block, width = acts.shape[0], bias.shape[0]
    tile = 256
    whole = pl.BlockSpec(acts.shape, lambda i: (0, 0))
    ospec = pl.BlockSpec((block, tile), lambda i: (0, i))
    return pl.pallas_call(
        partial(gate_kernel, len(gates)),
        grid=(width // tile,),
        in_specs=[whole, whole, pl.BlockSpec((1, tile), lambda i: (0, i))]
        + [pl.BlockSpec((gate.shape[0], tile), lambda i: (0, i)) for gate in gates]
        + [pl.BlockSpec((tile, out.shape[1]), lambda i: (i, 0)) for out in outs],
        out_specs=[ospec] * 3,
        out_shape=[jax.ShapeDtypeStruct((block, width), kind) for kind in (F32, F32, BF)],
        cost_estimate=cost(8),
    )(acts, upstream, bias.reshape(1, -1), *gates, *outs)


def bits(axis):
    size = lax.axis_size(axis)
    return [1 << k for k in range(size.bit_length() - 1)]


def swap(array, axis, mask):
    return lax.ppermute(array, axis, [(i, i ^ mask) for i in range(lax.axis_size(axis))])


def exchange_blocks(blocks, axis):
    return [blocks[0]] + [swap(blocks[q], axis, q) for q in range(1, len(blocks))]


def fence(*values):
    return lax.optimization_barrier(values)


def halve(array, dim):
    return jnp.split(array, 2, dim)


class PairSum:
    def __init__(self, array, axis):
        self.axis = axis
        index = lax.axis_index(axis)
        self.half = (index ^ (index >> 1)) & 1
        length = array.shape[0] // 2
        self.kept = lax.dynamic_slice_in_dim(array, self.half * length, length)
        self.sent = lax.dynamic_slice_in_dim(array, (1 - self.half) * length, length).astype(BF)

    def pairs(self):
        return swap(self.sent, self.axis, 1)

    def add_pairs(self, got):
        self.total = (self.kept.astype(F32) + got.astype(F32)).astype(BF)

    def mirrored(self):
        for bit in bits(self.axis)[2:]:
            self.total = (self.total.astype(F32) + swap(self.total, self.axis, bit).astype(F32)).astype(BF)
        return swap(self.total, self.axis, 3) if lax.axis_size(self.axis) > 2 else None

    def add_mirrored(self, got):
        if got is not None:
            self.total = (self.total.astype(F32) + got.astype(F32)).astype(BF)

    def back(self):
        return swap(self.total, self.axis, 1)

    def join(self, got):
        first = jnp.where(self.half == 0, self.total, got)
        second = jnp.where(self.half == 0, got, self.total)
        return jnp.concatenate([first, second]).astype(F32)


def small_sum(array, axis):
    left = bits(axis)
    while left:
        one, left = left[0], left[1:]
        if left:
            two, left = left[0], left[1:]
            array = (array + swap(array, axis, one)) + (swap(array, axis, two) + swap(array, axis, one | two))
        else:
            array = array + swap(array, axis, one)
    return array


def shards(
    inputs,
    norm_gain,
    norm_shift,
    gate_weight,
    gate_bias,
    value_weight,
    value_bias,
    log_step,
    decay_rate,
    frequency,
    readout,
    passthrough,
    expand_weight,
    output_weight,
    output_bias,
    cotangent,
):
    rows = lax.axis_size("row")
    cols = lax.axis_size("col")
    row_index = lax.axis_index("row")
    col_index = lax.axis_index("col")
    tokens, narrow = inputs.shape
    block = tokens // rows
    half_ff = FF // cols
    row_channels = VALUE // rows
    channels = row_channels // cols
    local_channels = rows * channels

    def own_channels(array):
        return lax.dynamic_slice_in_dim(array, col_index * channels, channels, 0)

    state_params = tuple(own_channels(a) for a in (log_step, decay_rate, frequency, readout))
    own_pass = own_channels(passthrough)
    weights, weights_pullback = jax.vjp(mode_weights, *state_params)
    real_rate, imag_rate, mode_real, mode_imag = weights
    growth = jnp.exp(real_rate)
    z_real, z_imag = growth * jnp.cos(imag_rate), growth * jnp.sin(imag_rate)
    me = row_index.astype(jnp.int32).reshape(1)
    every = range(rows)
    order = [0]
    for bit in reversed(bits("row")):
        order = order + [q | bit for q in order]

    def across(own, other):
        return [jnp.where(col_index == 0, own, other), jnp.where(col_index == 0, other, own)]

    def at_xor(array, q, dim=0):
        return lax.dynamic_index_in_dim(array, row_index ^ q, dim, False)

    def natural(blocks):
        stacked = jnp.stack(blocks)
        return jnp.stack([at_xor(stacked, q) for q in every])

    def features(own, other):
        first, second = across(own, other)
        return jnp.concatenate([part[k] for k in every for part in (first, second)], axis=1)

    def own_features(array, flip=0):
        return jnp.concatenate(
            [
                lax.dynamic_slice_in_dim(array, (k * cols + (col_index ^ flip)) * narrow, narrow, array.ndim - 1)
                for k in every
            ],
            axis=-1,
        )

    def by_order(blocks):
        return [blocks[q] for q in order]

    def ordered_features(vectors):
        blocks = vectors.reshape(vectors.shape[0], rows, -1)
        return jnp.concatenate([at_xor(blocks, q, 1) for q in order], axis=1)

    modes_in = (z_real, z_imag, mode_real, mode_imag)
    value_half = lax.dynamic_index_in_dim(
        value_weight.reshape(-1, rows, cols, channels), col_index, 2, False
    ).reshape(-1, local_channels)
    value_bias_half = lax.dynamic_index_in_dim(
        value_bias.reshape(rows, cols, channels), col_index, 1, False
    ).reshape(local_channels, 1)
    gate_bias_half = lax.dynamic_slice_in_dim(gate_bias, col_index * half_ff, half_ff)
    gain, shift, bias = ordered_features(jnp.stack([norm_gain, norm_shift, output_bias]))

    x_parts = exchange_blocks([at_xor(inputs.reshape(rows, block, narrow), q) for q in every], "row")
    value_2 = swap(value_half, "row", 2)
    value_1 = swap(value_half, "row", 1)
    x_parts, value_2, modes_in, upstream_blocks, gate_0 = fence(
        x_parts, value_2, modes_in, cotangent.reshape(rows, block, narrow), gate_weight
    )
    x_own = jnp.stack(by_order(x_parts))
    x_other = swap(x_own, "col", 1)
    g_parts = exchange_blocks([at_xor(upstream_blocks, q) for q in every], "row")
    gate_2 = swap(gate_0, "row", 2)
    kernels = generate(modes_in, tokens, 0, 2)
    kernels, value_2 = fence(kernels, value_2)
    value_3 = swap(value_2, "row", 1)
    x_other, g_parts, value_1, value_3, kernels, output_0 = fence(
        x_other, g_parts, value_1, value_3, kernels, output_weight
    )
    value_half = jnp.concatenate([value_half, value_2, value_1, value_3])
    x_full = features(x_own, x_other)
    g_own = jnp.stack(by_order(g_parts))
    g_other = swap(g_own, "col", 1)

    source = x_full.astype(F32)
    row_mean = jnp.mean(source, axis=-1, keepdims=True)
    centered = source - row_mean
    variance = jnp.mean(centered * centered, axis=-1, keepdims=True)
    rescale = lax.rsqrt(variance + EPSILON)
    normed = centered * rescale
    acts = (normed * gain + shift).astype(BF)

    value_pre = dot(value_half, acts, 0, 1) + value_bias_half
    values = gelu(value_pre).astype(BF).reshape(rows, channels, block)
    values_sent = [at_xor(values, q) for q in every]
    values_sent, modes_in, kernels = fence(values_sent, modes_in, kernels)
    values = exchange_blocks(values_sent, "row")
    kernels = generate(modes_in, tokens, 1, 2, kernels)
    output_2 = swap(output_0, "row", 2)
    values, kernels, g_other, gate_2, expand_0 = fence(values, kernels, g_other, gate_2, expand_weight)
    kernel, kernel_flipped = kernels
    values = jnp.stack(values)
    gate_1 = swap(gate_0, "row", 1)
    gate_3 = swap(gate_2, "row", 1)
    expand_2 = swap(expand_0, "row", 2)
    mixed = forward(me, values, kernel, own_pass, BF)
    mixed, gate_1, gate_3, output_0, expand_0 = fence(mixed, gate_1, gate_3, output_0, expand_0)
    mixed = exchange_blocks([mixed[q] for q in every], "row")
    output_1 = swap(output_0, "row", 1)
    mixed, output_2, output_1, g_own = fence(mixed, output_2, output_1, g_own)
    output_3 = swap(output_2, "row", 1)
    upstream = features(g_own, g_other)
    mixed = jnp.stack(by_order(mixed))
    mixed_other = swap(mixed, "col", 1)
    expand_1 = swap(expand_0, "row", 1)
    output_3, acts, mixed = fence(output_3, acts, mixed)
    gates = (gate_0, gate_2, gate_1, gate_3)
    outputs = (output_0, output_2, output_1, output_3)
    gate_act, gate_slope, expand_back = gate_stage(acts, upstream, gate_bias_half, gates, outputs)
    gate_act, gate_slope, expand_back, mixed_other, expand_1, expand_2 = fence(
        gate_act, gate_slope, expand_back, mixed_other, expand_1, expand_2
    )
    expand_3 = swap(expand_2, "row", 1)
    mixed = jnp.stack(across(mixed, mixed_other), axis=1).reshape(VALUE, block)
    expand_full = jnp.concatenate([expand_0, expand_2, expand_1, expand_3])
    mixed_back = dot(expand_full, expand_back, 1, 1).reshape(rows, cols, channels, block)
    sent = lax.dynamic_index_in_dim(mixed_back, 1 - col_index, 1, False).astype(BF)
    mixed_back = lax.dynamic_index_in_dim(mixed_back, col_index, 1, False)
    sent, mixed, expand_full = fence(sent, mixed, expand_full)
    got = swap(sent, "col", 1)

    expand_kept, expand_sent = [dot(piece, expand_back, 1, 0).astype(BF) for piece in halve(mixed, 0)]
    expand_got = swap(expand_sent, "row", 1)
    expanded = dot(mixed, expand_full, 0, 0)
    product = (gate_act * expanded).astype(BF)
    gate_back = (gate_slope * expanded).astype(BF)
    gate_bias_delta = jnp.sum(gate_back, axis=0, dtype=F32)
    product, gate_back, got = fence(product, gate_back, got)
    mixed_back = (mixed_back + got.astype(F32)).astype(BF)
    mixed_back, upstream, acts = fence(mixed_back, upstream, acts)
    mixed_back = exchange_blocks(by_order(mixed_back), "row")
    output_kept, output_sent = [dot(product, piece, 0, 0).astype(BF) for piece in halve(upstream, 1)]
    output_got = swap(output_sent, "row", 1)
    gate_kept, gate_sent = [dot(piece, gate_back, 0, 0).astype(BF) for piece in halve(acts, 1)]
    mixed_back, expand_got, output_got, gate_sent = fence(mixed_back, expand_got, output_got, gate_sent)

    def second(kept, got, dim):
        total = kept.astype(F32) + got.astype(F32)
        return halve(total.astype(BF), dim)

    gate_got = swap(gate_sent, "row", 1)
    mixed_back = jnp.stack(mixed_back)
    expand_kept, expand_sent = second(expand_kept, expand_got, 0)
    output_kept, output_sent = second(output_kept, output_got, 1)
    mixed_back, expand_sent, output_sent = fence(mixed_back, expand_sent, output_sent)
    expand_got = swap(expand_sent, "row", 2)
    output_got = swap(output_sent, "row", 2)
    state_args = (me, values, mixed_back, kernel_flipped, own_pass, z_real, z_imag)
    back = backward(*state_args, 0, 2)
    back, expand_got, gate_got = fence(back, expand_got, gate_got)
    expand_sum = PairSum(expand_kept.astype(F32) + expand_got.astype(F32), "dp")
    gate_kept, gate_sent = second(gate_kept, gate_got, 0)
    back, expand_sum.sent, gate_sent = fence(back, expand_sum.sent, gate_sent)
    expand_got = expand_sum.pairs()
    gate_got = swap(gate_sent, "row", 2)
    back = backward(*state_args, 1, 2, back)
    back, expand_got, output_got = fence(back, expand_got, output_got)
    values_back, sums = back
    gate_full, output_full = jnp.concatenate(gates), jnp.concatenate(outputs, axis=1)
    values_back = exchange_blocks([values_back[q] for q in every], "row")
    expand_sum.add_pairs(expand_got)
    output_sum = PairSum(output_kept.astype(F32) + output_got.astype(F32), "dp")
    output_sum.sent, expand_sum.total = fence(output_sum.sent, expand_sum.total)
    expand_got = expand_sum.mirrored()
    output_got = output_sum.pairs()
    values_back, expand_got, output_got = fence(values_back, expand_got, output_got)
    expand_sum.add_mirrored(expand_got)
    output_sum.add_pairs(output_got)
    expand_got = expand_sum.back()
    output_got = output_sum.mirrored()

    def to_tokens(array):
        blocks = by_order(jnp.split(array, rows, 1))
        return natural(exchange_blocks(blocks, "row")).reshape(tokens, narrow)

    values_back = natural(values_back).reshape(local_channels, block)
    value_back = gelu_back(value_pre, values_back.astype(F32)).astype(BF)
    value_kept, value_sent = [dot(piece, value_back, 0, 1).astype(BF) for piece in halve(acts, 1)]
    value_kept, value_sent = second(value_kept, swap(value_sent, "row", 1), 0)
    value_weight_delta = value_kept.astype(F32) + swap(value_sent, "row", 2).astype(F32)
    value_bias_delta = jnp.sum(value_back, axis=1, dtype=F32)
    passthrough_delta = jnp.sum(mixed_back.astype(F32) * values.astype(F32), axis=(0, 2))
    first_real, first_imag, second_real, second_imag = sums
    state_deltas = weights_pullback(
        (
            mode_real * second_real - mode_imag * second_imag,
            -mode_real * second_imag - mode_imag * second_real,
            first_real,
            -first_imag,
        )
    )

    acts_back = dot(gate_back, gate_full, 1, 1) + dot(value_back, value_half, 0, 1)
    weighted = acts_back * gain
    moments = jnp.stack([jnp.sum(weighted, axis=1), jnp.sum(weighted * normed, axis=1)])
    acts_sent = own_features(acts_back, 1).astype(BF)
    acts_got = swap(acts_sent, "col", 1)
    moments = small_sum(moments, "col") / D
    acts_got, moments, gate_got, expand_got = fence(acts_got, moments, gate_got, expand_got)
    expand_delta = expand_sum.join(expand_got)
    gate_sum = PairSum(gate_kept.astype(F32) + gate_got.astype(F32), "dp")
    gate_got = gate_sum.pairs()

    acts_back = own_features(acts_back) + acts_got.astype(F32)
    own_normed = own_features(normed)
    gain_delta = jnp.sum(acts_back * own_normed, axis=0)
    shift_delta = jnp.sum(acts_back, axis=0)
    input_delta = rescale * (acts_back * own_features(gain) - moments[0][:, None] - own_normed * moments[1][:, None])
    input_delta = cotangent.astype(F32) + to_tokens(input_delta.astype(BF)).astype(F32)
    input_delta, output_got, gate_got, product = fence(input_delta, output_got, gate_got, product)
    output_sum.add_mirrored(output_got)
    gate_sum.add_pairs(gate_got)
    output_got = output_sum.back()
    gate_got = gate_sum.mirrored()
    out_sum = dot(product, output_full, 1, 0)
    out_sum = own_features(out_sum) + swap(own_features(out_sum, 1).astype(BF), "col", 1).astype(F32)
    block_output = to_tokens((own_features(source) + out_sum + own_features(bias)).astype(BF))
    output_weight_delta = output_sum.join(output_got)
    gate_sum.add_mirrored(gate_got)
    gate_weight_delta = gate_sum.join(gate_sum.back())

    biases = jnp.concatenate([gate_bias_delta, value_bias_delta])
    norms = jnp.stack([gain_delta, shift_delta]).reshape(2, rows, narrow)
    small = exchange_blocks(
        [jnp.concatenate([norms[:, k].reshape(-1), biases]) for k in (order.index(q) for q in every)], "row"
    )
    while len(small) > 1:
        small = [a + b for a, b in zip(small[::2], small[1::2])]
    small = jnp.concatenate(
        [small[0], jnp.sum(cotangent, axis=0, dtype=F32), state_deltas[0], passthrough_delta]
    )
    small = small_sum(small, "dp")
    ends = [narrow, 2 * narrow, 2 * narrow + half_ff, 2 * narrow + half_ff + local_channels]
    gain_sum, shift_sum, gate_bias_sum, value_bias_sum, bias_sum, shared = jnp.split(small, ends + [ends[-1] + narrow])
    shared = jnp.concatenate([value_bias_sum, shared]).reshape(rows + 2, channels)
    shared = jnp.stack(across(shared, swap(shared, "col", 1)), axis=1).reshape(-1)
    value_bias_sum, step_sum, pass_sum = jnp.split(shared, [VALUE, VALUE + row_channels])

    state = jnp.concatenate(state_deltas[1:], axis=1)
    late = jnp.concatenate([value_weight_delta.reshape(-1), state.reshape(-1)]).reshape(-1, local_channels)
    late_sum = PairSum(late, "dp")
    late_sum.add_pairs(late_sum.pairs())
    late_sum.add_mirrored(late_sum.mirrored())
    late = late_sum.join(late_sum.back()).astype(BF)
    late = jnp.stack(across(late, swap(late, "col", 1)))
    value_rows = value_weight_delta.shape[0]
    value_weight_delta = late[:, :value_rows].reshape(cols, -1, rows, channels)
    value_weight_delta = value_weight_delta.transpose(1, 2, 0, 3).reshape(-1, VALUE).astype(F32)
    state = late[:, value_rows:].reshape(row_channels, -1).astype(F32)
    modes = decay_rate.shape[1]
    return (
        block_output,
        input_delta,
        gain_sum,
        shift_sum,
        gate_weight_delta,
        gate_bias_sum,
        value_weight_delta,
        value_bias_sum,
        step_sum,
        state[:, :modes],
        state[:, modes : 2 * modes],
        state[:, 2 * modes :],
        pass_sum,
        expand_delta,
        output_weight_delta,
        bias_sum,
    )


def solution(mesh):
    placed = (
        P("dp", ("row", "col")),
        P(),
        P(),
        P("row", "col"),
        P(),
        P("row", None),
        P(),
        P("row"),
        P("row", None),
        P("row", None),
        P("row", None),
        P("row"),
        P("row", "col"),
        P("col", "row"),
        P(),
        P("dp", ("row", "col")),
    )
    return jax.shard_map(
        shards,
        mesh=mesh,
        in_specs=placed,
        out_specs=(
            P("dp", ("row", "col")),
            P("dp", ("row", "col")),
            P(("row", "col")),
            P(("row", "col")),
            P("row", "col"),
            P("col"),
            P("row", None),
            P(),
            P("row"),
            P("row", None),
            P("row", None),
            P("row", None),
            P("row"),
            P("row", "col"),
            P("col", "row"),
            P(("row", "col")),
        ),
        check_vma=False,
    )
```

```python
from functools import partial
import math

import jax
import jax.numpy as jnp
from jax import lax
from jax.experimental import pallas as pl
from jax.experimental.pallas import tpu as pltpu
from jax.sharding import PartitionSpec as P

D = 1024
FF = 3072
VALUE = 512
LEN = 2048
EPSILON = 1e-05
BL = 128
GROUP = 8
BF = jnp.bfloat16
F32 = jnp.float32


def dot(left, right, left_dim, right_dim):
    return lax.dot_general(
        left, right, (((left_dim,), (right_dim,)), ((), ())), preferred_element_type=F32
    )


def gelu(pre_act):
    return jax.nn.gelu(pre_act, approximate=True)


def gelu_back(pre_act, upstream):
    return jax.vjp(gelu, pre_act)[1](upstream)[0]


def mode_weights(log_step, decay_rate, frequency, readout):
    time_step = jnp.exp(log_step)[:, None]
    real_rate = -decay_rate * time_step
    imag_rate = frequency * time_step
    growth = jnp.exp(real_rate)
    shift_real = growth * jnp.cos(imag_rate) - 1.0
    shift_imag = growth * jnp.sin(imag_rate)
    modulus = decay_rate * decay_rate + frequency * frequency
    ratio_real = (shift_imag * frequency - shift_real * decay_rate) / modulus
    ratio_imag = (-shift_imag * decay_rate - shift_real * frequency) / modulus
    modes = decay_rate.shape[1]
    out_real = readout[:, :modes]
    out_imag = readout[:, modes:]
    mode_real = out_real * ratio_real - out_imag * ratio_imag
    mode_imag = out_real * ratio_imag + out_imag * ratio_real
    return (real_rate, imag_rate, mode_real, mode_imag)


def cmul(a, b):
    return a[0]*b[0]-a[1]*b[1], a[0]*b[1]+a[1]*b[0]

def squarings(z, n):
    out=[z]
    for _ in range(n):
        r,i=out[-1]
        out.append((r*r-i*i, 2.0*r*i))
    return out

def ladder(steps, rows, order, first=None):
    M = steps[0][0].shape[1]
    idx = lax.broadcasted_iota(jnp.int32, (8, M), 0)
    if order < 0: idx = 7-idx
    wr = jnp.ones((8,M), jnp.float32); wi = jnp.zeros((8,M), jnp.float32)
    for b in range(3):
        hit = (idx >> b) & 1
        nr, ni = cmul((wr,wi), steps[b])
        wr = jnp.where(hit==1, nr, wr); wi = jnp.where(hit==1, ni, wi)
    groups=[(wr,wi)]
    k=3
    while len(groups)*8 < rows:
        groups += [cmul(g, steps[k]) for g in groups]
        k+=1
    if order<0: groups = groups[::-1]
    return jnp.concatenate([g[0] for g in groups],0), jnp.concatenate([g[1] for g in groups],0)

def row(p, i):
    return p[0][i:i+1], p[1][i:i+1]

def two_terms(x):
    high = x.astype(BF)
    return high, (x - high.astype(F32)).astype(BF)


def gen_kernel(nb, zr, zi, cr, ci, *refs):
    k_out, kr_out = refs[-2:]
    steps = squarings((zr[...], zi[...]), 6 + int(math.log2(nb)))
    rev = (lax.broadcasted_iota(jnp.int32,(BL,BL),0)+lax.broadcasted_iota(jnp.int32,(BL,BL),1)==BL-1).astype(F32).astype(BF)
    nt = (((1,),(1,)),((),()))
    for i in range(GROUP):
        st = [row(x,i) for x in steps]
        near = ladder(st[:7], BL, 1)
        far = ladder(st[7:], nb, 1)
        lead = cmul((cr[i:i+1,:], ci[i:i+1,:]), far)
        lh, ll = two_terms(jnp.concatenate([lead[0], -lead[1]],1))
        nh, nl = two_terms(jnp.concatenate(near,1))
        first = lax.dot_general(jnp.concatenate([lh, ll]), nh, nt, preferred_element_type=F32)
        k = first[:nb] + (first[nb:] + lax.dot_general(lh, nl, nt, preferred_element_type=F32))
        kb = k.astype(BF)
        k_out[i] = kb
    kr_out[...] = jnp.dot(k_out[...].reshape(GROUP*nb, BL), rev, preferred_element_type=F32).astype(BF).reshape(GROUP, nb, BL)


def cost(microseconds):
    return pl.CostEstimate(flops=int(microseconds * 1e9), bytes_accessed=1 << 20, transcendentals=0)


def generate(modes, length, part, parts, earlier=()):
    C, M = modes[0].shape
    nb = length//BL
    steps = C//GROUP//parts
    spec = pl.BlockSpec((GROUP, M), lambda i:(i + part*steps,0))
    ospec = pl.BlockSpec((GROUP, nb, BL), lambda i:(i + part*steps,0,0))
    sh = jax.ShapeDtypeStruct((C,nb,BL), BF)
    return pl.pallas_call(partial(gen_kernel, nb), grid=(steps,), in_specs=[spec]*4 + [pl.BlockSpec(memory_space=pl.ANY)]*len(earlier), out_specs=[ospec]*2,
        out_shape=[sh,sh], cost_estimate=cost(10/parts), input_output_aliases={4+k:k for k in range(len(earlier))})(*modes, *earlier)


def toeplitz_blocks(load, count, shift):
    r = lax.broadcasted_iota(jnp.int32,(BL,BL),0); c = lax.broadcasted_iota(jnp.int32,(BL,BL),1)
    mask = c >= r + shift
    def rot(j):
        x = load(j)
        if x is None: return jnp.zeros((BL,BL), BF)
        base = pltpu.roll(jnp.broadcast_to(x,(64,BL)), shift, 1, stride=1, stride_axis=0).astype(BF)
        return jnp.concatenate([base] + [pltpu.roll(base, 64, 1)], 0)
    out=[]
    cur = rot(0)
    for j in range(count):
        nxt = rot(j+1)
        out.append(jnp.where(mask, nxt, cur))
        cur = nxt
    return jnp.concatenate(out,0)


def toeplitz_old(load, count, shift):
    r = lax.broadcasted_iota(jnp.int32,(BL,BL),0); c = lax.broadcasted_iota(jnp.int32,(BL,BL),1)
    mask = c >= r + shift
    def rot(j):
        x = load(j)
        if x is None: return jnp.zeros((BL,BL), jnp.float32)
        return pltpu.roll(jnp.broadcast_to(x,(BL,BL)), shift, 1, stride=1, stride_axis=0)
    out=[]
    cur = rot(0)
    for j in range(count):
        nxt = rot(j+1)
        out.append(jnp.where(mask, nxt, cur).astype(jnp.bfloat16))
        cur = nxt
    return jnp.concatenate(out,0)


def spread(dst, src, me, per):
    for j in range(dst.shape[0]//GROUP):
        dst[j*GROUP:(j+1)*GROUP,:] = src[me ^ (j//per), :, (j%per)*BL:(j%per+1)*BL].astype(F32)


def gather_out(dst, src, extra, scale, me, per):
    for j in range(src.shape[0]//GROUP):
        rows = slice(j*GROUP,(j+1)*GROUP)
        dst[me ^ (j//per), :, (j%per)*BL:(j%per+1)*BL] = (src[rows,:] + scale*extra[rows,:]).astype(dst.dtype)


def shifted(pad_ref, nb, d):
    return pad_ref[pl.ds(nb-d, nb), :]


def fwd_kernel(nb, tb, me_ref, v_ref, kr_ref, p_ref, out_ref, pad, vf, of):
    per = tb//BL
    me = me_ref[0]
    pad[0:nb,:] = jnp.zeros((nb,BL), F32)
    spread(vf, v_ref, me, per)
    for i in range(GROUP):
        def load(j):
            return vf[(j-1)*GROUP+i:(j-1)*GROUP+i+1,:] if j else None
        H = toeplitz_old(load, nb, 0)
        pad[nb:2*nb,:] = kr_ref[i].astype(F32)
        X = jnp.concatenate([shifted(pad,nb,d) for d in range(nb)],1).astype(BF)
        of[pl.ds(i, nb, stride=GROUP),:] = jnp.dot(X, H, preferred_element_type=F32)
    gather_out(out_ref, of, vf, p_ref[...], me, per)


def forward(me, v, kr, passthrough, out_dtype=jnp.float32):
    R,C,tb = v.shape
    nb = R*tb//BL
    spec = pl.BlockSpec((R,GROUP,tb), lambda i,_:(0,i,0))
    kspec = pl.BlockSpec((GROUP,nb,BL), lambda i,_:(i,0,0))
    pspec = pl.BlockSpec((GROUP,1), lambda i,_:(i,0))
    grid_spec = pltpu.PrefetchScalarGridSpec(num_scalar_prefetch=1, grid=(C//GROUP,), in_specs=[spec,kspec,pspec], out_specs=spec,
        scratch_shapes=[pltpu.VMEM((2*nb,BL),F32)] + [pltpu.VMEM((nb*GROUP,BL),F32)]*2)
    return pl.pallas_call(partial(fwd_kernel,nb,tb), grid_spec=grid_spec,
        out_shape=jax.ShapeDtypeStruct(v.shape,out_dtype), cost_estimate=cost(13))(me,v,kr,passthrough[:,None])


def bwd_kernel(prec, nb, tb, me_ref, v_ref, m_ref, k_ref, p_ref, zr, zi, *refs):
    vb_ref, s_ref, pad, pad2, vf, mf, of = refs[-7:]
    per = tb//BL
    pad[0:nb,:] = jnp.zeros((nb,BL), F32)
    pad2[0:nb,:] = jnp.zeros((nb,BL), F32)
    me = me_ref[0]
    steps = squarings((zr[...], zi[...]), 6 + int(math.log2(nb)))
    rev = (lax.broadcasted_iota(jnp.int32,(BL,BL),0)+lax.broadcasted_iota(jnp.int32,(BL,BL),1)==BL-1).astype(F32).astype(BF)
    lane = lax.broadcasted_iota(jnp.int32,(nb,BL),1).astype(F32)
    M = zr.shape[1]
    arow = (nb-1-lax.broadcasted_iota(jnp.int32,(nb,M),0)).astype(F32)*BL
    spread(vf, v_ref, me, per)
    spread(mf, m_ref, me, per)
    vf[...] = jnp.dot(vf[...].astype(BF), rev, preferred_element_type=F32)
    for i in range(GROUP):
        def load(j):
            return mf[j*GROUP+i:j*GROUP+i+1,:] if j<nb else None
        H = toeplitz_blocks(load, nb, 1)
        pad[nb:2*nb,:] = k_ref[i].astype(F32)
        pad2[nb:2*nb,:] = vf[pl.ds(i, nb, stride=GROUP),:]
        X = jnp.concatenate([jnp.concatenate([shifted(pad,nb,nb-1-e) for e in range(nb)],1), jnp.concatenate([shifted(pad2,nb,nb-1-e) for e in range(nb)],1)],0).astype(BF)
        out = jnp.dot(X, H, preferred_element_type=F32)
        of[pl.ds(i, nb, stride=GROUP),:] = out[:nb,:]
        kb = out[nb:,:]
        st = [row(s,i) for s in steps]
        near = ladder(st[:7], BL, 1)
        far = ladder(st[7:], nb, -1)
        U = jnp.dot(jnp.concatenate([kb, kb*lane],0), jnp.concatenate(near,1), precision=prec, preferred_element_type=F32)
        u = U[:nb,:M], U[:nb,M:]
        w = U[nb:,:M]+arow*u[0], U[nb:,M:]+arow*u[1]
        s1 = cmul(u, far); s2 = cmul(w, far)
        for n,x in enumerate((*s1,*s2)):
            s_ref[n, i:i+1, :] = jnp.sum(x,0,keepdims=True)
    for j in range(nb):
        rows = slice((nb-1-j)*GROUP,(nb-j)*GROUP)
        vb_ref[me ^ (j//per), :, (j%per)*BL:(j%per+1)*BL] = (of[rows,:] + p_ref[...]*mf[j*GROUP:(j+1)*GROUP,:]).astype(vb_ref.dtype)


def backward(me, v, mb, k, passthrough, zr, zi, part, parts, earlier=(), prec=lax.Precision.DEFAULT):
    R,C,tb = v.shape
    M = zr.shape[1]
    nb = R*tb//BL
    steps = C//GROUP//parts
    spec = pl.BlockSpec((R,GROUP,tb), lambda i,_:(0,i + part*steps,0))
    kspec = pl.BlockSpec((GROUP,nb,BL), lambda i,_:(i + part*steps,0,0))
    pspec = pl.BlockSpec((GROUP,1), lambda i,_:(i + part*steps,0))
    zspec = pl.BlockSpec((GROUP,M), lambda i,_:(i + part*steps,0))
    grid_spec = pltpu.PrefetchScalarGridSpec(num_scalar_prefetch=1, grid=(steps,),
        in_specs=[spec,spec,kspec,pspec,zspec,zspec] + [pl.BlockSpec(memory_space=pl.ANY)]*len(earlier),
        out_specs=[spec, pl.BlockSpec((4,GROUP,M), lambda i,_:(0,i + part*steps,0))], scratch_shapes=[pltpu.VMEM((2*nb,BL),F32)]*2 + [pltpu.VMEM((nb*GROUP,BL),F32)]*3)
    return pl.pallas_call(partial(bwd_kernel,prec,nb,tb), grid_spec=grid_spec,
        out_shape=[jax.ShapeDtypeStruct(v.shape,BF), jax.ShapeDtypeStruct((4,C,M),jnp.float32)],
        cost_estimate=cost(21/parts), input_output_aliases={7+n:n for n in range(len(earlier))})(me,v,mb,k,passthrough[:,None],zr,zi,*earlier)


def gate_kernel(pieces, acts_ref, up_ref, bias_ref, *refs):
    gates, outs, (act_ref, slope_ref, back_ref) = refs[:pieces], refs[pieces : 2 * pieces], refs[2 * pieces :]
    width = gates[0].shape[0]
    gate_pre = bias_ref[...]
    product_back = 0.0
    for k in range(pieces):
        lanes = slice(k * width, (k + 1) * width)
        gate_pre = gate_pre + jnp.dot(acts_ref[:, lanes], gates[k][...], preferred_element_type=F32)
        product_back = product_back + dot(up_ref[:, lanes], outs[k][...], 1, 1)
    square = gate_pre * gate_pre
    bend = jnp.tanh(0.7978845608 * gate_pre * (1.0 + 0.044715 * square))
    gate_act = 0.5 * gate_pre * (1.0 + bend)
    slope = 0.5 * (1.0 + bend) + 0.5 * gate_pre * (1.0 - bend * bend) * (0.7978845608 * (1.0 + 0.134145 * square))
    act_ref[...] = gate_act
    slope_ref[...] = slope * product_back
    back_ref[...] = (product_back * gate_act).astype(BF)


def gate_stage(acts, upstream, bias, gates, outs):
    block, width = acts.shape[0], bias.shape[0]
    tile = 256
    whole = pl.BlockSpec(acts.shape, lambda i: (0, 0))
    ospec = pl.BlockSpec((block, tile), lambda i: (0, i))
    return pl.pallas_call(
        partial(gate_kernel, len(gates)),
        grid=(width // tile,),
        in_specs=[whole, whole, pl.BlockSpec((1, tile), lambda i: (0, i))]
        + [pl.BlockSpec((gate.shape[0], tile), lambda i: (0, i)) for gate in gates]
        + [pl.BlockSpec((tile, out.shape[1]), lambda i: (i, 0)) for out in outs],
        out_specs=[ospec] * 3,
        out_shape=[jax.ShapeDtypeStruct((block, width), kind) for kind in (F32, F32, BF)],
        cost_estimate=cost(8),
    )(acts, upstream, bias.reshape(1, -1), *gates, *outs)


def bits(axis):
    size = lax.axis_size(axis)
    return [1 << k for k in range(size.bit_length() - 1)]


def swap(array, axis, mask):
    return lax.ppermute(array, axis, [(i, i ^ mask) for i in range(lax.axis_size(axis))])


def exchange_blocks(blocks, axis):
    return [blocks[0]] + [swap(blocks[q], axis, q) for q in range(1, len(blocks))]


def fence(*values):
    return lax.optimization_barrier(values)


def halve(array, dim):
    return jnp.split(array, 2, dim)


class PairSum:
    def __init__(self, array, axis):
        self.axis = axis
        index = lax.axis_index(axis)
        self.half = (index ^ (index >> 1)) & 1
        length = array.shape[0] // 2
        self.kept = lax.dynamic_slice_in_dim(array, self.half * length, length)
        self.sent = lax.dynamic_slice_in_dim(array, (1 - self.half) * length, length).astype(BF)

    def pairs(self):
        return swap(self.sent, self.axis, 1)

    def add_pairs(self, got):
        self.total = (self.kept.astype(F32) + got.astype(F32)).astype(BF)

    def mirrored(self):
        for bit in bits(self.axis)[2:]:
            self.total = (self.total.astype(F32) + swap(self.total, self.axis, bit).astype(F32)).astype(BF)
        return swap(self.total, self.axis, 3) if lax.axis_size(self.axis) > 2 else None

    def add_mirrored(self, got):
        if got is not None:
            self.total = (self.total.astype(F32) + got.astype(F32)).astype(BF)

    def back(self):
        return swap(self.total, self.axis, 1)

    def join(self, got):
        first = jnp.where(self.half == 0, self.total, got)
        second = jnp.where(self.half == 0, got, self.total)
        return jnp.concatenate([first, second]).astype(F32)


def small_sum(array, axis):
    left = bits(axis)
    while left:
        one, left = left[0], left[1:]
        if left:
            two, left = left[0], left[1:]
            array = (array + swap(array, axis, one)) + (swap(array, axis, two) + swap(array, axis, one | two))
        else:
            array = array + swap(array, axis, one)
    return array


def shards(
    inputs,
    norm_gain,
    norm_shift,
    gate_weight,
    gate_bias,
    value_weight,
    value_bias,
    log_step,
    decay_rate,
    frequency,
    readout,
    passthrough,
    expand_weight,
    output_weight,
    output_bias,
    cotangent,
):
    rows = lax.axis_size("row")
    cols = lax.axis_size("col")
    row_index = lax.axis_index("row")
    col_index = lax.axis_index("col")
    tokens, narrow = inputs.shape
    block = tokens // rows
    half_ff = FF // cols
    row_channels = VALUE // rows
    channels = row_channels // cols
    local_channels = rows * channels

    def own_channels(array):
        return lax.dynamic_slice_in_dim(array, col_index * channels, channels, 0)

    state_params = tuple(own_channels(a) for a in (log_step, decay_rate, frequency, readout))
    own_pass = own_channels(passthrough)
    weights, weights_pullback = jax.vjp(mode_weights, *state_params)
    real_rate, imag_rate, mode_real, mode_imag = weights
    growth = jnp.exp(real_rate)
    z_real, z_imag = growth * jnp.cos(imag_rate), growth * jnp.sin(imag_rate)
    me = row_index.astype(jnp.int32).reshape(1)
    every = range(rows)
    order = [0]
    for bit in reversed(bits("row")):
        order = order + [q | bit for q in order]

    def across(own, other):
        return [jnp.where(col_index == 0, own, other), jnp.where(col_index == 0, other, own)]

    def at_xor(array, q, dim=0):
        return lax.dynamic_index_in_dim(array, row_index ^ q, dim, False)

    def natural(blocks):
        stacked = jnp.stack(blocks)
        return jnp.stack([at_xor(stacked, q) for q in every])

    def features(own, other):
        first, second = across(own, other)
        return jnp.concatenate([part[k] for k in every for part in (first, second)], axis=1)

    def own_features(array, flip=0):
        return jnp.concatenate(
            [
                lax.dynamic_slice_in_dim(array, (k * cols + (col_index ^ flip)) * narrow, narrow, array.ndim - 1)
                for k in every
            ],
            axis=-1,
        )

    def by_order(blocks):
        return [blocks[q] for q in order]

    def ordered_features(vectors):
        blocks = vectors.reshape(vectors.shape[0], rows, -1)
        return jnp.concatenate([at_xor(blocks, q, 1) for q in order], axis=1)

    modes_in = (z_real, z_imag, mode_real, mode_imag)
    value_half = lax.dynamic_index_in_dim(
        value_weight.reshape(-1, rows, cols, channels), col_index, 2, False
    ).reshape(-1, local_channels)
    value_bias_half = lax.dynamic_index_in_dim(
        value_bias.reshape(rows, cols, channels), col_index, 1, False
    ).reshape(local_channels, 1)
    gate_bias_half = lax.dynamic_slice_in_dim(gate_bias, col_index * half_ff, half_ff)
    gain, shift, bias = ordered_features(jnp.stack([norm_gain, norm_shift, output_bias]))

    x_parts = exchange_blocks([at_xor(inputs.reshape(rows, block, narrow), q) for q in every], "row")
    value_2 = swap(value_half, "row", 2)
    value_1 = swap(value_half, "row", 1)
    x_parts, value_2, modes_in, upstream_blocks, gate_0 = fence(
        x_parts, value_2, modes_in, cotangent.reshape(rows, block, narrow), gate_weight
    )
    x_own = jnp.stack(by_order(x_parts))
    x_other = swap(x_own, "col", 1)
    g_parts = exchange_blocks([at_xor(upstream_blocks, q) for q in every], "row")
    gate_2 = swap(gate_0, "row", 2)
    kernels = generate(modes_in, tokens, 0, 2)
    kernels, value_2 = fence(kernels, value_2)
    value_3 = swap(value_2, "row", 1)
    x_other, g_parts, value_1, value_3, kernels, output_0 = fence(
        x_other, g_parts, value_1, value_3, kernels, output_weight
    )
    value_half = jnp.concatenate([value_half, value_2, value_1, value_3])
    x_full = features(x_own, x_other)
    g_own = jnp.stack(by_order(g_parts))
    g_other = swap(g_own, "col", 1)

    source = x_full.astype(F32)
    row_mean = jnp.mean(source, axis=-1, keepdims=True)
    centered = source - row_mean
    variance = jnp.mean(centered * centered, axis=-1, keepdims=True)
    rescale = lax.rsqrt(variance + EPSILON)
    normed = centered * rescale
    acts = (normed * gain + shift).astype(BF)

    value_pre = dot(value_half, acts, 0, 1) + value_bias_half
    values = gelu(value_pre).astype(BF).reshape(rows, channels, block)
    values_sent = [at_xor(values, q) for q in every]
    values_sent, modes_in, kernels = fence(values_sent, modes_in, kernels)
    values = exchange_blocks(values_sent, "row")
    kernels = generate(modes_in, tokens, 1, 2, kernels)
    output_2 = swap(output_0, "row", 2)
    values, kernels, g_other, gate_2, expand_0 = fence(values, kernels, g_other, gate_2, expand_weight)
    kernel, kernel_flipped = kernels
    values = jnp.stack(values)
    gate_1 = swap(gate_0, "row", 1)
    gate_3 = swap(gate_2, "row", 1)
    expand_2 = swap(expand_0, "row", 2)
    mixed = forward(me, values, kernel, own_pass, BF)
    mixed, gate_1, gate_3, output_0, expand_0 = fence(mixed, gate_1, gate_3, output_0, expand_0)
    mixed = exchange_blocks([mixed[q] for q in every], "row")
    output_1 = swap(output_0, "row", 1)
    mixed, output_2, output_1, g_own = fence(mixed, output_2, output_1, g_own)
    output_3 = swap(output_2, "row", 1)
    upstream = features(g_own, g_other)
    mixed = jnp.stack(by_order(mixed))
    mixed_other = swap(mixed, "col", 1)
    expand_1 = swap(expand_0, "row", 1)
    output_3, acts, mixed = fence(output_3, acts, mixed)
    gates = (gate_0, gate_2, gate_1, gate_3)
    outputs = (output_0, output_2, output_1, output_3)
    gate_act, gate_slope, expand_back = gate_stage(acts, upstream, gate_bias_half, gates, outputs)
    gate_act, gate_slope, expand_back, mixed_other, expand_1, expand_2 = fence(
        gate_act, gate_slope, expand_back, mixed_other, expand_1, expand_2
    )
    expand_3 = swap(expand_2, "row", 1)
    mixed = jnp.stack(across(mixed, mixed_other), axis=1).reshape(VALUE, block)
    expand_full = jnp.concatenate([expand_0, expand_2, expand_1, expand_3])
    mixed_back = dot(expand_full, expand_back, 1, 1).reshape(rows, cols, channels, block)
    sent = lax.dynamic_index_in_dim(mixed_back, 1 - col_index, 1, False).astype(BF)
    mixed_back = lax.dynamic_index_in_dim(mixed_back, col_index, 1, False)
    sent, mixed, expand_full = fence(sent, mixed, expand_full)
    got = swap(sent, "col", 1)

    expand_kept, expand_sent = [dot(piece, expand_back, 1, 0).astype(BF) for piece in halve(mixed, 0)]
    expand_got = swap(expand_sent, "row", 1)
    expanded = dot(mixed, expand_full, 0, 0)
    product = (gate_act * expanded).astype(BF)
    gate_back = (gate_slope * expanded).astype(BF)
    gate_bias_delta = jnp.sum(gate_back, axis=0, dtype=F32)
    product, gate_back, got = fence(product, gate_back, got)
    mixed_back = (mixed_back + got.astype(F32)).astype(BF)
    mixed_back, upstream, acts = fence(mixed_back, upstream, acts)
    mixed_back = exchange_blocks(by_order(mixed_back), "row")
    output_kept, output_sent = [dot(product, piece, 0, 0).astype(BF) for piece in halve(upstream, 1)]
    output_got = swap(output_sent, "row", 1)
    gate_kept, gate_sent = [dot(piece, gate_back, 0, 0).astype(BF) for piece in halve(acts, 1)]
    mixed_back, expand_got, output_got, gate_sent = fence(mixed_back, expand_got, output_got, gate_sent)

    def second(kept, got, dim):
        total = kept.astype(F32) + got.astype(F32)
        return halve(total.astype(BF), dim)

    gate_got = swap(gate_sent, "row", 1)
    mixed_back = jnp.stack(mixed_back)
    expand_kept, expand_sent = second(expand_kept, expand_got, 0)
    output_kept, output_sent = second(output_kept, output_got, 1)
    mixed_back, expand_sent, output_sent = fence(mixed_back, expand_sent, output_sent)
    expand_got = swap(expand_sent, "row", 2)
    output_got = swap(output_sent, "row", 2)
    state_args = (me, values, mixed_back, kernel_flipped, own_pass, z_real, z_imag)
    back = backward(*state_args, 0, 2)
    back, expand_got, gate_got = fence(back, expand_got, gate_got)
    expand_sum = PairSum(expand_kept.astype(F32) + expand_got.astype(F32), "dp")
    gate_kept, gate_sent = second(gate_kept, gate_got, 0)
    back, expand_sum.sent, gate_sent = fence(back, expand_sum.sent, gate_sent)
    expand_got = expand_sum.pairs()
    gate_got = swap(gate_sent, "row", 2)
    back = backward(*state_args, 1, 2, back)
    back, expand_got, output_got = fence(back, expand_got, output_got)
    values_back, sums = back
    gate_full, output_full = jnp.concatenate(gates), jnp.concatenate(outputs, axis=1)
    values_back = exchange_blocks([values_back[q] for q in every], "row")
    expand_sum.add_pairs(expand_got)
    output_sum = PairSum(output_kept.astype(F32) + output_got.astype(F32), "dp")
    output_sum.sent, expand_sum.total = fence(output_sum.sent, expand_sum.total)
    expand_got = expand_sum.mirrored()
    output_got = output_sum.pairs()
    values_back, expand_got, output_got = fence(values_back, expand_got, output_got)
    expand_sum.add_mirrored(expand_got)
    output_sum.add_pairs(output_got)
    expand_got = expand_sum.back()
    output_got = output_sum.mirrored()

    def to_tokens(array):
        blocks = by_order(jnp.split(array, rows, 1))
        return natural(exchange_blocks(blocks, "row")).reshape(tokens, narrow)

    values_back = natural(values_back).reshape(local_channels, block)
    value_back = gelu_back(value_pre, values_back.astype(F32)).astype(BF)
    value_kept, value_sent = [dot(piece, value_back, 0, 1).astype(BF) for piece in halve(acts, 1)]
    value_kept, value_sent = second(value_kept, swap(value_sent, "row", 1), 0)
    value_weight_delta = value_kept.astype(F32) + swap(value_sent, "row", 2).astype(F32)
    value_bias_delta = jnp.sum(value_back, axis=1, dtype=F32)
    passthrough_delta = jnp.sum(mixed_back.astype(F32) * values.astype(F32), axis=(0, 2))
    first_real, first_imag, second_real, second_imag = sums
    state_deltas = weights_pullback(
        (
            mode_real * second_real - mode_imag * second_imag,
            -mode_real * second_imag - mode_imag * second_real,
            first_real,
            -first_imag,
        )
    )

    acts_back = dot(gate_back, gate_full, 1, 1) + dot(value_back, value_half, 0, 1)
    weighted = acts_back * gain
    moments = jnp.stack([jnp.sum(weighted, axis=1), jnp.sum(weighted * normed, axis=1)])
    acts_sent = own_features(acts_back, 1).astype(BF)
    acts_got = swap(acts_sent, "col", 1)
    moments = small_sum(moments, "col") / D
    acts_got, moments, gate_got, expand_got = fence(acts_got, moments, gate_got, expand_got)
    expand_delta = expand_sum.join(expand_got)
    gate_sum = PairSum(gate_kept.astype(F32) + gate_got.astype(F32), "dp")
    gate_got = gate_sum.pairs()

    acts_back = own_features(acts_back) + acts_got.astype(F32)
    own_normed = own_features(normed)
    gain_delta = jnp.sum(acts_back * own_normed, axis=0)
    shift_delta = jnp.sum(acts_back, axis=0)
    input_delta = rescale * (acts_back * own_features(gain) - moments[0][:, None] - own_normed * moments[1][:, None])
    input_delta = cotangent.astype(F32) + to_tokens(input_delta.astype(BF)).astype(F32)
    input_delta, output_got, gate_got, product = fence(input_delta, output_got, gate_got, product)
    output_sum.add_mirrored(output_got)
    gate_sum.add_pairs(gate_got)
    output_got = output_sum.back()
    gate_got = gate_sum.mirrored()
    out_sum = dot(product, output_full, 1, 0)
    out_sum = own_features(out_sum) + swap(own_features(out_sum, 1).astype(BF), "col", 1).astype(F32)
    block_output = to_tokens((own_features(source) + out_sum + own_features(bias)).astype(BF))
    output_weight_delta = output_sum.join(output_got)
    gate_sum.add_mirrored(gate_got)
    gate_weight_delta = gate_sum.join(gate_sum.back())

    biases = jnp.concatenate([gate_bias_delta, value_bias_delta])
    norms = jnp.stack([gain_delta, shift_delta]).reshape(2, rows, narrow)
    small = exchange_blocks(
        [jnp.concatenate([norms[:, k].reshape(-1), biases]) for k in (order.index(q) for q in every)], "row"
    )
    while len(small) > 1:
        small = [a + b for a, b in zip(small[::2], small[1::2])]
    small = jnp.concatenate(
        [small[0], jnp.sum(cotangent, axis=0, dtype=F32), state_deltas[0], passthrough_delta]
    )
    small = small_sum(small, "dp")
    ends = [narrow, 2 * narrow, 2 * narrow + half_ff, 2 * narrow + half_ff + local_channels]
    gain_sum, shift_sum, gate_bias_sum, value_bias_sum, bias_sum, shared = jnp.split(small, ends + [ends[-1] + narrow])
    shared = jnp.concatenate([value_bias_sum, shared]).reshape(rows + 2, channels)
    shared = jnp.stack(across(shared, swap(shared, "col", 1)), axis=1).reshape(-1)
    value_bias_sum, step_sum, pass_sum = jnp.split(shared, [VALUE, VALUE + row_channels])

    state = jnp.concatenate(state_deltas[1:], axis=1)
    late = jnp.concatenate([value_weight_delta.reshape(-1), state.reshape(-1)]).reshape(-1, local_channels)
    late_sum = PairSum(late, "dp")
    late_sum.add_pairs(late_sum.pairs())
    late_sum.add_mirrored(late_sum.mirrored())
    late = late_sum.join(late_sum.back()).astype(BF)
    late = jnp.stack(across(late, swap(late, "col", 1)))
    value_rows = value_weight_delta.shape[0]
    value_weight_delta = late[:, :value_rows].reshape(cols, -1, rows, channels)
    value_weight_delta = value_weight_delta.transpose(1, 2, 0, 3).reshape(-1, VALUE).astype(F32)
    state = late[:, value_rows:].reshape(row_channels, -1).astype(F32)
    modes = decay_rate.shape[1]
    return (
        block_output,
        input_delta,
        gain_sum,
        shift_sum,
        gate_weight_delta,
        gate_bias_sum,
        value_weight_delta,
        value_bias_sum,
        step_sum,
        state[:, :modes],
        state[:, modes : 2 * modes],
        state[:, 2 * modes :],
        pass_sum,
        expand_delta,
        output_weight_delta,
        bias_sum,
    )


def solution(mesh):
    placed = (
        P("dp", ("row", "col")),
        P(),
        P(),
        P("row", "col"),
        P(),
        P("row", None),
        P(),
        P("row"),
        P("row", None),
        P("row", None),
        P("row", None),
        P("row"),
        P("row", "col"),
        P("col", "row"),
        P(),
        P("dp", ("row", "col")),
    )
    return jax.shard_map(
        shards,
        mesh=mesh,
        in_specs=placed,
        out_specs=(
            P("dp", ("row", "col")),
            P("dp", ("row", "col")),
            P(("row", "col")),
            P(("row", "col")),
            P("row", "col"),
            P("col"),
            P("row", None),
            P(),
            P("row"),
            P("row", None),
            P("row", None),
            P("row", None),
            P("row"),
            P("row", "col"),
            P("col", "row"),
            P(("row", "col")),
        ),
        check_vma=False,
    )
```

```python
from functools import partial
import math

import jax
import jax.numpy as jnp
from jax import lax
from jax.experimental import pallas as pl
from jax.experimental.pallas import tpu as pltpu
from jax.sharding import PartitionSpec as P

D = 1024
FF = 3072
VALUE = 512
LEN = 2048
EPSILON = 1e-05
BL = 128
GROUP = 8
BF = jnp.bfloat16
F32 = jnp.float32


def dot(left, right, left_dim, right_dim):
    return lax.dot_general(
        left, right, (((left_dim,), (right_dim,)), ((), ())), preferred_element_type=F32
    )


def gelu(pre_act):
    return jax.nn.gelu(pre_act, approximate=True)


def gelu_back(pre_act, upstream):
    return jax.vjp(gelu, pre_act)[1](upstream)[0]


def mode_weights(log_step, decay_rate, frequency, readout):
    time_step = jnp.exp(log_step)[:, None]
    real_rate = -decay_rate * time_step
    imag_rate = frequency * time_step
    growth = jnp.exp(real_rate)
    shift_real = growth * jnp.cos(imag_rate) - 1.0
    shift_imag = growth * jnp.sin(imag_rate)
    modulus = decay_rate * decay_rate + frequency * frequency
    ratio_real = (shift_imag * frequency - shift_real * decay_rate) / modulus
    ratio_imag = (-shift_imag * decay_rate - shift_real * frequency) / modulus
    modes = decay_rate.shape[1]
    out_real = readout[:, :modes]
    out_imag = readout[:, modes:]
    mode_real = out_real * ratio_real - out_imag * ratio_imag
    mode_imag = out_real * ratio_imag + out_imag * ratio_real
    return (real_rate, imag_rate, mode_real, mode_imag)


def cmul(a, b):
    return a[0]*b[0]-a[1]*b[1], a[0]*b[1]+a[1]*b[0]

def squarings(z, n):
    out=[z]
    for _ in range(n):
        r,i=out[-1]
        out.append((r*r-i*i, 2.0*r*i))
    return out

def ladder(steps, rows, order, first=None):
    M = steps[0][0].shape[1]
    idx = lax.broadcasted_iota(jnp.int32, (8, M), 0)
    if order < 0: idx = 7-idx
    wr = jnp.ones((8,M), jnp.float32); wi = jnp.zeros((8,M), jnp.float32)
    for b in range(3):
        hit = (idx >> b) & 1
        nr, ni = cmul((wr,wi), steps[b])
        wr = jnp.where(hit==1, nr, wr); wi = jnp.where(hit==1, ni, wi)
    groups=[(wr,wi)]
    k=3
    while len(groups)*8 < rows:
        groups += [cmul(g, steps[k]) for g in groups]
        k+=1
    if order<0: groups = groups[::-1]
    return jnp.concatenate([g[0] for g in groups],0), jnp.concatenate([g[1] for g in groups],0)

def row(p, i):
    return p[0][i:i+1], p[1][i:i+1]

def two_terms(x):
    high = x.astype(BF)
    return high, (x - high.astype(F32)).astype(BF)


def gen_kernel(nb, zr, zi, cr, ci, *refs):
    k_out, kr_out = refs[-2:]
    steps = squarings((zr[...], zi[...]), 6 + int(math.log2(nb)))
    rev = (lax.broadcasted_iota(jnp.int32,(BL,BL),0)+lax.broadcasted_iota(jnp.int32,(BL,BL),1)==BL-1).astype(F32).astype(BF)
    nt = (((1,),(1,)),((),()))
    for i in range(GROUP):
        st = [row(x,i) for x in steps]
        near = ladder(st[:7], BL, 1)
        far = ladder(st[7:], nb, 1)
        lead = cmul((cr[i:i+1,:], ci[i:i+1,:]), far)
        lh, ll = two_terms(jnp.concatenate([lead[0], -lead[1]],1))
        nh, nl = two_terms(jnp.concatenate(near,1))
        first = lax.dot_general(jnp.concatenate([lh, ll]), nh, nt, preferred_element_type=F32)
        k = first[:nb] + (first[nb:] + lax.dot_general(lh, nl, nt, preferred_element_type=F32))
        kb = k.astype(BF)
        k_out[i] = kb
    kr_out[...] = jnp.dot(k_out[...].reshape(GROUP*nb, BL), rev, preferred_element_type=F32).astype(BF).reshape(GROUP, nb, BL)


def cost(microseconds):
    return pl.CostEstimate(flops=int(microseconds * 1e9), bytes_accessed=1 << 20, transcendentals=0)


def generate(modes, length, part, parts, earlier=()):
    C, M = modes[0].shape
    nb = length//BL
    steps = C//GROUP//parts
    spec = pl.BlockSpec((GROUP, M), lambda i:(i + part*steps,0))
    ospec = pl.BlockSpec((GROUP, nb, BL), lambda i:(i + part*steps,0,0))
    sh = jax.ShapeDtypeStruct((C,nb,BL), BF)
    return pl.pallas_call(partial(gen_kernel, nb), grid=(steps,), in_specs=[spec]*4 + [pl.BlockSpec(memory_space=pl.ANY)]*len(earlier), out_specs=[ospec]*2,
        out_shape=[sh,sh], cost_estimate=cost(10/parts), input_output_aliases={4+k:k for k in range(len(earlier))})(*modes, *earlier)


def toeplitz_blocks(load, count, shift):
    r = lax.broadcasted_iota(jnp.int32,(BL,BL),0); c = lax.broadcasted_iota(jnp.int32,(BL,BL),1)
    mask = c >= r + shift
    def rot(j):
        x = load(j)
        if x is None: return jnp.zeros((BL,BL), BF)
        base = pltpu.roll(jnp.broadcast_to(x,(64,BL)), shift, 1, stride=1, stride_axis=0).astype(BF)
        return jnp.concatenate([base] + [pltpu.roll(base, 64, 1)], 0)
    out=[]
    cur = rot(0)
    for j in range(count):
        nxt = rot(j+1)
        out.append(jnp.where(mask, nxt, cur))
        cur = nxt
    return jnp.concatenate(out,0)


def toeplitz_old(load, count, shift):
    r = lax.broadcasted_iota(jnp.int32,(BL,BL),0); c = lax.broadcasted_iota(jnp.int32,(BL,BL),1)
    mask = c >= r + shift
    def rot(j):
        x = load(j)
        if x is None: return jnp.zeros((BL,BL), jnp.float32)
        return pltpu.roll(jnp.broadcast_to(x,(BL,BL)), shift, 1, stride=1, stride_axis=0)
    out=[]
    cur = rot(0)
    for j in range(count):
        nxt = rot(j+1)
        out.append(jnp.where(mask, nxt, cur).astype(jnp.bfloat16))
        cur = nxt
    return jnp.concatenate(out,0)


def spread(dst, src, me, per):
    for j in range(dst.shape[0]//GROUP):
        dst[j*GROUP:(j+1)*GROUP,:] = src[me ^ (j//per), :, (j%per)*BL:(j%per+1)*BL].astype(F32)


def gather_out(dst, src, extra, scale, me, per):
    for j in range(src.shape[0]//GROUP):
        rows = slice(j*GROUP,(j+1)*GROUP)
        dst[me ^ (j//per), :, (j%per)*BL:(j%per+1)*BL] = (src[rows,:] + scale*extra[rows,:]).astype(dst.dtype)


def shifted(pad_ref, nb, d):
    return pad_ref[pl.ds(nb-d, nb), :]


def fwd_kernel(nb, tb, me_ref, v_ref, kr_ref, p_ref, out_ref, pad, vf, of):
    per = tb//BL
    me = me_ref[0]
    pad[0:nb,:] = jnp.zeros((nb,BL), F32)
    spread(vf, v_ref, me, per)
    for i in range(GROUP):
        def load(j):
            return vf[(j-1)*GROUP+i:(j-1)*GROUP+i+1,:] if j else None
        H = toeplitz_old(load, nb, 0)
        pad[nb:2*nb,:] = kr_ref[i].astype(F32)
        X = jnp.concatenate([shifted(pad,nb,d) for d in range(nb)],1).astype(BF)
        of[pl.ds(i, nb, stride=GROUP),:] = jnp.dot(X, H, preferred_element_type=F32)
    gather_out(out_ref, of, vf, p_ref[...], me, per)


def forward(me, v, kr, passthrough, out_dtype=jnp.float32):
    R,C,tb = v.shape
    nb = R*tb//BL
    spec = pl.BlockSpec((R,GROUP,tb), lambda i,_:(0,i,0))
    kspec = pl.BlockSpec((GROUP,nb,BL), lambda i,_:(i,0,0))
    pspec = pl.BlockSpec((GROUP,1), lambda i,_:(i,0))
    grid_spec = pltpu.PrefetchScalarGridSpec(num_scalar_prefetch=1, grid=(C//GROUP,), in_specs=[spec,kspec,pspec], out_specs=spec,
        scratch_shapes=[pltpu.VMEM((2*nb,BL),F32)] + [pltpu.VMEM((nb*GROUP,BL),F32)]*2)
    return pl.pallas_call(partial(fwd_kernel,nb,tb), grid_spec=grid_spec,
        out_shape=jax.ShapeDtypeStruct(v.shape,out_dtype), cost_estimate=cost(13))(me,v,kr,passthrough[:,None])


def bwd_kernel(prec, nb, tb, me_ref, v_ref, m_ref, k_ref, p_ref, zr, zi, *refs):
    vb_ref, s_ref, pad, pad2, vf, mf, of = refs[-7:]
    per = tb//BL
    pad[0:nb,:] = jnp.zeros((nb,BL), F32)
    pad2[0:nb,:] = jnp.zeros((nb,BL), F32)
    me = me_ref[0]
    steps = squarings((zr[...], zi[...]), 6 + int(math.log2(nb)))
    rev = (lax.broadcasted_iota(jnp.int32,(BL,BL),0)+lax.broadcasted_iota(jnp.int32,(BL,BL),1)==BL-1).astype(F32).astype(BF)
    lane = lax.broadcasted_iota(jnp.int32,(nb,BL),1).astype(F32)
    M = zr.shape[1]
    arow = (nb-1-lax.broadcasted_iota(jnp.int32,(nb,M),0)).astype(F32)*BL
    spread(vf, v_ref, me, per)
    spread(mf, m_ref, me, per)
    vf[...] = jnp.dot(vf[...].astype(BF), rev, preferred_element_type=F32)
    for i in range(GROUP):
        def load(j):
            return mf[j*GROUP+i:j*GROUP+i+1,:] if j<nb else None
        H = toeplitz_blocks(load, nb, 1)
        pad[nb:2*nb,:] = k_ref[i].astype(F32)
        pad2[nb:2*nb,:] = vf[pl.ds(i, nb, stride=GROUP),:]
        X = jnp.concatenate([jnp.concatenate([shifted(pad,nb,nb-1-e) for e in range(nb)],1), jnp.concatenate([shifted(pad2,nb,nb-1-e) for e in range(nb)],1)],0).astype(BF)
        out = jnp.dot(X, H, preferred_element_type=F32)
        of[pl.ds(i, nb, stride=GROUP),:] = out[:nb,:]
        kb = out[nb:,:]
        st = [row(s,i) for s in steps]
        near = ladder(st[:7], BL, 1)
        far = ladder(st[7:], nb, -1)
        U = jnp.dot(jnp.concatenate([kb, kb*lane],0), jnp.concatenate(near,1), precision=prec, preferred_element_type=F32)
        u = U[:nb,:M], U[:nb,M:]
        w = U[nb:,:M]+arow*u[0], U[nb:,M:]+arow*u[1]
        s1 = cmul(u, far); s2 = cmul(w, far)
        for n,x in enumerate((*s1,*s2)):
            s_ref[n, i:i+1, :] = jnp.sum(x,0,keepdims=True)
    for j in range(nb):
        rows = slice((nb-1-j)*GROUP,(nb-j)*GROUP)
        vb_ref[me ^ (j//per), :, (j%per)*BL:(j%per+1)*BL] = (of[rows,:] + p_ref[...]*mf[j*GROUP:(j+1)*GROUP,:]).astype(vb_ref.dtype)


def backward(me, v, mb, k, passthrough, zr, zi, part, parts, earlier=(), prec=lax.Precision.DEFAULT):
    R,C,tb = v.shape
    M = zr.shape[1]
    nb = R*tb//BL
    steps = C//GROUP//parts
    spec = pl.BlockSpec((R,GROUP,tb), lambda i,_:(0,i + part*steps,0))
    kspec = pl.BlockSpec((GROUP,nb,BL), lambda i,_:(i + part*steps,0,0))
    pspec = pl.BlockSpec((GROUP,1), lambda i,_:(i + part*steps,0))
    zspec = pl.BlockSpec((GROUP,M), lambda i,_:(i + part*steps,0))
    grid_spec = pltpu.PrefetchScalarGridSpec(num_scalar_prefetch=1, grid=(steps,),
        in_specs=[spec,spec,kspec,pspec,zspec,zspec] + [pl.BlockSpec(memory_space=pl.ANY)]*len(earlier),
        out_specs=[spec, pl.BlockSpec((4,GROUP,M), lambda i,_:(0,i + part*steps,0))], scratch_shapes=[pltpu.VMEM((2*nb,BL),F32)]*2 + [pltpu.VMEM((nb*GROUP,BL),F32)]*3)
    return pl.pallas_call(partial(bwd_kernel,prec,nb,tb), grid_spec=grid_spec,
        out_shape=[jax.ShapeDtypeStruct(v.shape,BF), jax.ShapeDtypeStruct((4,C,M),jnp.float32)],
        cost_estimate=cost(21/parts), input_output_aliases={7+n:n for n in range(len(earlier))})(me,v,mb,k,passthrough[:,None],zr,zi,*earlier)


def gate_kernel(pieces, acts_ref, up_ref, bias_ref, *refs):
    gates, outs, (act_ref, slope_ref, back_ref) = refs[:pieces], refs[pieces : 2 * pieces], refs[2 * pieces :]
    width = gates[0].shape[0]
    gate_pre = bias_ref[...]
    product_back = 0.0
    for k in range(pieces):
        lanes = slice(k * width, (k + 1) * width)
        gate_pre = gate_pre + jnp.dot(acts_ref[:, lanes], gates[k][...], preferred_element_type=F32)
        product_back = product_back + dot(up_ref[:, lanes], outs[k][...], 1, 1)
    square = gate_pre * gate_pre
    bend = jnp.tanh(0.7978845608 * gate_pre * (1.0 + 0.044715 * square))
    gate_act = 0.5 * gate_pre * (1.0 + bend)
    slope = 0.5 * (1.0 + bend) + 0.5 * gate_pre * (1.0 - bend * bend) * (0.7978845608 * (1.0 + 0.134145 * square))
    act_ref[...] = gate_act
    slope_ref[...] = slope * product_back
    back_ref[...] = (product_back * gate_act).astype(BF)


def gate_stage(acts, upstream, bias, gates, outs):
    block, width = acts.shape[0], bias.shape[0]
    tile = 512
    whole = pl.BlockSpec(acts.shape, lambda i: (0, 0))
    ospec = pl.BlockSpec((block, tile), lambda i: (0, i))
    return pl.pallas_call(
        partial(gate_kernel, len(gates)),
        grid=(width // tile,),
        in_specs=[whole, whole, pl.BlockSpec((1, tile), lambda i: (0, i))]
        + [pl.BlockSpec((gate.shape[0], tile), lambda i: (0, i)) for gate in gates]
        + [pl.BlockSpec((tile, out.shape[1]), lambda i: (i, 0)) for out in outs],
        out_specs=[ospec] * 3,
        out_shape=[jax.ShapeDtypeStruct((block, width), kind) for kind in (F32, F32, BF)],
        cost_estimate=cost(8),
    )(acts, upstream, bias.reshape(1, -1), *gates, *outs)


def bits(axis):
    size = lax.axis_size(axis)
    return [1 << k for k in range(size.bit_length() - 1)]


def swap(array, axis, mask):
    return lax.ppermute(array, axis, [(i, i ^ mask) for i in range(lax.axis_size(axis))])


def exchange_blocks(blocks, axis):
    return [blocks[0]] + [swap(blocks[q], axis, q) for q in range(1, len(blocks))]


def fence(*values):
    return lax.optimization_barrier(values)


def halve(array, dim):
    return jnp.split(array, 2, dim)


class PairSum:
    def __init__(self, array, axis):
        self.axis = axis
        index = lax.axis_index(axis)
        self.half = (index ^ (index >> 1)) & 1
        length = array.shape[0] // 2
        self.kept = lax.dynamic_slice_in_dim(array, self.half * length, length)
        self.sent = lax.dynamic_slice_in_dim(array, (1 - self.half) * length, length).astype(BF)

    def pairs(self):
        return swap(self.sent, self.axis, 1)

    def add_pairs(self, got):
        self.total = (self.kept.astype(F32) + got.astype(F32)).astype(BF)

    def mirrored(self):
        for bit in bits(self.axis)[2:]:
            self.total = (self.total.astype(F32) + swap(self.total, self.axis, bit).astype(F32)).astype(BF)
        return swap(self.total, self.axis, 3) if lax.axis_size(self.axis) > 2 else None

    def add_mirrored(self, got):
        if got is not None:
            self.total = (self.total.astype(F32) + got.astype(F32)).astype(BF)

    def back(self):
        return swap(self.total, self.axis, 1)

    def join(self, got):
        first = jnp.where(self.half == 0, self.total, got)
        second = jnp.where(self.half == 0, got, self.total)
        return jnp.concatenate([first, second]).astype(F32)


def small_sum(array, axis):
    left = bits(axis)
    while left:
        one, left = left[0], left[1:]
        if left:
            two, left = left[0], left[1:]
            array = (array + swap(array, axis, one)) + (swap(array, axis, two) + swap(array, axis, one | two))
        else:
            array = array + swap(array, axis, one)
    return array


def shards(
    inputs,
    norm_gain,
    norm_shift,
    gate_weight,
    gate_bias,
    value_weight,
    value_bias,
    log_step,
    decay_rate,
    frequency,
    readout,
    passthrough,
    expand_weight,
    output_weight,
    output_bias,
    cotangent,
):
    rows = lax.axis_size("row")
    cols = lax.axis_size("col")
    row_index = lax.axis_index("row")
    col_index = lax.axis_index("col")
    tokens, narrow = inputs.shape
    block = tokens // rows
    half_ff = FF // cols
    row_channels = VALUE // rows
    channels = row_channels // cols
    local_channels = rows * channels

    def own_channels(array):
        return lax.dynamic_slice_in_dim(array, col_index * channels, channels, 0)

    state_params = tuple(own_channels(a) for a in (log_step, decay_rate, frequency, readout))
    own_pass = own_channels(passthrough)
    weights, weights_pullback = jax.vjp(mode_weights, *state_params)
    real_rate, imag_rate, mode_real, mode_imag = weights
    growth = jnp.exp(real_rate)
    z_real, z_imag = growth * jnp.cos(imag_rate), growth * jnp.sin(imag_rate)
    me = row_index.astype(jnp.int32).reshape(1)
    every = range(rows)
    order = [0]
    for bit in reversed(bits("row")):
        order = order + [q | bit for q in order]

    def across(own, other):
        return [jnp.where(col_index == 0, own, other), jnp.where(col_index == 0, other, own)]

    def at_xor(array, q, dim=0):
        return lax.dynamic_index_in_dim(array, row_index ^ q, dim, False)

    def natural(blocks):
        stacked = jnp.stack(blocks)
        return jnp.stack([at_xor(stacked, q) for q in every])

    def features(own, other):
        first, second = across(own, other)
        return jnp.concatenate([part[k] for k in every for part in (first, second)], axis=1)

    def own_features(array, flip=0):
        return jnp.concatenate(
            [
                lax.dynamic_slice_in_dim(array, (k * cols + (col_index ^ flip)) * narrow, narrow, array.ndim - 1)
                for k in every
            ],
            axis=-1,
        )

    def by_order(blocks):
        return [blocks[q] for q in order]

    def ordered_features(vectors):
        blocks = vectors.reshape(vectors.shape[0], rows, -1)
        return jnp.concatenate([at_xor(blocks, q, 1) for q in order], axis=1)

    modes_in = (z_real, z_imag, mode_real, mode_imag)
    value_half = lax.dynamic_index_in_dim(
        value_weight.reshape(-1, rows, cols, channels), col_index, 2, False
    ).reshape(-1, local_channels)
    value_bias_half = lax.dynamic_index_in_dim(
        value_bias.reshape(rows, cols, channels), col_index, 1, False
    ).reshape(local_channels, 1)
    gate_bias_half = lax.dynamic_slice_in_dim(gate_bias, col_index * half_ff, half_ff)
    gain, shift, bias = ordered_features(jnp.stack([norm_gain, norm_shift, output_bias]))

    x_parts = exchange_blocks([at_xor(inputs.reshape(rows, block, narrow), q) for q in every], "row")
    value_2 = swap(value_half, "row", 2)
    value_1 = swap(value_half, "row", 1)
    x_parts, value_2, modes_in, upstream_blocks, gate_0 = fence(
        x_parts, value_2, modes_in, cotangent.reshape(rows, block, narrow), gate_weight
    )
    x_own = jnp.stack(by_order(x_parts))
    x_other = swap(x_own, "col", 1)
    g_parts = exchange_blocks([at_xor(upstream_blocks, q) for q in every], "row")
    gate_2 = swap(gate_0, "row", 2)
    gate_1 = swap(gate_0, "row", 1)
    kernels = generate(modes_in, tokens, 0, 2)
    value_3 = swap(value_2, "row", 1)
    x_other, value_1, value_3, kernels, output_0 = fence(x_other, value_1, value_3, kernels, output_weight)
    value_half = jnp.concatenate([value_half, value_2, value_1, value_3])
    x_full = features(x_own, x_other)

    source = x_full.astype(F32)
    row_mean = jnp.mean(source, axis=-1, keepdims=True)
    centered = source - row_mean
    variance = jnp.mean(centered * centered, axis=-1, keepdims=True)
    rescale = lax.rsqrt(variance + EPSILON)
    normed = centered * rescale
    acts = (normed * gain + shift).astype(BF)

    value_pre = dot(value_half, acts, 0, 1) + value_bias_half
    values = gelu(value_pre).astype(BF).reshape(rows, channels, block)
    values_sent = [at_xor(values, q) for q in every]
    values_sent, modes_in, kernels, gate_2, gate_1 = fence(values_sent, modes_in, kernels, gate_2, gate_1)
    values = exchange_blocks(values_sent, "row")
    kernels = generate(modes_in, tokens, 1, 2, kernels)
    output_2 = swap(output_0, "row", 2)
    values, kernels, g_parts, expand_0 = fence(values, kernels, g_parts, expand_weight)
    g_own = jnp.stack(by_order(g_parts))
    g_other = swap(g_own, "col", 1)
    kernel, kernel_flipped = kernels
    values = jnp.stack(values)
    gate_3 = swap(gate_2, "row", 1)
    expand_2 = swap(expand_0, "row", 2)
    mixed = forward(me, values, kernel, own_pass, BF)
    mixed, gate_1, gate_3, output_0, expand_0, g_other = fence(mixed, gate_1, gate_3, output_0, expand_0, g_other)
    mixed = exchange_blocks([mixed[q] for q in every], "row")
    output_1 = swap(output_0, "row", 1)
    mixed, output_2, output_1, g_own = fence(mixed, output_2, output_1, g_own)
    output_3 = swap(output_2, "row", 1)
    upstream = features(g_own, g_other)
    mixed = jnp.stack(by_order(mixed))
    mixed_other = swap(mixed, "col", 1)
    expand_1 = swap(expand_0, "row", 1)
    output_3, acts, mixed = fence(output_3, acts, mixed)
    gates = (gate_0, gate_2, gate_1, gate_3)
    outputs = (output_0, output_2, output_1, output_3)
    gate_act, gate_slope, expand_back = gate_stage(acts, upstream, gate_bias_half, gates, outputs)
    gate_act, gate_slope, expand_back, mixed_other, expand_1, expand_2 = fence(
        gate_act, gate_slope, expand_back, mixed_other, expand_1, expand_2
    )
    expand_3 = swap(expand_2, "row", 1)
    mixed = jnp.stack(across(mixed, mixed_other), axis=1).reshape(VALUE, block)
    expand_full = jnp.concatenate([expand_0, expand_2, expand_1, expand_3])
    mixed_back = dot(expand_full, expand_back, 1, 1).reshape(rows, cols, channels, block)
    sent = lax.dynamic_index_in_dim(mixed_back, 1 - col_index, 1, False).astype(BF)
    mixed_back = lax.dynamic_index_in_dim(mixed_back, col_index, 1, False)
    sent, mixed, expand_full = fence(sent, mixed, expand_full)
    got = swap(sent, "col", 1)

    expand_kept, expand_sent = [dot(piece, expand_back, 1, 0).astype(BF) for piece in halve(mixed, 0)]
    expand_got = swap(expand_sent, "row", 1)
    expanded = dot(mixed, expand_full, 0, 0)
    product = (gate_act * expanded).astype(BF)
    gate_back = (gate_slope * expanded).astype(BF)
    gate_bias_delta = jnp.sum(gate_back, axis=0, dtype=F32)
    product, gate_back, got = fence(product, gate_back, got)
    mixed_back = (mixed_back + got.astype(F32)).astype(BF)
    mixed_back, upstream, acts = fence(mixed_back, upstream, acts)
    mixed_back = exchange_blocks(by_order(mixed_back), "row")
    output_kept, output_sent = [dot(product, piece, 0, 0).astype(BF) for piece in halve(upstream, 1)]
    output_got = swap(output_sent, "row", 1)
    gate_kept, gate_sent = [dot(piece, gate_back, 0, 0).astype(BF) for piece in halve(acts, 1)]
    mixed_back, expand_got, output_got, gate_sent = fence(mixed_back, expand_got, output_got, gate_sent)

    def second(kept, got, dim):
        total = kept.astype(F32) + got.astype(F32)
        return halve(total.astype(BF), dim)

    gate_got = swap(gate_sent, "row", 1)
    mixed_back = jnp.stack(mixed_back)
    expand_kept, expand_sent = second(expand_kept, expand_got, 0)
    output_kept, output_sent = second(output_kept, output_got, 1)
    mixed_back, expand_sent, output_sent = fence(mixed_back, expand_sent, output_sent)
    expand_got = swap(expand_sent, "row", 2)
    output_got = swap(output_sent, "row", 2)
    state_args = (me, values, mixed_back, kernel_flipped, own_pass, z_real, z_imag)
    back = backward(*state_args, 0, 2)
    back, expand_got, gate_got = fence(back, expand_got, gate_got)
    expand_sum = PairSum(expand_kept.astype(F32) + expand_got.astype(F32), "dp")
    gate_kept, gate_sent = second(gate_kept, gate_got, 0)
    back, expand_sum.sent, gate_sent = fence(back, expand_sum.sent, gate_sent)
    expand_got = expand_sum.pairs()
    gate_got = swap(gate_sent, "row", 2)
    back = backward(*state_args, 1, 2, back)
    back, expand_got, output_got = fence(back, expand_got, output_got)
    values_back, sums = back
    gate_full, output_full = jnp.concatenate(gates), jnp.concatenate(outputs, axis=1)
    values_back = exchange_blocks([values_back[q] for q in every], "row")
    expand_sum.add_pairs(expand_got)
    output_sum = PairSum(output_kept.astype(F32) + output_got.astype(F32), "dp")
    output_sum.sent, expand_sum.total = fence(output_sum.sent, expand_sum.total)
    expand_got = expand_sum.mirrored()
    output_got = output_sum.pairs()
    values_back, expand_got, output_got = fence(values_back, expand_got, output_got)
    expand_sum.add_mirrored(expand_got)
    output_sum.add_pairs(output_got)
    expand_got = expand_sum.back()
    output_got = output_sum.mirrored()

    def to_tokens(array):
        blocks = by_order(jnp.split(array, rows, 1))
        return natural(exchange_blocks(blocks, "row")).reshape(tokens, narrow)

    values_back = natural(values_back).reshape(local_channels, block)
    value_back = gelu_back(value_pre, values_back.astype(F32)).astype(BF)
    value_kept, value_sent = [dot(piece, value_back, 0, 1).astype(BF) for piece in halve(acts, 1)]
    value_kept, value_sent = second(value_kept, swap(value_sent, "row", 1), 0)
    value_weight_delta = value_kept.astype(F32) + swap(value_sent, "row", 2).astype(F32)
    value_bias_delta = jnp.sum(value_back, axis=1, dtype=F32)
    passthrough_delta = jnp.sum(mixed_back.astype(F32) * values.astype(F32), axis=(0, 2))
    first_real, first_imag, second_real, second_imag = sums
    state_deltas = weights_pullback(
        (
            mode_real * second_real - mode_imag * second_imag,
            -mode_real * second_imag - mode_imag * second_real,
            first_real,
            -first_imag,
        )
    )

    acts_back = dot(gate_back, gate_full, 1, 1) + dot(value_back, value_half, 0, 1)
    weighted = acts_back * gain
    moments = jnp.stack([jnp.sum(weighted, axis=1), jnp.sum(weighted * normed, axis=1)])
    acts_sent = own_features(acts_back, 1).astype(BF)
    acts_got = swap(acts_sent, "col", 1)
    moments = small_sum(moments, "col") / D
    acts_got, moments, gate_got, expand_got = fence(acts_got, moments, gate_got, expand_got)
    expand_delta = expand_sum.join(expand_got)
    gate_sum = PairSum(gate_kept.astype(F32) + gate_got.astype(F32), "dp")
    gate_got = gate_sum.pairs()

    acts_back = own_features(acts_back) + acts_got.astype(F32)
    own_normed = own_features(normed)
    gain_delta = jnp.sum(acts_back * own_normed, axis=0)
    shift_delta = jnp.sum(acts_back, axis=0)
    input_delta = rescale * (acts_back * own_features(gain) - moments[0][:, None] - own_normed * moments[1][:, None])
    input_delta = cotangent.astype(F32) + to_tokens(input_delta.astype(BF)).astype(F32)
    input_delta, output_got, gate_got, product = fence(input_delta, output_got, gate_got, product)
    output_sum.add_mirrored(output_got)
    gate_sum.add_pairs(gate_got)
    output_got = output_sum.back()
    gate_got = gate_sum.mirrored()
    out_sum = dot(product, output_full, 1, 0)
    out_sum = own_features(out_sum) + swap(own_features(out_sum, 1).astype(BF), "col", 1).astype(F32)
    block_output = to_tokens((own_features(source) + out_sum + own_features(bias)).astype(BF))
    output_weight_delta = output_sum.join(output_got)
    gate_sum.add_mirrored(gate_got)
    gate_weight_delta = gate_sum.join(gate_sum.back())

    biases = jnp.concatenate([gate_bias_delta, value_bias_delta])
    norms = jnp.stack([gain_delta, shift_delta]).reshape(2, rows, narrow)
    small = exchange_blocks(
        [jnp.concatenate([norms[:, k].reshape(-1), biases]) for k in (order.index(q) for q in every)], "row"
    )
    while len(small) > 1:
        small = [a + b for a, b in zip(small[::2], small[1::2])]
    small = jnp.concatenate(
        [small[0], jnp.sum(cotangent, axis=0, dtype=F32), state_deltas[0], passthrough_delta]
    )
    small = small_sum(small, "dp")
    ends = [narrow, 2 * narrow, 2 * narrow + half_ff, 2 * narrow + half_ff + local_channels]
    gain_sum, shift_sum, gate_bias_sum, value_bias_sum, bias_sum, shared = jnp.split(small, ends + [ends[-1] + narrow])
    shared = jnp.concatenate([value_bias_sum, shared]).reshape(rows + 2, channels)
    shared = jnp.stack(across(shared, swap(shared, "col", 1)), axis=1).reshape(-1)
    value_bias_sum, step_sum, pass_sum = jnp.split(shared, [VALUE, VALUE + row_channels])

    state = jnp.concatenate(state_deltas[1:], axis=1)
    late = jnp.concatenate([value_weight_delta.reshape(-1), state.reshape(-1)]).reshape(-1, local_channels)
    late_sum = PairSum(late, "dp")
    late_sum.add_pairs(late_sum.pairs())
    late_sum.add_mirrored(late_sum.mirrored())
    late = late_sum.join(late_sum.back()).astype(BF)
    late = jnp.stack(across(late, swap(late, "col", 1)))
    value_rows = value_weight_delta.shape[0]
    value_weight_delta = late[:, :value_rows].reshape(cols, -1, rows, channels)
    value_weight_delta = value_weight_delta.transpose(1, 2, 0, 3).reshape(-1, VALUE).astype(F32)
    state = late[:, value_rows:].reshape(row_channels, -1).astype(F32)
    modes = decay_rate.shape[1]
    return (
        block_output,
        input_delta,
        gain_sum,
        shift_sum,
        gate_weight_delta,
        gate_bias_sum,
        value_weight_delta,
        value_bias_sum,
        step_sum,
        state[:, :modes],
        state[:, modes : 2 * modes],
        state[:, 2 * modes :],
        pass_sum,
        expand_delta,
        output_weight_delta,
        bias_sum,
    )


def solution(mesh):
    placed = (
        P("dp", ("row", "col")),
        P(),
        P(),
        P("row", "col"),
        P(),
        P("row", None),
        P(),
        P("row"),
        P("row", None),
        P("row", None),
        P("row", None),
        P("row"),
        P("row", "col"),
        P("col", "row"),
        P(),
        P("dp", ("row", "col")),
    )
    return jax.shard_map(
        shards,
        mesh=mesh,
        in_specs=placed,
        out_specs=(
            P("dp", ("row", "col")),
            P("dp", ("row", "col")),
            P(("row", "col")),
            P(("row", "col")),
            P("row", "col"),
            P("col"),
            P("row", None),
            P(),
            P("row"),
            P("row", None),
            P("row", None),
            P("row", None),
            P("row"),
            P("row", "col"),
            P("col", "row"),
            P(("row", "col")),
        ),
        check_vma=False,
    )
```

```python
from functools import partial
import math

import jax
import jax.numpy as jnp
from jax import lax
from jax.experimental import pallas as pl
from jax.experimental.pallas import tpu as pltpu
from jax.sharding import PartitionSpec as P

D = 1024
FF = 3072
VALUE = 512
LEN = 2048
EPSILON = 1e-05
BL = 128
GROUP = 8
BF = jnp.bfloat16
F32 = jnp.float32


def dot(left, right, left_dim, right_dim):
    return lax.dot_general(
        left, right, (((left_dim,), (right_dim,)), ((), ())), preferred_element_type=F32
    )


def gelu(pre_act):
    return jax.nn.gelu(pre_act, approximate=True)


def gelu_back(pre_act, upstream):
    return jax.vjp(gelu, pre_act)[1](upstream)[0]


def mode_weights(log_step, decay_rate, frequency, readout):
    time_step = jnp.exp(log_step)[:, None]
    real_rate = -decay_rate * time_step
    imag_rate = frequency * time_step
    growth = jnp.exp(real_rate)
    shift_real = growth * jnp.cos(imag_rate) - 1.0
    shift_imag = growth * jnp.sin(imag_rate)
    modulus = decay_rate * decay_rate + frequency * frequency
    ratio_real = (shift_imag * frequency - shift_real * decay_rate) / modulus
    ratio_imag = (-shift_imag * decay_rate - shift_real * frequency) / modulus
    modes = decay_rate.shape[1]
    out_real = readout[:, :modes]
    out_imag = readout[:, modes:]
    mode_real = out_real * ratio_real - out_imag * ratio_imag
    mode_imag = out_real * ratio_imag + out_imag * ratio_real
    return (real_rate, imag_rate, mode_real, mode_imag)


def cmul(a, b):
    return a[0]*b[0]-a[1]*b[1], a[0]*b[1]+a[1]*b[0]

def squarings(z, n):
    out=[z]
    for _ in range(n):
        r,i=out[-1]
        out.append((r*r-i*i, 2.0*r*i))
    return out

def ladder(steps, rows, order, first=None):
    M = steps[0][0].shape[1]
    idx = lax.broadcasted_iota(jnp.int32, (8, M), 0)
    if order < 0: idx = 7-idx
    wr = jnp.ones((8,M), jnp.float32); wi = jnp.zeros((8,M), jnp.float32)
    for b in range(3):
        hit = (idx >> b) & 1
        nr, ni = cmul((wr,wi), steps[b])
        wr = jnp.where(hit==1, nr, wr); wi = jnp.where(hit==1, ni, wi)
    groups=[(wr,wi)]
    k=3
    while len(groups)*8 < rows:
        groups += [cmul(g, steps[k]) for g in groups]
        k+=1
    if order<0: groups = groups[::-1]
    return jnp.concatenate([g[0] for g in groups],0), jnp.concatenate([g[1] for g in groups],0)

def row(p, i):
    return p[0][i:i+1], p[1][i:i+1]

def two_terms(x):
    high = x.astype(BF)
    return high, (x - high.astype(F32)).astype(BF)


def gen_kernel(nb, zr, zi, cr, ci, *refs):
    k_out, kr_out = refs[-2:]
    steps = squarings((zr[...], zi[...]), 6 + int(math.log2(nb)))
    rev = (lax.broadcasted_iota(jnp.int32,(BL,BL),0)+lax.broadcasted_iota(jnp.int32,(BL,BL),1)==BL-1).astype(F32).astype(BF)
    nt = (((1,),(1,)),((),()))
    for i in range(GROUP):
        st = [row(x,i) for x in steps]
        near = ladder(st[:7], BL, 1)
        far = ladder(st[7:], nb, 1)
        lead = cmul((cr[i:i+1,:], ci[i:i+1,:]), far)
        lh, ll = two_terms(jnp.concatenate([lead[0], -lead[1]],1))
        nh, nl = two_terms(jnp.concatenate(near,1))
        first = lax.dot_general(jnp.concatenate([lh, ll]), nh, nt, preferred_element_type=F32)
        k = first[:nb] + (first[nb:] + lax.dot_general(lh, nl, nt, preferred_element_type=F32))
        kb = k.astype(BF)
        k_out[i] = kb
    kr_out[...] = jnp.dot(k_out[...].reshape(GROUP*nb, BL), rev, preferred_element_type=F32).astype(BF).reshape(GROUP, nb, BL)


def cost(microseconds):
    return pl.CostEstimate(flops=int(microseconds * 1e9), bytes_accessed=1 << 20, transcendentals=0)


def generate(modes, length, part, parts, earlier=()):
    C, M = modes[0].shape
    nb = length//BL
    steps = C//GROUP//parts
    spec = pl.BlockSpec((GROUP, M), lambda i:(i + part*steps,0))
    ospec = pl.BlockSpec((GROUP, nb, BL), lambda i:(i + part*steps,0,0))
    sh = jax.ShapeDtypeStruct((C,nb,BL), BF)
    return pl.pallas_call(partial(gen_kernel, nb), grid=(steps,), in_specs=[spec]*4 + [pl.BlockSpec(memory_space=pl.ANY)]*len(earlier), out_specs=[ospec]*2,
        out_shape=[sh,sh], cost_estimate=cost(10/parts), input_output_aliases={4+k:k for k in range(len(earlier))})(*modes, *earlier)


def toeplitz_blocks(load, count, shift):
    r = lax.broadcasted_iota(jnp.int32,(BL,BL),0); c = lax.broadcasted_iota(jnp.int32,(BL,BL),1)
    mask = c >= r + shift
    def rot(j):
        x = load(j)
        if x is None: return jnp.zeros((BL,BL), BF)
        base = pltpu.roll(jnp.broadcast_to(x,(64,BL)), shift, 1, stride=1, stride_axis=0).astype(BF)
        return jnp.concatenate([base] + [pltpu.roll(base, 64, 1)], 0)
    out=[]
    cur = rot(0)
    for j in range(count):
        nxt = rot(j+1)
        out.append(jnp.where(mask, nxt, cur))
        cur = nxt
    return jnp.concatenate(out,0)


def toeplitz_old(load, count, shift):
    r = lax.broadcasted_iota(jnp.int32,(BL,BL),0); c = lax.broadcasted_iota(jnp.int32,(BL,BL),1)
    mask = c >= r + shift
    def rot(j):
        x = load(j)
        if x is None: return jnp.zeros((BL,BL), jnp.float32)
        return pltpu.roll(jnp.broadcast_to(x,(BL,BL)), shift, 1, stride=1, stride_axis=0)
    out=[]
    cur = rot(0)
    for j in range(count):
        nxt = rot(j+1)
        out.append(jnp.where(mask, nxt, cur).astype(jnp.bfloat16))
        cur = nxt
    return jnp.concatenate(out,0)


def spread(dst, src, me, per):
    for j in range(dst.shape[0]//GROUP):
        dst[j*GROUP:(j+1)*GROUP,:] = src[me ^ (j//per), :, (j%per)*BL:(j%per+1)*BL].astype(F32)


def gather_out(dst, src, extra, scale, me, per):
    for j in range(src.shape[0]//GROUP):
        rows = slice(j*GROUP,(j+1)*GROUP)
        dst[me ^ (j//per), :, (j%per)*BL:(j%per+1)*BL] = (src[rows,:] + scale*extra[rows,:]).astype(dst.dtype)


def shifted(pad_ref, nb, d):
    return pad_ref[pl.ds(nb-d, nb), :]


def fwd_kernel(nb, tb, me_ref, v_ref, kr_ref, p_ref, out_ref, pad, vf, of):
    per = tb//BL
    me = me_ref[0]
    pad[0:nb,:] = jnp.zeros((nb,BL), F32)
    spread(vf, v_ref, me, per)
    for i in range(GROUP):
        def load(j):
            return vf[(j-1)*GROUP+i:(j-1)*GROUP+i+1,:] if j else None
        H = toeplitz_old(load, nb, 0)
        pad[nb:2*nb,:] = kr_ref[i].astype(F32)
        X = jnp.concatenate([shifted(pad,nb,d) for d in range(nb)],1).astype(BF)
        of[pl.ds(i, nb, stride=GROUP),:] = jnp.dot(X, H, preferred_element_type=F32)
    gather_out(out_ref, of, vf, p_ref[...], me, per)


def forward(me, v, kr, passthrough, out_dtype=jnp.float32):
    R,C,tb = v.shape
    nb = R*tb//BL
    spec = pl.BlockSpec((R,GROUP,tb), lambda i,_:(0,i,0))
    kspec = pl.BlockSpec((GROUP,nb,BL), lambda i,_:(i,0,0))
    pspec = pl.BlockSpec((GROUP,1), lambda i,_:(i,0))
    grid_spec = pltpu.PrefetchScalarGridSpec(num_scalar_prefetch=1, grid=(C//GROUP,), in_specs=[spec,kspec,pspec], out_specs=spec,
        scratch_shapes=[pltpu.VMEM((2*nb,BL),F32)] + [pltpu.VMEM((nb*GROUP,BL),F32)]*2)
    return pl.pallas_call(partial(fwd_kernel,nb,tb), grid_spec=grid_spec,
        out_shape=jax.ShapeDtypeStruct(v.shape,out_dtype), cost_estimate=cost(13))(me,v,kr,passthrough[:,None])


def bwd_kernel(prec, nb, tb, me_ref, v_ref, m_ref, k_ref, p_ref, zr, zi, *refs):
    vb_ref, s_ref, pad, pad2, vf, mf, of = refs[-7:]
    per = tb//BL
    pad[0:nb,:] = jnp.zeros((nb,BL), F32)
    pad2[0:nb,:] = jnp.zeros((nb,BL), F32)
    me = me_ref[0]
    steps = squarings((zr[...], zi[...]), 6 + int(math.log2(nb)))
    rev = (lax.broadcasted_iota(jnp.int32,(BL,BL),0)+lax.broadcasted_iota(jnp.int32,(BL,BL),1)==BL-1).astype(F32).astype(BF)
    lane = lax.broadcasted_iota(jnp.int32,(nb,BL),1).astype(F32)
    M = zr.shape[1]
    arow = (nb-1-lax.broadcasted_iota(jnp.int32,(nb,M),0)).astype(F32)*BL
    spread(vf, v_ref, me, per)
    spread(mf, m_ref, me, per)
    vf[...] = jnp.dot(vf[...].astype(BF), rev, preferred_element_type=F32)
    for i in range(GROUP):
        def load(j):
            return mf[j*GROUP+i:j*GROUP+i+1,:] if j<nb else None
        H = toeplitz_blocks(load, nb, 1)
        pad[nb:2*nb,:] = k_ref[i].astype(F32)
        pad2[nb:2*nb,:] = vf[pl.ds(i, nb, stride=GROUP),:]
        X = jnp.concatenate([jnp.concatenate([shifted(pad,nb,nb-1-e) for e in range(nb)],1), jnp.concatenate([shifted(pad2,nb,nb-1-e) for e in range(nb)],1)],0).astype(BF)
        out = jnp.dot(X, H, preferred_element_type=F32)
        of[pl.ds(i, nb, stride=GROUP),:] = out[:nb,:]
        kb = out[nb:,:]
        st = [row(s,i) for s in steps]
        near = ladder(st[:7], BL, 1)
        far = ladder(st[7:], nb, -1)
        U = jnp.dot(jnp.concatenate([kb, kb*lane],0), jnp.concatenate(near,1), precision=prec, preferred_element_type=F32)
        u = U[:nb,:M], U[:nb,M:]
        w = U[nb:,:M]+arow*u[0], U[nb:,M:]+arow*u[1]
        s1 = cmul(u, far); s2 = cmul(w, far)
        for n,x in enumerate((*s1,*s2)):
            s_ref[n, i:i+1, :] = jnp.sum(x,0,keepdims=True)
    for j in range(nb):
        rows = slice((nb-1-j)*GROUP,(nb-j)*GROUP)
        vb_ref[me ^ (j//per), :, (j%per)*BL:(j%per+1)*BL] = (of[rows,:] + p_ref[...]*mf[j*GROUP:(j+1)*GROUP,:]).astype(vb_ref.dtype)


def backward(me, v, mb, k, passthrough, zr, zi, part, parts, earlier=(), prec=lax.Precision.DEFAULT):
    R,C,tb = v.shape
    M = zr.shape[1]
    nb = R*tb//BL
    steps = C//GROUP//parts
    spec = pl.BlockSpec((R,GROUP,tb), lambda i,_:(0,i + part*steps,0))
    kspec = pl.BlockSpec((GROUP,nb,BL), lambda i,_:(i + part*steps,0,0))
    pspec = pl.BlockSpec((GROUP,1), lambda i,_:(i + part*steps,0))
    zspec = pl.BlockSpec((GROUP,M), lambda i,_:(i + part*steps,0))
    grid_spec = pltpu.PrefetchScalarGridSpec(num_scalar_prefetch=1, grid=(steps,),
        in_specs=[spec,spec,kspec,pspec,zspec,zspec] + [pl.BlockSpec(memory_space=pl.ANY)]*len(earlier),
        out_specs=[spec, pl.BlockSpec((4,GROUP,M), lambda i,_:(0,i + part*steps,0))], scratch_shapes=[pltpu.VMEM((2*nb,BL),F32)]*2 + [pltpu.VMEM((nb*GROUP,BL),F32)]*3)
    return pl.pallas_call(partial(bwd_kernel,prec,nb,tb), grid_spec=grid_spec,
        out_shape=[jax.ShapeDtypeStruct(v.shape,BF), jax.ShapeDtypeStruct((4,C,M),jnp.float32)],
        cost_estimate=cost(21/parts), input_output_aliases={7+n:n for n in range(len(earlier))})(me,v,mb,k,passthrough[:,None],zr,zi,*earlier)


def gate_kernel(pieces, acts_ref, up_ref, bias_ref, *refs):
    gates, outs, (act_ref, slope_ref, back_ref) = refs[:pieces], refs[pieces : 2 * pieces], refs[2 * pieces :]
    width = gates[0].shape[0]
    gate_pre = bias_ref[...]
    product_back = 0.0
    for k in range(pieces):
        lanes = slice(k * width, (k + 1) * width)
        gate_pre = gate_pre + jnp.dot(acts_ref[:, lanes], gates[k][...], preferred_element_type=F32)
        product_back = product_back + dot(up_ref[:, lanes], outs[k][...], 1, 1)
    square = gate_pre * gate_pre
    bend = jnp.tanh(0.7978845608 * gate_pre * (1.0 + 0.044715 * square))
    gate_act = 0.5 * gate_pre * (1.0 + bend)
    slope = 0.5 * (1.0 + bend) + 0.5 * gate_pre * (1.0 - bend * bend) * (0.7978845608 * (1.0 + 0.134145 * square))
    act_ref[...] = gate_act
    slope_ref[...] = slope * product_back
    back_ref[...] = (product_back * gate_act).astype(BF)


def gate_stage(acts, upstream, bias, gates, outs):
    block, width = acts.shape[0], bias.shape[0]
    tile = 512
    whole = pl.BlockSpec(acts.shape, lambda i: (0, 0))
    ospec = pl.BlockSpec((block, tile), lambda i: (0, i))
    return pl.pallas_call(
        partial(gate_kernel, len(gates)),
        grid=(width // tile,),
        in_specs=[whole, whole, pl.BlockSpec((1, tile), lambda i: (0, i))]
        + [pl.BlockSpec((gate.shape[0], tile), lambda i: (0, i)) for gate in gates]
        + [pl.BlockSpec((tile, out.shape[1]), lambda i: (i, 0)) for out in outs],
        out_specs=[ospec] * 3,
        out_shape=[jax.ShapeDtypeStruct((block, width), kind) for kind in (F32, F32, BF)],
        cost_estimate=cost(8),
    )(acts, upstream, bias.reshape(1, -1), *gates, *outs)


def bits(axis):
    size = lax.axis_size(axis)
    return [1 << k for k in range(size.bit_length() - 1)]


def swap(array, axis, mask):
    return lax.ppermute(array, axis, [(i, i ^ mask) for i in range(lax.axis_size(axis))])


def exchange_blocks(blocks, axis):
    return [blocks[0]] + [swap(blocks[q], axis, q) for q in range(1, len(blocks))]


def fence(*values):
    return lax.optimization_barrier(values)


def halve(array, dim):
    return jnp.split(array, 2, dim)


class PairSum:
    def __init__(self, array, axis):
        self.axis = axis
        index = lax.axis_index(axis)
        self.half = (index ^ (index >> 1)) & 1
        length = array.shape[0] // 2
        self.kept = lax.dynamic_slice_in_dim(array, self.half * length, length)
        self.sent = lax.dynamic_slice_in_dim(array, (1 - self.half) * length, length).astype(BF)

    def pairs(self):
        return swap(self.sent, self.axis, 1)

    def add_pairs(self, got):
        self.total = (self.kept.astype(F32) + got.astype(F32)).astype(BF)

    def mirrored(self):
        for bit in bits(self.axis)[2:]:
            self.total = (self.total.astype(F32) + swap(self.total, self.axis, bit).astype(F32)).astype(BF)
        return swap(self.total, self.axis, 3) if lax.axis_size(self.axis) > 2 else None

    def add_mirrored(self, got):
        if got is not None:
            self.total = (self.total.astype(F32) + got.astype(F32)).astype(BF)

    def back(self):
        return swap(self.total, self.axis, 1)

    def join(self, got):
        first = jnp.where(self.half == 0, self.total, got)
        second = jnp.where(self.half == 0, got, self.total)
        return jnp.concatenate([first, second]).astype(F32)


def small_sum(array, axis):
    left = bits(axis)
    while left:
        one, left = left[0], left[1:]
        if left:
            two, left = left[0], left[1:]
            array = (array + swap(array, axis, one)) + (swap(array, axis, two) + swap(array, axis, one | two))
        else:
            array = array + swap(array, axis, one)
    return array


def shards(
    inputs,
    norm_gain,
    norm_shift,
    gate_weight,
    gate_bias,
    value_weight,
    value_bias,
    log_step,
    decay_rate,
    frequency,
    readout,
    passthrough,
    expand_weight,
    output_weight,
    output_bias,
    cotangent,
):
    rows = lax.axis_size("row")
    cols = lax.axis_size("col")
    row_index = lax.axis_index("row")
    col_index = lax.axis_index("col")
    tokens, narrow = inputs.shape
    block = tokens // rows
    half_ff = FF // cols
    row_channels = VALUE // rows
    channels = row_channels // cols
    local_channels = rows * channels

    def own_channels(array):
        return lax.dynamic_slice_in_dim(array, col_index * channels, channels, 0)

    state_params = tuple(own_channels(a) for a in (log_step, decay_rate, frequency, readout))
    own_pass = own_channels(passthrough)
    weights, weights_pullback = jax.vjp(mode_weights, *state_params)
    real_rate, imag_rate, mode_real, mode_imag = weights
    growth = jnp.exp(real_rate)
    z_real, z_imag = growth * jnp.cos(imag_rate), growth * jnp.sin(imag_rate)
    me = row_index.astype(jnp.int32).reshape(1)
    every = range(rows)
    order = [0]
    for bit in reversed(bits("row")):
        order = order + [q | bit for q in order]

    def across(own, other):
        return [jnp.where(col_index == 0, own, other), jnp.where(col_index == 0, other, own)]

    def at_xor(array, q, dim=0):
        return lax.dynamic_index_in_dim(array, row_index ^ q, dim, False)

    def natural(blocks):
        stacked = jnp.stack(blocks)
        return jnp.stack([at_xor(stacked, q) for q in every])

    def features(own, other):
        first, second = across(own, other)
        return jnp.concatenate([part[k] for k in every for part in (first, second)], axis=1)

    def own_features(array, flip=0):
        return jnp.concatenate(
            [
                lax.dynamic_slice_in_dim(array, (k * cols + (col_index ^ flip)) * narrow, narrow, array.ndim - 1)
                for k in every
            ],
            axis=-1,
        )

    def by_order(blocks):
        return [blocks[q] for q in order]

    def ordered_features(vectors):
        blocks = vectors.reshape(vectors.shape[0], rows, -1)
        return jnp.concatenate([at_xor(blocks, q, 1) for q in order], axis=1)

    modes_in = (z_real, z_imag, mode_real, mode_imag)
    value_half = lax.dynamic_index_in_dim(
        value_weight.reshape(-1, rows, cols, channels), col_index, 2, False
    ).reshape(-1, local_channels)
    value_bias_half = lax.dynamic_index_in_dim(
        value_bias.reshape(rows, cols, channels), col_index, 1, False
    ).reshape(local_channels, 1)
    gate_bias_half = lax.dynamic_slice_in_dim(gate_bias, col_index * half_ff, half_ff)
    gain, shift, bias = ordered_features(jnp.stack([norm_gain, norm_shift, output_bias]))

    x_parts = exchange_blocks([at_xor(inputs.reshape(rows, block, narrow), q) for q in every], "row")
    value_2 = swap(value_half, "row", 2)
    value_1 = swap(value_half, "row", 1)
    x_parts, value_2, modes_in, upstream_blocks, gate_0 = fence(
        x_parts, value_2, modes_in, cotangent.reshape(rows, block, narrow), gate_weight
    )
    x_own = jnp.stack(by_order(x_parts))
    x_other = swap(x_own, "col", 1)
    g_parts = exchange_blocks([at_xor(upstream_blocks, q) for q in every], "row")
    gate_2 = swap(gate_0, "row", 2)
    gate_1 = swap(gate_0, "row", 1)
    kernels = generate(modes_in, tokens, 0, 1)
    value_3 = swap(value_2, "row", 1)
    x_other, value_1, value_3, kernels, output_0 = fence(x_other, value_1, value_3, kernels, output_weight)
    value_half = jnp.concatenate([value_half, value_2, value_1, value_3])
    x_full = features(x_own, x_other)

    source = x_full.astype(F32)
    row_mean = jnp.mean(source, axis=-1, keepdims=True)
    centered = source - row_mean
    variance = jnp.mean(centered * centered, axis=-1, keepdims=True)
    rescale = lax.rsqrt(variance + EPSILON)
    normed = centered * rescale
    acts = (normed * gain + shift).astype(BF)

    value_pre = dot(value_half, acts, 0, 1) + value_bias_half
    values = gelu(value_pre).astype(BF).reshape(rows, channels, block)
    values_sent = [at_xor(values, q) for q in every]
    values_sent, modes_in, kernels, gate_2, gate_1 = fence(values_sent, modes_in, kernels, gate_2, gate_1)
    values = exchange_blocks(values_sent, "row")
    output_2 = swap(output_0, "row", 2)
    values, kernels, g_parts, expand_0 = fence(values, kernels, g_parts, expand_weight)
    g_own = jnp.stack(by_order(g_parts))
    g_other = swap(g_own, "col", 1)
    kernel, kernel_flipped = kernels
    values = jnp.stack(values)
    gate_3 = swap(gate_2, "row", 1)
    expand_2 = swap(expand_0, "row", 2)
    output_1 = swap(output_0, "row", 1)
    mixed = forward(me, values, kernel, own_pass, BF)
    mixed, gate_1, gate_3, output_0, expand_0, g_other = fence(mixed, gate_1, gate_3, output_0, expand_0, g_other)
    mixed = exchange_blocks([mixed[q] for q in every], "row")
    mixed, output_2, output_1, g_own = fence(mixed, output_2, output_1, g_own)
    output_3 = swap(output_2, "row", 1)
    upstream = features(g_own, g_other)
    mixed = jnp.stack(by_order(mixed))
    mixed_other = swap(mixed, "col", 1)
    expand_1 = swap(expand_0, "row", 1)
    output_3, acts, mixed = fence(output_3, acts, mixed)
    gates = (gate_0, gate_2, gate_1, gate_3)
    outputs = (output_0, output_2, output_1, output_3)
    gate_act, gate_slope, expand_back = gate_stage(acts, upstream, gate_bias_half, gates, outputs)
    gate_act, gate_slope, expand_back, mixed_other, expand_1, expand_2 = fence(
        gate_act, gate_slope, expand_back, mixed_other, expand_1, expand_2
    )
    expand_3 = swap(expand_2, "row", 1)
    mixed = jnp.stack(across(mixed, mixed_other), axis=1).reshape(VALUE, block)
    expand_full = jnp.concatenate([expand_0, expand_2, expand_1, expand_3])
    mixed_back = dot(expand_full, expand_back, 1, 1).reshape(rows, cols, channels, block)
    sent = lax.dynamic_index_in_dim(mixed_back, 1 - col_index, 1, False).astype(BF)
    mixed_back = lax.dynamic_index_in_dim(mixed_back, col_index, 1, False)
    sent, mixed, expand_full = fence(sent, mixed, expand_full)
    got = swap(sent, "col", 1)

    expand_kept, expand_sent = [dot(piece, expand_back, 1, 0).astype(BF) for piece in halve(mixed, 0)]
    expand_got = swap(expand_sent, "row", 1)
    expanded = dot(mixed, expand_full, 0, 0)
    product = (gate_act * expanded).astype(BF)
    gate_back = (gate_slope * expanded).astype(BF)
    gate_bias_delta = jnp.sum(gate_back, axis=0, dtype=F32)
    output_kept, output_sent = [dot(product, piece, 0, 0).astype(BF) for piece in halve(upstream, 1)]
    output_got = swap(output_sent, "row", 1)
    product, gate_back, got, output_kept = fence(product, gate_back, got, output_kept)
    mixed_back = (mixed_back + got.astype(F32)).astype(BF)
    mixed_back, upstream, acts = fence(mixed_back, upstream, acts)
    mixed_back = exchange_blocks(by_order(mixed_back), "row")
    gate_kept, gate_sent = [dot(piece, gate_back, 0, 0).astype(BF) for piece in halve(acts, 1)]
    mixed_back, expand_got, output_got, gate_sent = fence(mixed_back, expand_got, output_got, gate_sent)

    def second(kept, got, dim):
        total = kept.astype(F32) + got.astype(F32)
        return halve(total.astype(BF), dim)

    gate_got = swap(gate_sent, "row", 1)
    mixed_back = jnp.stack(mixed_back)
    expand_kept, expand_sent = second(expand_kept, expand_got, 0)
    output_kept, output_sent = second(output_kept, output_got, 1)
    mixed_back, expand_sent, output_sent = fence(mixed_back, expand_sent, output_sent)
    expand_got = swap(expand_sent, "row", 2)
    output_got = swap(output_sent, "row", 2)
    state_args = (me, values, mixed_back, kernel_flipped, own_pass, z_real, z_imag)
    back = backward(*state_args, 0, 2)
    back, expand_got, gate_got = fence(back, expand_got, gate_got)
    expand_sum = PairSum(expand_kept.astype(F32) + expand_got.astype(F32), "dp")
    gate_kept, gate_sent = second(gate_kept, gate_got, 0)
    back, expand_sum.sent, gate_sent = fence(back, expand_sum.sent, gate_sent)
    expand_got = expand_sum.pairs()
    gate_got = swap(gate_sent, "row", 2)
    back = backward(*state_args, 1, 2, back)
    back, expand_got, output_got = fence(back, expand_got, output_got)
    values_back, sums = back
    gate_full, output_full = jnp.concatenate(gates), jnp.concatenate(outputs, axis=1)
    values_back = exchange_blocks([values_back[q] for q in every], "row")
    expand_sum.add_pairs(expand_got)
    output_sum = PairSum(output_kept.astype(F32) + output_got.astype(F32), "dp")
    output_sum.sent, expand_sum.total = fence(output_sum.sent, expand_sum.total)
    expand_got = expand_sum.mirrored()
    output_got = output_sum.pairs()
    values_back, expand_got, output_got = fence(values_back, expand_got, output_got)
    expand_sum.add_mirrored(expand_got)
    output_sum.add_pairs(output_got)
    expand_got = expand_sum.back()
    output_got = output_sum.mirrored()

    def to_tokens(array):
        blocks = by_order(jnp.split(array, rows, 1))
        return natural(exchange_blocks(blocks, "row")).reshape(tokens, narrow)

    values_back = natural(values_back).reshape(local_channels, block)
    value_back = gelu_back(value_pre, values_back.astype(F32)).astype(BF)
    value_kept, value_sent = [dot(piece, value_back, 0, 1).astype(BF) for piece in halve(acts, 1)]
    value_kept, value_sent = second(value_kept, swap(value_sent, "row", 1), 0)
    value_weight_delta = value_kept.astype(F32) + swap(value_sent, "row", 2).astype(F32)
    value_bias_delta = jnp.sum(value_back, axis=1, dtype=F32)
    passthrough_delta = jnp.sum(mixed_back.astype(F32) * values.astype(F32), axis=(0, 2))
    first_real, first_imag, second_real, second_imag = sums
    state_deltas = weights_pullback(
        (
            mode_real * second_real - mode_imag * second_imag,
            -mode_real * second_imag - mode_imag * second_real,
            first_real,
            -first_imag,
        )
    )

    acts_back = dot(gate_back, gate_full, 1, 1) + dot(value_back, value_half, 0, 1)
    weighted = acts_back * gain
    moments = jnp.stack([jnp.sum(weighted, axis=1), jnp.sum(weighted * normed, axis=1)])
    acts_sent = own_features(acts_back, 1).astype(BF)
    acts_got = swap(acts_sent, "col", 1)
    moments = small_sum(moments, "col") / D
    acts_got, moments, gate_got, expand_got = fence(acts_got, moments, gate_got, expand_got)
    expand_delta = expand_sum.join(expand_got)
    gate_sum = PairSum(gate_kept.astype(F32) + gate_got.astype(F32), "dp")
    gate_got = gate_sum.pairs()

    acts_back = own_features(acts_back) + acts_got.astype(F32)
    own_normed = own_features(normed)
    gain_delta = jnp.sum(acts_back * own_normed, axis=0)
    shift_delta = jnp.sum(acts_back, axis=0)
    input_delta = rescale * (acts_back * own_features(gain) - moments[0][:, None] - own_normed * moments[1][:, None])
    input_delta = cotangent.astype(F32) + to_tokens(input_delta.astype(BF)).astype(F32)
    input_delta, output_got, gate_got, product = fence(input_delta, output_got, gate_got, product)
    output_sum.add_mirrored(output_got)
    gate_sum.add_pairs(gate_got)
    output_got = output_sum.back()
    gate_got = gate_sum.mirrored()
    out_sum = dot(product, output_full, 1, 0)
    out_sum = own_features(out_sum) + swap(own_features(out_sum, 1).astype(BF), "col", 1).astype(F32)
    block_output = to_tokens((own_features(source) + out_sum + own_features(bias)).astype(BF))
    output_weight_delta = output_sum.join(output_got)
    gate_sum.add_mirrored(gate_got)
    gate_weight_delta = gate_sum.join(gate_sum.back())

    biases = jnp.concatenate([gate_bias_delta, value_bias_delta])
    norms = jnp.stack([gain_delta, shift_delta]).reshape(2, rows, narrow)
    small = exchange_blocks(
        [jnp.concatenate([norms[:, k].reshape(-1), biases]) for k in (order.index(q) for q in every)], "row"
    )
    while len(small) > 1:
        small = [a + b for a, b in zip(small[::2], small[1::2])]
    small = jnp.concatenate(
        [small[0], jnp.sum(cotangent, axis=0, dtype=F32), state_deltas[0], passthrough_delta]
    )
    small = small_sum(small, "dp")
    ends = [narrow, 2 * narrow, 2 * narrow + half_ff, 2 * narrow + half_ff + local_channels]
    gain_sum, shift_sum, gate_bias_sum, value_bias_sum, bias_sum, shared = jnp.split(small, ends + [ends[-1] + narrow])
    shared = jnp.concatenate([value_bias_sum, shared]).reshape(rows + 2, channels)
    shared = jnp.stack(across(shared, swap(shared, "col", 1)), axis=1).reshape(-1)
    value_bias_sum, step_sum, pass_sum = jnp.split(shared, [VALUE, VALUE + row_channels])

    state = jnp.concatenate(state_deltas[1:], axis=1)
    late = jnp.concatenate([value_weight_delta.reshape(-1), state.reshape(-1)]).reshape(-1, local_channels)
    late_sum = PairSum(late, "dp")
    late_sum.add_pairs(late_sum.pairs())
    late_sum.add_mirrored(late_sum.mirrored())
    late = late_sum.join(late_sum.back()).astype(BF)
    late = jnp.stack(across(late, swap(late, "col", 1)))
    value_rows = value_weight_delta.shape[0]
    value_weight_delta = late[:, :value_rows].reshape(cols, -1, rows, channels)
    value_weight_delta = value_weight_delta.transpose(1, 2, 0, 3).reshape(-1, VALUE).astype(F32)
    state = late[:, value_rows:].reshape(row_channels, -1).astype(F32)
    modes = decay_rate.shape[1]
    return (
        block_output,
        input_delta,
        gain_sum,
        shift_sum,
        gate_weight_delta,
        gate_bias_sum,
        value_weight_delta,
        value_bias_sum,
        step_sum,
        state[:, :modes],
        state[:, modes : 2 * modes],
        state[:, 2 * modes :],
        pass_sum,
        expand_delta,
        output_weight_delta,
        bias_sum,
    )


def solution(mesh):
    placed = (
        P("dp", ("row", "col")),
        P(),
        P(),
        P("row", "col"),
        P(),
        P("row", None),
        P(),
        P("row"),
        P("row", None),
        P("row", None),
        P("row", None),
        P("row"),
        P("row", "col"),
        P("col", "row"),
        P(),
        P("dp", ("row", "col")),
    )
    return jax.shard_map(
        shards,
        mesh=mesh,
        in_specs=placed,
        out_specs=(
            P("dp", ("row", "col")),
            P("dp", ("row", "col")),
            P(("row", "col")),
            P(("row", "col")),
            P("row", "col"),
            P("col"),
            P("row", None),
            P(),
            P("row"),
            P("row", None),
            P("row", None),
            P("row", None),
            P("row"),
            P("row", "col"),
            P("col", "row"),
            P(("row", "col")),
        ),
        check_vma=False,
    )
```
